32 devices in a mesh: seq: 8 (over y, x, core), dp: 4 (over z).
Axes of the slice: x: 2, y: 2, z: 4, core: 2. Of those that a mesh axis runs over, the one named last changes fastest.
Arguments:
- tokens: bfloat16 [4, 8192, 512], P('dp', 'seq'), may hold values from -8 to 8
- grad_out: bfloat16 [4, 8192, 512], P('dp', 'seq'), may hold values from -8 to 8
- doc_ids: int32 [4, 8192], P('dp', 'seq'), may hold values from 0 to 3, never falling along the last dimension, each value on 1 to 4096 neighbouring positions
- qkv_w: float32 [512, 1536], P(('seq', 'dp')), may hold values from -0.25 to 0.25
- qkv_m: float32 [512, 1536], P(('seq', 'dp')), may hold values from -0.25 to 0.25
- qkv_a: float32 [512, 1536], P(('seq', 'dp')), may hold values from -0.25 to 0.25
- out_w: float32 [512, 512], P(('seq', 'dp')), may hold values from -1.5 to 1.5
- out_m: float32 [512, 512], P(('seq', 'dp')), may hold values from -1.5 to 1.5
- out_a: float32 [512, 512], P(('seq', 'dp')), may hold values from -1.5 to 1.5
- up_w: float32 [512, 2048], P(('seq', 'dp')), may hold values from -0.25 to 0.25
- up_m: float32 [512, 2048], P(('seq', 'dp')), may hold values from -0.25 to 0.25
- up_a: float32 [512, 2048], P(('seq', 'dp')), may hold values from -0.25 to 0.25
- down_w: float32 [2048, 512], P(('seq', 'dp')), may hold values from -0.125 to 0.125
- down_m: float32 [2048, 512], P(('seq', 'dp')), may hold values from -0.125 to 0.125
- down_a: float32 [2048, 512], P(('seq', 'dp')), may hold values from -0.125 to 0.125
- norm_w: float32 [4, 512], P(None, ('seq', 'dp')), may hold values from 0.25 to 1.75
- norm_m: float32 [4, 512], P(None, ('seq', 'dp')), may hold values from -1.5 to 1.5
- norm_a: float32 [4, 512], P(None, ('seq', 'dp')), may hold values from 0.25 to 1.75
Outputs:
- block_out: bfloat16 [4, 8192, 512], P('dp', 'seq')
- input_grad: float32 [4, 8192, 512], P('dp', 'seq')
- norm_stats: float32 [4, 2], P('dp')
- stat_grads: float32 [4, 2], P('dp')
- qkv_state: float32 [3, 512, 1536], P(None, ('seq', 'dp'))
- out_state: float32 [3, 512, 512], P(None, ('seq', 'dp'))
- up_state: float32 [3, 512, 2048], P(None, ('seq', 'dp'))
- down_state: float32 [3, 2048, 512], P(None, ('seq', 'dp'))
- norm_state: float32 [3, 4, 512], P(None, None, ('seq', 'dp'))
The draws below stay inside these ranges and needn't reach their ends.
Inputs may be any that keep to these rules, and one draw needn't show every extreme that they name: `doc_ids`: document ids never fall along a sequence; each sequence holds 4 documents, the longest exactly 4096 positions.
All inputs are finite; a program needn't handle non-finite values.
Results may differ from the reference program's by a relative error of at most 0.005.
The reference program's roundings to bfloat16 on the way count: a program that leaves them out, or rounds other values in their place, can miss the bound.
Values may be sent and summed in bfloat16 or wider, within the bound.
A program may use at most 128 MiB of HBM per device.

```python
import math
import jax
import jax.numpy as jnp
import numpy as np
from jax import lax

D = 512
H = 8
E = 64
FF = 2048
SPAN = 128
LENGTH = 8192
NSEQ = 4
TOKENS = 32768


def rising_field(key, start, finish):
    noise_key, line_key = jax.random.split(key)
    noise = jnp.clip(jax.random.normal(noise_key, (NSEQ, LENGTH, D), jnp.float32), -4.0, 4.0)
    first, last = (start, finish)
    direction = jnp.clip(jax.random.normal(line_key, (NSEQ, 1, D), jnp.float32), -3.0, 3.0)
    place = jnp.arange(LENGTH, dtype=jnp.float32) / (LENGTH - 1)
    amount = first + (last - first) * place
    return noise + amount[None, :, None] * direction


def draw_tokens(key, part):
    return rising_field(jax.random.fold_in(key, 11), 0.3, 1.2).astype(jnp.bfloat16)


def draw_grad_out(key, part):
    return rising_field(jax.random.fold_in(key, 23), 0.2, 0.8).astype(jnp.bfloat16)


def shard_levels(rng, dims, pieces, low, largest):
    loudness = 1.0
    for position, shards_of in pieces:
        draws = jax.random.uniform(jax.random.fold_in(jax.random.fold_in(rng, 6), position), (shards_of,), jnp.float32, low / len(pieces), largest / len(pieces))
        loudness = loudness * jnp.repeat(jnp.exp(draws), dims[position] // shards_of).reshape((-1,) + (1,) * (len(dims) - 1 - position))
    return loudness


def profile(number_of, total, limit, lean):
    weights = [(1 << 20) // math.isqrt(rank ** lean) + 1 for rank in range(2, number_of + 1)]
    spare, given = total - limit - (number_of - 1), [1] * (number_of - 1)
    while spare > 0:
        free = [i for i in range(number_of - 1) if given[i] < limit]
        pool, left = sum([weights[i] for i in free]), spare
        for i in free:
            more = min(limit - given[i], max(1, left * weights[i] // pool), spare)
            given[i] = given[i] + more
            spare = spare - more
    return np.array([limit] + given)


def uneven(key, count, total, bound, slope):
    if count == 2:
        one = jax.random.randint(key, (), max(1, total - bound), min(bound, total - 1) + 1)
        return jnp.stack([one, total - one])
    lengths = jnp.asarray(profile(count, total, bound, slope), jnp.int32)
    twos = (count - 1) // 2
    source_of, sink = lengths[1:1 + 2 * twos:2], lengths[2:2 + 2 * twos:2]
    margin = jnp.minimum(source_of - 1, bound - sink)
    shifted = jax.random.randint(jax.random.fold_in(key, 1), (twos,), 0, 1 << 20) % (margin + 1)
    lengths = lengths.at[1:1 + 2 * twos:2].set(source_of - shifted).at[2:2 + 2 * twos:2].set(sink + shifted)
    return lengths[jax.random.permutation(jax.random.fold_in(key, 2), count)]


def gaussian(own_key, extent, scale, bound, shards=(), kind=jnp.bfloat16):
    drawn = scale * jax.random.normal(own_key, extent, jnp.float32)
    if shards:
        drawn = drawn * shard_levels(own_key, extent, shards, -0.22, 0.18)
    return jnp.clip(drawn, -bound, bound).astype(kind)


def setup_inputs(seed: int = 0) -> dict:
    splits = jax.random.split(jax.random.key(seed), 19)
    return {
        "tokens": draw_tokens(jax.random.fold_in(splits[18], 71), 0),
        "grad_out": draw_grad_out(jax.random.fold_in(splits[18], 71), 0),
        "doc_ids": jax.vmap(lambda own: jnp.searchsorted(jnp.cumsum(uneven(own, 4, LENGTH, LENGTH // 2, 0)), jnp.arange(LENGTH), side="right"))(jax.random.split(splits[2], NSEQ)).reshape((NSEQ, LENGTH)).astype(jnp.int32),
        "qkv_w": gaussian(splits[3], (D, 3 * D), D ** -0.5, 0.25, ((0, 32),), jnp.float32),
        "qkv_m": gaussian(splits[4], (D, 3 * D), D ** -0.5, 0.25, ((0, 32),), jnp.float32),
        "qkv_a": gaussian(splits[5], (D, 3 * D), D ** -0.5, 0.25, ((0, 32),), jnp.float32),
        "out_w": gaussian(splits[6], (D, D), (D // 32) ** -0.5, 1.5, ((0, 32),), jnp.float32),
        "out_m": gaussian(splits[7], (D, D), (D // 32) ** -0.5, 1.5, ((0, 32),), jnp.float32),
        "out_a": gaussian(splits[8], (D, D), (D // 32) ** -0.5, 1.5, ((0, 32),), jnp.float32),
        "up_w": gaussian(splits[9], (D, FF), D ** -0.5, 0.25, ((0, 32),), jnp.float32),
        "up_m": gaussian(splits[10], (D, FF), D ** -0.5, 0.25, ((0, 32),), jnp.float32),
        "up_a": gaussian(splits[11], (D, FF), D ** -0.5, 0.25, ((0, 32),), jnp.float32),
        "down_w": gaussian(splits[12], (FF, D), FF ** -0.5, 0.125, ((0, 32),), jnp.float32),
        "down_m": gaussian(splits[13], (FF, D), FF ** -0.5, 0.125, ((0, 32),), jnp.float32),
        "down_a": gaussian(splits[14], (FF, D), FF ** -0.5, 0.125, ((0, 32),), jnp.float32),
        "norm_w": jnp.clip(1.0 + 0.15 * jax.random.normal(splits[15], (4, D), jnp.float32), 0.25, 1.75),
        "norm_m": gaussian(splits[16], (4, D), 0.1, 1.5, ((1, 32),), jnp.float32),
        "norm_a": jnp.clip(1.0 + 0.15 * jax.random.normal(splits[17], (4, D), jnp.float32), 0.25, 1.75),
    }


@jax.custom_vjp
def low(v):
    return lax.optimization_barrier(v.astype(jnp.bfloat16)).astype(jnp.float32)

@jax.custom_vjp
def low_back(v):
    return v

def low_keep(v):
    return (low(v), None)

def low_pass(kept, grad):
    return (grad,)

def back_keep(v):
    return (v, None)

def back_low(kept, grad):
    return (low(grad),)
low.defvjp(low_keep, low_pass)
low_back.defvjp(back_keep, back_low)
highest = lax.Precision.HIGHEST

def matmul(left, right):
    return jnp.dot(left, right, precision=highest, preferred_element_type=jnp.float32)

def both_round(value):
    return low(low_back(value))

def layer_norm(values, gain_row, shift_row):
    centre = values - lax.optimization_barrier(jnp.mean(values, -1, keepdims=True))
    spread = lax.optimization_barrier(jnp.mean(centre * centre, -1, keepdims=True))
    return centre * lax.rsqrt(spread + 1e-05) * gain_row + shift_row

def sequence_layer(inputs, doc_row, stat_shift, w_qkv, w_out, w_up, w_down, norm_rows):
    length = inputs.shape[0]
    spans = length // SPAN
    act_one = low(layer_norm(inputs, norm_rows[0], norm_rows[1]))
    mixed = matmul(act_one, w_qkv)
    query = both_round(mixed[:, :D])
    key_all = both_round(mixed[:, D:2 * D])
    value_all = both_round(mixed[:, 2 * D:])
    doc_span = doc_row.reshape(spans, SPAN)
    last_doc = doc_span[:, -1]
    member = (doc_span == last_doc[:, None]).astype(jnp.float32)
    counts = lax.optimization_barrier(jnp.sum(member, 1))
    key_span = key_all.reshape(spans, SPAN, D)
    value_span = value_all.reshape(spans, SPAN, D)
    sum_key = jnp.einsum('ns,nsd->nd', member, key_span, precision=highest) / counts[:, None]
    sum_value = jnp.einsum('ns,nsd->nd', member, value_span, precision=highest) / counts[:, None]
    stat_mean = jnp.mean(sum_key)
    stat_var = jnp.mean((sum_key - stat_mean) * (sum_key - stat_mean))
    key_norm = (sum_key - (stat_mean + stat_shift[0])) * lax.rsqrt(stat_var + stat_shift[1] + 1e-05)
    key_send = low(key_norm).reshape(spans, H, E)
    value_send = low(sum_value).reshape(spans, H, E)
    query_blk = query.reshape(spans, SPAN, H, E)
    key_blk = key_all.reshape(spans, SPAN, H, E)
    value_blk = value_all.reshape(spans, SPAN, H, E)
    local = jnp.einsum('pqhe,pkhe->phqk', query_blk, key_blk, precision=highest) * 0.125
    remote = jnp.einsum('pqhe,nhe->phqn', query_blk, key_send, precision=highest) * 0.125
    scores = low_back(jnp.concatenate([local, remote], -1))
    positions = jnp.arange(SPAN)
    causal = positions[:, None] >= positions[None, :]
    same_doc = doc_span[:, :, None] == doc_span[:, None, :]
    mask_local = (same_doc & causal[None])[:, None]
    span_ids = jnp.arange(spans)
    earlier = span_ids[None, :] < span_ids[:, None]
    match = doc_span[:, :, None] == last_doc[None, None, :]
    mask_remote = (match & earlier[:, None, :])[:, None]
    allowed = jnp.concatenate([mask_local, mask_remote], -1)
    probs = jax.nn.softmax(jnp.where(allowed, scores, -1e+30), axis=-1)
    probs_low = low(probs)
    attended = jnp.einsum('phqk,pkhe->pqhe', probs_low[..., :SPAN], value_blk, precision=highest)
    attended = attended + jnp.einsum('phqn,nhe->pqhe', probs_low[..., SPAN:], value_send, precision=highest)
    heads_out = both_round(attended.reshape(length, D))
    after_attn = inputs + low_back(matmul(heads_out, w_out))
    act_two = low(layer_norm(after_attn, norm_rows[2], norm_rows[3]))
    hidden = low_back(matmul(act_two, w_up))
    act_three = low(jax.nn.gelu(hidden, approximate=True))
    result = after_attn + low_back(matmul(act_three, w_down))
    return (result, jnp.stack([stat_mean, stat_var]))

def advance(weight, moment, average, grad):
    rate = 0.02 * TOKENS ** (-0.5)
    new_moment = 0.9 * moment + rate * grad
    new_weight = weight - (rate * grad + 0.9 * new_moment)
    new_average = 0.99 * average + 0.01 * new_weight
    return jnp.stack([new_weight, new_moment, new_average])

def reference(tokens, grad_out, doc_ids, qkv_w, qkv_m, qkv_a, out_w, out_m, out_a, up_w, up_m, up_a, down_w, down_m, down_a, norm_w, norm_m, norm_a):

    def forward(inputs, w_qkv, w_out, w_up, w_down, norm_rows, shifts):
        rounded = [low(w_qkv), low(w_out), low(w_up), low(w_down), low(norm_rows)]

        def one_seq(triple):
            return jax.checkpoint(sequence_layer)(triple[0], triple[1], triple[2], *rounded)
        result, stats = lax.map(one_seq, (inputs, doc_ids, shifts))
        return (result, stats)
    zero_shift = jnp.zeros((tokens.shape[0], 2), jnp.float32)
    result, pull, stats = jax.vjp(forward, tokens.astype(jnp.float32), qkv_w, out_w, up_w, down_w, norm_w, zero_shift, has_aux=True)
    grads = pull(grad_out.astype(jnp.float32))
    return (result.astype(jnp.bfloat16), grads[0], stats, grads[6], advance(qkv_w, qkv_m, qkv_a, grads[1]), advance(out_w, out_m, out_a, grads[2]), advance(up_w, up_m, up_a, grads[3]), advance(down_w, down_m, down_a, grads[4]), advance(norm_w, norm_m, norm_a, grads[5]))
```

```python
import functools
import math

import jax
import jax.numpy as jnp
from jax import lax
from jax.experimental import pallas as pl
from jax.experimental.pallas import tpu as pltpu
from jax.sharding import PartitionSpec as P

H = 8
SPAN = 128
MESH = pl.DeviceIdType.MESH
DMA = pltpu.SemaphoreType.DMA


class Place:
    def __init__(self, chain):
        self.chain = chain
        self.s = lax.axis_index("seq")
        self.z = lax.axis_index("dp")
        self.core = lax.rem(self.s, 2)
        self.group = lax.div(self.s, 2)
        self.sib = self.flip(self.s, 1)
        self.xs = self.flip(self.s, 2)
        self.ys = self.flip(self.s, 4)
        self.ds = self.flip(self.xs, 4)

    @staticmethod
    def flip(value, bit):
        return value + bit - 2 * bit * lax.rem(lax.div(value, bit), 2)

    def dev(self, s, z=None):
        return {"seq": s, "dp": self.z if z is None else z}

    def zpeer(self, step):
        return lax.rem(self.z + step, self.chain)

    def barrier(self, extra=()):
        sem = pltpu.get_barrier_semaphore()
        peers = [self.dev(self.sib), self.dev(self.xs), self.dev(self.ys)]
        peers += [self.dev(self.s, self.zpeer(k)) for k in range(1, self.chain)]
        peers += list(extra)
        for peer in peers:
            pl.semaphore_signal(sem, inc=1, device_id=peer, device_id_type=MESH)
        pl.semaphore_wait(sem, len(peers))


def remote(src, dst, send, recv, peer):
    return pltpu.make_async_remote_copy(
        src_ref=src, dst_ref=dst, send_sem=send, recv_sem=recv, device_id=peer, device_id_type=MESH
    )


class Gather:
    def __init__(self, place, full, rows, send, recv):
        self.p, self.full, self.rows = place, full, rows
        self.send, self.recv = send, recv
        self.gr = place.chain * rows
        self.half = full.shape[1] // 2
        self.sent = []

    def region(self, s, cols=None):
        rows = pl.ds(pl.multiple_of(s * self.gr, self.gr), self.gr)
        if cols is None:
            return self.full.at[rows]
        return self.full.at[rows, cols]

    def own(self, z):
        start = pl.multiple_of(self.p.s * self.gr + z * self.rows, self.rows)
        return self.full.at[pl.ds(start, self.rows)]

    def go(self, k, ref, peer):
        copy = remote(ref, ref, self.send.at[k], self.recv.at[k], peer)
        copy.start()
        self.sent.append(copy)

    def got(self, k, ref):
        remote(ref, ref, self.send.at[k], self.recv.at[k], self.p.dev(self.p.sib)).wait_recv()

    def start(self):
        p = self.p
        for k in range(1, p.chain):
            self.go(k - 1, self.own(p.z), p.dev(p.s, p.zpeer(k)))

    def chain_done(self):
        p = self.p
        for k in range(1, p.chain):
            self.got(k - 1, self.own(p.zpeer(p.chain - k)))
        self.go(3, self.region(p.s), p.dev(p.xs))
        self.go(4, self.region(p.s), p.dev(p.ys))
        self.go(7, self.region(p.s), p.dev(p.sib))

    def sides_done(self):
        p = self.p
        first, second = pl.ds(0, self.half), pl.ds(self.half, self.half)
        self.got(3, self.region(p.xs))
        self.go(5, self.region(p.xs, first), p.dev(p.ys))
        self.go(8, self.region(p.xs), p.dev(p.sib))
        self.got(4, self.region(p.ys))
        self.go(6, self.region(p.ys, second), p.dev(p.xs))
        self.go(9, self.region(p.ys), p.dev(p.sib))

    def corner_done(self):
        p = self.p
        first, second = pl.ds(0, self.half), pl.ds(self.half, self.half)
        self.got(5, self.region(p.ds, first))
        self.got(6, self.region(p.ds, second))
        self.go(10, self.region(p.ds), p.dev(p.sib))

    def done(self):
        p = self.p
        for k, s in ((7, p.s), (8, p.xs), (9, p.ys), (10, p.ds)):
            self.got(k, self.region(p.flip(s, 1)))

    def drain(self):
        for copy in self.sent:
            copy.wait_send()


GATHER_SEMS = 11


def by_rows(count, step, body):
    def trip(i, carry):
        body(pl.multiple_of(i * step, step))
        return carry

    lax.fori_loop(0, count // step, trip, 0)


class Scatter:
    def __init__(self, place, rows, bufs, send, recv):
        self.p, self.rows = place, rows
        self.gr = place.chain * rows
        self.own, self.out2, self.in2, self.stage, self.land, self.zout, self.zin = bufs
        self.cols = self.own.shape[1]
        self.half = self.cols // 2
        self.step = min(16, self.gr)
        self.send, self.recv = send, recv
        self.sent = []

    def go(self, k, src, dst, peer):
        copy = remote(src, dst, self.send.at[k], self.recv.at[k], peer)
        copy.start()
        self.sent.append(copy)

    def got(self, k, ref):
        remote(ref, ref, self.send.at[k], self.recv.at[k], self.p.dev(self.p.sib)).wait_recv()

    def base(self, bits):
        g = self.p.group
        for bit in (1, 2):
            if bits & bit:
                g = Place.flip(g, bit)
        return pl.multiple_of(g * self.gr, self.gr)

    def cut(self, ref, slot, which):
        return ref.at[pl.ds(slot * self.gr, self.gr), pl.ds(which * self.half, self.half)]

    def start(self):
        self.go(0, self.out2, self.in2, self.p.dev(self.p.sib))

    def core_done(self):
        p, gr, step = self.p, self.gr, self.step
        self.got(0, self.in2)
        far, xg, yg, me = self.base(3), self.base(1), self.base(2), self.base(0)

        def sum_far(i):
            rows = pl.ds(pl.multiple_of(far + i, step), step)
            total = self.own[rows] + self.in2[rows].astype(jnp.float32)
            self.stage[pl.ds(i, step)] = total.astype(jnp.bfloat16)

        by_rows(gr, step, sum_far)
        self.go(1, self.cut(self.stage, 0, 0), self.cut(self.land, 0, 0), p.dev(p.xs))
        self.go(2, self.cut(self.stage, 0, 1), self.cut(self.land, 0, 1), p.dev(p.ys))
        for slot, start in ((1, xg), (2, yg)):

            def sum_side(i, slot=slot, start=start):
                rows = pl.ds(pl.multiple_of(start + i, step), step)
                total = self.own[rows] + self.in2[rows].astype(jnp.float32)
                self.own[rows] = total
                cols = pl.ds((slot - 1) * self.half, self.half)
                part = total[:, : self.half] if slot == 1 else total[:, self.half :]
                self.stage[pl.ds(slot * gr + i, step), cols] = part.astype(jnp.bfloat16)

            by_rows(gr, step, sum_side)
        self.go(3, self.cut(self.stage, 1, 0), self.cut(self.land, 1, 0), p.dev(p.xs))
        self.go(4, self.cut(self.stage, 2, 1), self.cut(self.land, 2, 1), p.dev(p.ys))

        def sum_me(i):
            rows = pl.ds(pl.multiple_of(me + i, step), step)
            self.own[rows] = self.own[rows] + self.in2[rows].astype(jnp.float32)

        by_rows(gr, step, sum_me)

    def sides_done(self):
        p, gr, step = self.p, self.gr, self.step
        xg, yg = self.base(1), self.base(2)
        for k, slot, which, start, peer in ((5, 2, 0, yg, p.ys), (6, 1, 1, xg, p.xs)):
            self.got(k - 4, self.cut(self.land, 0, which))

            def add(i, slot=slot, which=which, start=start):
                rows = pl.ds(pl.multiple_of(start + i, step), step)
                cols = pl.ds(which * self.half, self.half)
                total = self.own[rows, cols] + self.land[pl.ds(i, step), cols].astype(jnp.float32)
                self.stage[pl.ds(slot * gr + i, step), cols] = total.astype(jnp.bfloat16)

            by_rows(gr, step, add)
            self.go(k, self.cut(self.stage, slot, which), self.cut(self.land, slot, which), p.dev(peer))

    def mine_done(self):
        p, gr, step = self.p, self.gr, self.step
        me = self.base(0)
        for k, slot, which in ((3, 1, 0), (4, 2, 1), (5, 2, 0), (6, 1, 1)):
            self.got(k, self.cut(self.land, slot, which))

        def add(i):
            rows = pl.ds(pl.multiple_of(me + i, step), step)
            sides = self.land[pl.ds(gr + i, step)].astype(jnp.float32)
            sides = sides + self.land[pl.ds(2 * gr + i, step)].astype(jnp.float32)
            total = self.own[rows] + sides
            self.own[rows] = total
            self.zout[pl.ds(i, step)] = total.astype(jnp.bfloat16)

        by_rows(gr, step, add)
        for k in range(1, p.chain):
            z = p.zpeer(k)
            src = self.zout.at[pl.ds(pl.multiple_of(z * self.rows, self.rows), self.rows)]
            dst = self.zin.at[pl.ds((k - 1) * self.rows, self.rows)]
            self.go(6 + k, src, dst, p.dev(p.s, z))

    def done(self, result):
        p, step = self.p, self.step
        for k in range(1, p.chain):
            self.got(6 + k, self.zin.at[pl.ds((k - 1) * self.rows, self.rows)])
        start = self.base(0) + p.z * self.rows

        def add(i):
            total = self.own[pl.ds(pl.multiple_of(start + i, step), step)]
            for k in range(1, p.chain):
                total = total + self.zin[pl.ds((k - 1) * self.rows + i, step)].astype(jnp.float32)
            result[pl.ds(i, step)] = total

        by_rows(self.rows, step, add)

    def drain(self):
        for copy in self.sent:
            copy.wait_send()


SCATTER_SEMS = 10


def scatter_scratch(chain, rows, cols):
    f32, bf16 = jnp.float32, jnp.bfloat16
    gr = chain * rows
    return [
        pltpu.VMEM((4 * gr, cols), f32),
        pltpu.VMEM((4 * gr, cols), bf16),
        pltpu.VMEM((4 * gr, cols), bf16),
        pltpu.VMEM((3 * gr, cols), bf16),
        pltpu.VMEM((3 * gr, cols), bf16),
        pltpu.VMEM((gr, cols), bf16),
        pltpu.VMEM((max(1, chain - 1) * rows, cols), bf16),
    ]


def gather_kernel(chain, shards, *refs):
    n = len(shards)
    pieces, fulls, (send, recv) = refs[:n], refs[n : 2 * n], refs[2 * n :]
    place = Place(chain)
    gathers = [
        Gather(place, full, rows, send.at[m], recv.at[m])
        for m, (full, rows) in enumerate(zip(fulls, shards))
    ]
    for piece, g in zip(pieces, gathers):
        g.own(place.z)[...] = piece[...]
    place.barrier()
    for step in ("start", "chain_done", "sides_done", "corner_done", "done", "drain"):
        for g in gathers:
            getattr(g, step)()


def gather_weights(chain, devices, pieces):
    vmem = pl.BlockSpec(memory_space=pltpu.VMEM)
    n = len(pieces)
    return pl.pallas_call(
        functools.partial(gather_kernel, chain, [piece.shape[0] for piece in pieces]),
        out_shape=[
            jax.ShapeDtypeStruct((devices * piece.shape[0], piece.shape[1]), piece.dtype)
            for piece in pieces
        ],
        in_specs=[vmem] * n,
        out_specs=[vmem] * n,
        scratch_shapes=[DMA((n, GATHER_SEMS)), DMA((n, GATHER_SEMS))],
        compiler_params=pltpu.CompilerParams(collective_id=0, has_side_effects=True),
    )(*pieces)


def scatter_kernel(chain, shards, *refs):
    n = len(shards)
    grads, sums, refs = refs[:n], refs[n : 2 * n], refs[2 * n :]
    send, recv = refs[-2:]
    place = Place(chain)
    scatters = []
    for m, (grad, rows) in enumerate(zip(grads, shards)):
        one = Scatter(place, rows, refs[7 * m : 7 * m + 7], send.at[m], recv.at[m])
        scatters.append(one)
    place.barrier()
    for grad, one in zip(grads, scatters):
        gr, step = one.gr, one.step
        for g in range(4):

            def split(i, g=g, grad=grad, one=one, gr=gr, step=step):
                for mine in (0, 1):
                    core = place.core if mine else 1 - place.core
                    row = pl.multiple_of((2 * g + core) * gr + i, step)
                    value = grad[pl.ds(row, step)]
                    if mine:
                        one.own[pl.ds(g * gr + i, step)] = value
                    else:
                        one.out2[pl.ds(g * gr + i, step)] = value.astype(jnp.bfloat16)

            by_rows(gr, step, split)
        one.start()
    for step in ("core_done", "sides_done", "mine_done"):
        for one in scatters:
            getattr(one, step)()
    for total, one in zip(sums, scatters):
        one.done(total)
    for one in scatters:
        one.drain()


def scatter_grads(chain, devices, grads):
    vmem = pl.BlockSpec(memory_space=pltpu.VMEM)
    n = len(grads)
    shards = [grad.shape[0] // devices for grad in grads]
    scratch = []
    for rows, grad in zip(shards, grads):
        scratch += scatter_scratch(chain, rows, grad.shape[1])
    return pl.pallas_call(
        functools.partial(scatter_kernel, chain, shards),
        out_shape=[
            jax.ShapeDtypeStruct((rows, grad.shape[1]), jnp.float32)
            for rows, grad in zip(shards, grads)
        ],
        in_specs=[vmem] * n,
        out_specs=[vmem] * n,
        scratch_shapes=scratch + [DMA((n, SCATTER_SEMS)), DMA((n, SCATTER_SEMS))],
        compiler_params=pltpu.CompilerParams(
            collective_id=1, has_side_effects=True, vmem_limit_bytes=58 * 2**20
        ),
    )(*grads)


def norm_forward(values, gain_row, shift_row):
    centre = values - jnp.mean(values, -1, keepdims=True)
    spread = jnp.mean(centre * centre, -1, keepdims=True)
    inv_std = lax.rsqrt(spread + 1e-05)
    normal = centre * inv_std
    return (normal * gain_row + shift_row, normal, inv_std)


def norm_backward(grad_in, normal, inv_std, gain_row):
    scaled = grad_in * gain_row
    centred = (
        scaled
        - jnp.mean(scaled, -1, keepdims=True)
        - normal * jnp.mean(scaled * normal, -1, keepdims=True)
    )
    return (inv_std * centred, jnp.sum(grad_in * normal, 0), jnp.sum(grad_in, 0))


def gelu_tanh(values):
    return jax.nn.gelu(values, approximate=True)


def span_probs(query_blk, key_blk, key_remote, doc_span, last_remote, span_first):
    span_len = doc_span.shape[2]
    local = (
        jnp.einsum("bpqhe,bpkhe->bphqk", query_blk, key_blk, preferred_element_type=jnp.float32)
        * 0.125
    )
    remote = (
        jnp.einsum("bpqhe,bnhe->bphqn", query_blk, key_remote, preferred_element_type=jnp.float32)
        * 0.125
    )
    positions = jnp.arange(span_len)
    causal = positions[:, None] >= positions[None, :]
    same_doc = doc_span[:, :, :, None] == doc_span[:, :, None, :]
    mask_local = (same_doc & causal[None, None])[:, :, None]
    span_ids = span_first + jnp.arange(doc_span.shape[1])
    earlier = jnp.arange(key_remote.shape[1])[None, :] < span_ids[:, None]
    doc_float = doc_span.astype(jnp.float32)
    match = doc_float[:, :, :, None] == last_remote.astype(jnp.float32)[:, None, None, :]
    mask_remote = (match & earlier[None, :, None, :])[:, :, None]
    allowed = jnp.concatenate([mask_local, mask_remote], -1)
    scores = jnp.where(allowed, jnp.concatenate([local, remote], -1), -1e30)
    peak_score = jnp.max(scores, -1, keepdims=True)
    raised = jnp.exp(scores - peak_score)
    return raised / jnp.sum(raised, -1, keepdims=True)


def advance(weight, moment, average, grad, rate):
    new_moment = 0.9 * moment + rate * grad
    new_weight = weight - (rate * grad + 0.9 * new_moment)
    new_average = 0.99 * average + 0.01 * new_weight
    return jnp.stack([new_weight, new_moment, new_average])


def shards(
    tokens,
    grad_out,
    doc_ids,
    qkv_w,
    qkv_m,
    qkv_a,
    out_w,
    out_m,
    out_a,
    up_w,
    up_m,
    up_a,
    down_w,
    down_m,
    down_a,
    norm_w,
    norm_m,
    norm_a,
):
    seqs, seq_len, width = tokens.shape
    span_len = SPAN
    cycle_size = lax.axis_size("seq")
    cycle_rank = lax.axis_index("seq")
    spans_dev = seq_len // span_len
    spans_all = spans_dev * cycle_size
    rows_dev = seqs * seq_len
    head_size = width // H
    bf16 = jnp.bfloat16
    f32 = jnp.float32
    chain = lax.axis_size("dp")
    devices = cycle_size * chain
    own_kernels = cycle_size == 8 and qkv_w.shape[0] % 16 == 0
    if own_kernels:
        per = norm_w.shape[1]
        norm_piece = jnp.pad(norm_w.astype(bf16), ((0, 12), (0, 256 - per)))
        w_qkv, w_out, w_up, w_down, norm_all = gather_weights(
            chain,
            devices,
            [qkv_w.astype(bf16), out_w.astype(bf16), up_w.astype(bf16), down_w.astype(bf16), norm_piece],
        )
        norm_low = norm_all.reshape(devices, 16, 256)[:, :4, :per].transpose(1, 0, 2).reshape(4, width)
    else:
        w_qkv, w_out, w_up, w_down, norm_low = (
            lax.all_gather(qkv_w.astype(bf16), ("seq", "dp"), axis=0, tiled=True),
            lax.all_gather(out_w.astype(bf16), ("seq", "dp"), axis=0, tiled=True),
            lax.all_gather(up_w.astype(bf16), ("seq", "dp"), axis=0, tiled=True),
            lax.all_gather(down_w.astype(bf16), ("seq", "dp"), axis=0, tiled=True),
            lax.all_gather(norm_w.astype(bf16), ("seq", "dp"), axis=1, tiled=True),
        )
    norm_rows = norm_low.astype(f32)
    inputs = tokens.reshape(rows_dev, width).astype(f32)
    normed_one, normal_one, inv_one = norm_forward(inputs, norm_rows[0], norm_rows[1])
    act_one = normed_one.astype(bf16)
    mixed = jnp.dot(act_one, w_qkv, preferred_element_type=f32)
    query = mixed[:, :width].astype(bf16)
    key_all = mixed[:, width : 2 * width].astype(bf16)
    value_all = mixed[:, 2 * width :].astype(bf16)
    block_shape = (seqs, spans_dev, span_len, H, head_size)
    query_blk = query.reshape(block_shape)
    key_blk = key_all.reshape(block_shape)
    value_blk = value_all.reshape(block_shape)
    doc_span = doc_ids.reshape(seqs, spans_dev, span_len)
    last_doc = doc_span[:, :, -1]
    member = (doc_span == last_doc[:, :, None]).astype(f32)
    counts = jnp.sum(member, -1)
    member_low = member.astype(bf16)
    key_four = key_all.reshape(seqs, spans_dev, span_len, width)
    value_four = value_all.reshape(seqs, spans_dev, span_len, width)
    sum_key = (
        jnp.einsum("bpt,bptd->bpd", member_low, key_four, preferred_element_type=f32)
        / counts[..., None]
    )
    sum_value = (
        jnp.einsum("bpt,bptd->bpd", member_low, value_four, preferred_element_type=f32)
        / counts[..., None]
    )
    total_sum, total_square = lax.psum(
        (jnp.sum(sum_key, (1, 2)), jnp.sum(sum_key * sum_key, (1, 2))), "seq"
    )
    entries = spans_all * width
    stat_mean = total_sum / entries
    stat_var = total_square / entries - stat_mean * stat_mean
    inv_sum = lax.rsqrt(stat_var + 1e-05)
    key_norm = (sum_key - stat_mean[:, None, None]) * inv_sum[:, None, None]
    key_send = key_norm.astype(bf16)
    value_send = sum_value.astype(bf16)
    last_send = last_doc.astype(bf16)
    key_remote, value_remote, last_remote = (
        lax.all_gather(key_send, "seq", axis=1, tiled=True),
        lax.all_gather(value_send, "seq", axis=1, tiled=True),
        lax.all_gather(last_send, "seq", axis=1, tiled=True),
    )
    remote_shape = (seqs, spans_all, H, head_size)
    span_first = cycle_rank * spans_dev
    probs = span_probs(
        query_blk, key_blk, key_remote.reshape(remote_shape), doc_span, last_remote, span_first
    )
    probs_low = probs.astype(bf16)
    attended = jnp.einsum(
        "bphqk,bpkhe->bpqhe", probs_low[..., :span_len], value_blk, preferred_element_type=f32
    )
    attended = attended + jnp.einsum(
        "bphqn,bnhe->bpqhe",
        probs_low[..., span_len:],
        value_remote.reshape(remote_shape),
        preferred_element_type=f32,
    )
    heads_out = attended.reshape(rows_dev, width).astype(bf16)
    after_attn = inputs + jnp.dot(heads_out, w_out, preferred_element_type=f32)
    normed_two, normal_two, inv_two = norm_forward(after_attn, norm_rows[2], norm_rows[3])
    act_two = normed_two.astype(bf16)
    hidden = jnp.dot(act_two, w_up, preferred_element_type=f32)
    act_three = gelu_tanh(hidden).astype(bf16)
    result = after_attn + jnp.dot(act_three, w_down, preferred_element_type=f32)
    block_out = result.astype(bf16).reshape(seqs, seq_len, width)
    stats_out = jnp.stack([stat_mean, stat_var], -1)
    grad_low = grad_out.reshape(rows_dev, width)
    grad_down = jnp.einsum("tf,td->fd", act_three, grad_low, preferred_element_type=f32)
    d_three = jnp.einsum("td,fd->tf", grad_low, w_down, preferred_element_type=f32)
    unused_out, gelu_pull = jax.vjp(gelu_tanh, hidden)
    d_hidden = gelu_pull(d_three)[0].astype(bf16)
    grad_up = jnp.einsum("td,tf->df", act_two, d_hidden, preferred_element_type=f32)
    d_two = jnp.einsum("tf,df->td", d_hidden, w_up, preferred_element_type=f32)
    d_norm_two, gain_two, shift_two = norm_backward(d_two, normal_two, inv_two, norm_rows[2])
    d_after = grad_low.astype(f32) + d_norm_two
    d_after_low = d_after.astype(bf16)
    grad_outw = jnp.einsum("tc,td->cd", heads_out, d_after_low, preferred_element_type=f32)
    d_heads = jnp.einsum("td,cd->tc", d_after_low, w_out, preferred_element_type=f32).astype(bf16)
    key_back, value_back, last_back = (key_remote, value_remote, last_remote)
    key_back_blk = key_back.reshape(remote_shape)
    value_back_blk = value_back.reshape(remote_shape)
    probs_back = span_probs(query_blk, key_blk, key_back_blk, doc_span, last_back, span_first)
    probs_back_low = probs_back.astype(bf16)
    d_heads_blk = d_heads.reshape(block_shape)
    d_probs = jnp.concatenate(
        [
            jnp.einsum("bpqhe,bpkhe->bphqk", d_heads_blk, value_blk, preferred_element_type=f32),
            jnp.einsum(
                "bpqhe,bnhe->bphqn", d_heads_blk, value_back_blk, preferred_element_type=f32
            ),
        ],
        -1,
    )
    row_dot = jnp.sum(probs_back * d_probs, -1, keepdims=True)
    d_scores = (probs_back * (d_probs - row_dot)).astype(bf16)
    d_local = d_scores[..., :span_len]
    d_remote = d_scores[..., span_len:]
    d_query = 0.125 * (
        jnp.einsum("bphqk,bpkhe->bpqhe", d_local, key_blk, preferred_element_type=f32)
        + jnp.einsum("bphqn,bnhe->bpqhe", d_remote, key_back_blk, preferred_element_type=f32)
    )
    d_key = 0.125 * jnp.einsum("bphqk,bpqhe->bpkhe", d_local, query_blk, preferred_element_type=f32)
    d_value = jnp.einsum(
        "bphqk,bpqhe->bpkhe",
        probs_back_low[..., :span_len],
        d_heads_blk,
        preferred_element_type=f32,
    )
    d_key_sum = (
        0.125 * jnp.einsum("bphqn,bpqhe->bnhe", d_remote, query_blk, preferred_element_type=f32)
    ).reshape(seqs, spans_all, width)
    d_value_sum = jnp.einsum(
        "bphqn,bpqhe->bnhe", probs_back_low[..., span_len:], d_heads_blk, preferred_element_type=f32
    ).reshape(seqs, spans_all, width)
    owned_key, owned_value = (
        lax.psum_scatter(
            d_key_sum.astype(jnp.bfloat16), "seq", scatter_dimension=1, tiled=True
        ).astype(jnp.float32),
        lax.psum_scatter(
            d_value_sum.astype(jnp.bfloat16), "seq", scatter_dimension=1, tiled=True
        ).astype(jnp.float32),
    )
    back_sum, back_cross = lax.psum(
        (jnp.sum(owned_key, (1, 2)), jnp.sum(owned_key * key_norm, (1, 2))), "seq"
    )
    stat_grads = jnp.stack([-inv_sum * back_sum, -0.5 * inv_sum * inv_sum * back_cross], -1)
    d_sum_key = inv_sum[:, None, None] * (
        owned_key
        - back_sum[:, None, None] / entries
        - key_norm * back_cross[:, None, None] / entries
    )
    share = member / counts[..., None]
    d_key_all = (
        d_key.reshape(seqs, spans_dev, span_len, width)
        + share[..., None] * d_sum_key[:, :, None, :]
    )
    d_value_all = (
        d_value.reshape(seqs, spans_dev, span_len, width)
        + share[..., None] * owned_value[:, :, None, :]
    )
    d_mixed = jnp.concatenate(
        [
            d_query.reshape(rows_dev, width),
            d_key_all.reshape(rows_dev, width),
            d_value_all.reshape(rows_dev, width),
        ],
        -1,
    ).astype(bf16)
    grad_qkv = jnp.einsum("td,tf->df", act_one, d_mixed, preferred_element_type=f32)
    d_one = jnp.einsum("tf,df->td", d_mixed, w_qkv, preferred_element_type=f32)
    d_norm_one, gain_one, shift_one = norm_backward(d_one, normal_one, inv_one, norm_rows[0])
    input_grad = (d_after + d_norm_one).reshape(seqs, seq_len, width)
    grad_norm = jnp.stack([gain_one, shift_one, gain_two, shift_two])
    if own_kernels:
        spread = grad_norm.reshape(4, devices, per).transpose(1, 0, 2)
        spread = jnp.pad(spread, ((0, 0), (0, 12), (0, 256 - per))).reshape(devices * 16, 256)
        sum_qkv, sum_outw, sum_up, sum_down, sum_norm = scatter_grads(
            chain, devices, [grad_qkv, grad_outw, grad_up, grad_down, spread]
        )
        sum_norm = sum_norm[:4, :per]
    else:
        sum_qkv, sum_outw, sum_up, sum_down, sum_norm = (
            lax.psum_scatter(grad_qkv, ("seq", "dp"), scatter_dimension=0, tiled=True),
            lax.psum_scatter(grad_outw, ("seq", "dp"), scatter_dimension=0, tiled=True),
            lax.psum_scatter(grad_up, ("seq", "dp"), scatter_dimension=0, tiled=True),
            lax.psum_scatter(grad_down, ("seq", "dp"), scatter_dimension=0, tiled=True),
            lax.psum_scatter(grad_norm, ("seq", "dp"), scatter_dimension=1, tiled=True),
        )
    tokens_all = rows_dev * cycle_size * lax.axis_size("dp")
    rate = 0.02 / math.sqrt(tokens_all)
    return (
        block_out,
        input_grad,
        stats_out,
        stat_grads,
        advance(qkv_w, qkv_m, qkv_a, sum_qkv, rate),
        advance(out_w, out_m, out_a, sum_outw, rate),
        advance(up_w, up_m, up_a, sum_up, rate),
        advance(down_w, down_m, down_a, sum_down, rate),
        advance(norm_w, norm_m, norm_a, sum_norm, rate),
    )


def solution(mesh):
    placed = (
        P("dp", "seq", None),
        P("dp", "seq", None),
        P("dp", "seq"),
        P(("seq", "dp"), None),
        P(("seq", "dp"), None),
        P(("seq", "dp"), None),
        P(("seq", "dp"), None),
        P(("seq", "dp"), None),
        P(("seq", "dp"), None),
        P(("seq", "dp"), None),
        P(("seq", "dp"), None),
        P(("seq", "dp"), None),
        P(("seq", "dp"), None),
        P(("seq", "dp"), None),
        P(("seq", "dp"), None),
        P(None, ("seq", "dp")),
        P(None, ("seq", "dp")),
        P(None, ("seq", "dp")),
    )
    return jax.shard_map(
        shards,
        mesh=mesh,
        in_specs=placed,
        out_specs=(
            P("dp", "seq", None),
            P("dp", "seq", None),
            P("dp", None),
            P("dp", None),
            P(None, ("seq", "dp"), None),
            P(None, ("seq", "dp"), None),
            P(None, ("seq", "dp"), None),
            P(None, ("seq", "dp"), None),
            P(None, None, ("seq", "dp")),
        ),
        check_vma=False,
    )
```

```python
import functools
import math

import jax
import jax.numpy as jnp
from jax import lax
from jax.experimental import pallas as pl
from jax.experimental.pallas import tpu as pltpu
from jax.sharding import PartitionSpec as P

H = 8
SPAN = 128
MESH = pl.DeviceIdType.MESH
DMA = pltpu.SemaphoreType.DMA


class Place:
    def __init__(self, chain):
        self.chain = chain
        self.s = lax.axis_index("seq")
        self.z = lax.axis_index("dp")
        self.core = lax.rem(self.s, 2)
        self.group = lax.div(self.s, 2)
        self.sib = self.flip(self.s, 1)
        self.xs = self.flip(self.s, 2)
        self.ys = self.flip(self.s, 4)
        self.ds = self.flip(self.xs, 4)

    @staticmethod
    def flip(value, bit):
        return value + bit - 2 * bit * lax.rem(lax.div(value, bit), 2)

    def dev(self, s, z=None):
        return {"seq": s, "dp": self.z if z is None else z}

    def zpeer(self, step):
        return lax.rem(self.z + step, self.chain)

    def barrier(self, extra=()):
        sem = pltpu.get_barrier_semaphore()
        peers = [self.dev(self.sib), self.dev(self.xs), self.dev(self.ys)]
        peers += [self.dev(self.s, self.zpeer(k)) for k in range(1, self.chain)]
        peers += list(extra)
        for peer in peers:
            pl.semaphore_signal(sem, inc=1, device_id=peer, device_id_type=MESH)
        pl.semaphore_wait(sem, len(peers))


def remote(src, dst, send, recv, peer):
    return pltpu.make_async_remote_copy(
        src_ref=src, dst_ref=dst, send_sem=send, recv_sem=recv, device_id=peer, device_id_type=MESH
    )


class Gather:
    def __init__(self, place, full, rows, send, recv):
        self.p, self.full, self.rows = place, full, rows
        self.send, self.recv = send, recv
        self.gr = place.chain * rows
        self.half = full.shape[1] // 2
        self.sent = []

    def region(self, s, cols=None):
        rows = pl.ds(pl.multiple_of(s * self.gr, self.gr), self.gr)
        if cols is None:
            return self.full.at[rows]
        return self.full.at[rows, cols]

    def own(self, z):
        start = pl.multiple_of(self.p.s * self.gr + z * self.rows, self.rows)
        return self.full.at[pl.ds(start, self.rows)]

    def go(self, k, ref, peer):
        copy = remote(ref, ref, self.send.at[k], self.recv.at[k], peer)
        copy.start()
        self.sent.append(copy)

    def got(self, k, ref):
        remote(ref, ref, self.send.at[k], self.recv.at[k], self.p.dev(self.p.sib)).wait_recv()

    def start(self):
        p = self.p
        for k in range(1, p.chain):
            self.go(k - 1, self.own(p.z), p.dev(p.s, p.zpeer(k)))

    def chain_done(self):
        p = self.p
        for k in range(1, p.chain):
            self.got(k - 1, self.own(p.zpeer(p.chain - k)))
        self.go(3, self.region(p.s), p.dev(p.xs))
        self.go(4, self.region(p.s), p.dev(p.ys))
        self.go(7, self.region(p.s), p.dev(p.sib))

    def sides_done(self):
        p = self.p
        first, second = pl.ds(0, self.half), pl.ds(self.half, self.half)
        self.got(3, self.region(p.xs))
        self.go(5, self.region(p.xs, first), p.dev(p.ys))
        self.go(8, self.region(p.xs), p.dev(p.sib))
        self.got(4, self.region(p.ys))
        self.go(6, self.region(p.ys, second), p.dev(p.xs))
        self.go(9, self.region(p.ys), p.dev(p.sib))

    def corner_done(self):
        p = self.p
        first, second = pl.ds(0, self.half), pl.ds(self.half, self.half)
        self.got(5, self.region(p.ds, first))
        self.got(6, self.region(p.ds, second))
        self.go(10, self.region(p.ds), p.dev(p.sib))

    def done(self):
        p = self.p
        for k, s in ((7, p.s), (8, p.xs), (9, p.ys), (10, p.ds)):
            self.got(k, self.region(p.flip(s, 1)))

    def drain(self):
        for copy in self.sent:
            copy.wait_send()


GATHER_SEMS = 11


def by_rows(count, step, body):
    def trip(i, carry):
        body(pl.multiple_of(i * step, step))
        return carry

    lax.fori_loop(0, count // step, trip, 0)


class Scatter:
    def __init__(self, place, rows, flip, bufs, send, recv):
        self.p, self.rows, self.turned = place, rows, flip
        self.full, self.in2, self.stage, self.land, self.mine, self.zout, self.zin = bufs
        self.gr, self.cols = self.full.shape[2], self.full.shape[3]
        self.half = self.cols // 2
        self.step = 16
        self.send, self.recv = send, recv
        self.sent = []

    def go(self, k, src, dst, peer):
        copy = remote(src, dst, self.send.at[k], self.recv.at[k], peer)
        copy.start()
        self.sent.append(copy)

    def got(self, k, ref):
        remote(ref, ref, self.send.at[k], self.recv.at[k], self.p.dev(self.p.sib)).wait_recv()

    def near(self, bits):
        g = self.p.group
        for bit in (1, 2):
            if bits & bit:
                g = Place.flip(g, bit)
        return g

    def cut(self, ref, slot, which):
        return ref.at[slot, :, pl.ds(which * self.half, self.half)]

    def both(self, g, rows, cols):
        mine = self.full[g, self.p.core, rows, cols].astype(jnp.float32)
        return mine + self.in2[g, rows, cols].astype(jnp.float32)

    def start(self):
        self.go(0, self.full.at[:, 1 - self.p.core], self.in2, self.p.dev(self.p.sib))

    def core_done(self):
        p, step = self.p, self.step
        self.got(0, self.in2)
        far, xg, yg = self.near(3), self.near(1), self.near(2)
        whole = pl.ds(0, self.cols)
        first, second = pl.ds(0, self.half), pl.ds(self.half, self.half)

        def sum_far(i):
            rows = pl.ds(i, step)
            self.stage[0, rows] = self.both(far, rows, whole).astype(jnp.bfloat16)

        by_rows(self.gr, step, sum_far)
        self.go(1, self.cut(self.stage, 0, 0), self.cut(self.land, 0, 0), p.dev(p.xs))
        self.go(2, self.cut(self.stage, 0, 1), self.cut(self.land, 0, 1), p.dev(p.ys))

        def sum_sides(i):
            rows = pl.ds(i, step)
            self.stage[1, rows, first] = self.both(xg, rows, first).astype(jnp.bfloat16)
            self.stage[2, rows, second] = self.both(yg, rows, second).astype(jnp.bfloat16)

        by_rows(self.gr, step, sum_sides)
        self.go(3, self.cut(self.stage, 1, 0), self.cut(self.land, 1, 0), p.dev(p.xs))
        self.go(4, self.cut(self.stage, 2, 1), self.cut(self.land, 2, 1), p.dev(p.ys))

    def sides_done(self):
        p, step = self.p, self.step
        for k, slot, which, bits, peer in ((5, 2, 0, 2, p.ys), (6, 1, 1, 1, p.xs)):
            self.got(k - 4, self.cut(self.land, 0, which))
            cols = pl.ds(which * self.half, self.half)
            g = self.near(bits)

            def add(i, slot=slot, cols=cols, g=g):
                rows = pl.ds(i, step)
                total = self.both(g, rows, cols) + self.land[0, rows, cols].astype(jnp.float32)
                self.stage[slot, rows, cols] = total.astype(jnp.bfloat16)

            by_rows(self.gr, step, add)
            self.go(k, self.cut(self.stage, slot, which), self.cut(self.land, slot, which), p.dev(peer))

    def mine_done(self):
        p, step = self.p, self.step
        me = p.group
        for k, slot, which in ((3, 1, 0), (4, 2, 1), (5, 2, 0), (6, 1, 1)):
            self.got(k, self.cut(self.land, slot, which))

        def total(rows, cols):
            sides = self.land[1, rows, cols].astype(jnp.float32)
            sides = sides + self.land[2, rows, cols].astype(jnp.float32)
            return self.both(me, rows, cols) + sides

        if self.turned:

            def turn(i):
                cols = pl.ds(pl.multiple_of(i, 128), 128)
                value = total(pl.ds(0, self.gr), cols).T
                self.mine[cols] = value
                self.zout[cols] = value.astype(jnp.bfloat16)

            by_rows(self.cols, 128, turn)
        else:

            def add(i):
                rows = pl.ds(i, step)
                value = total(rows, pl.ds(0, self.cols))
                self.mine[rows] = value
                self.zout[rows] = value.astype(jnp.bfloat16)

            by_rows(self.gr, step, add)
        for k in range(1, p.chain):
            z = p.zpeer(k)
            src = self.zout.at[pl.ds(pl.multiple_of(z * self.rows, self.rows), self.rows)]
            dst = self.zin.at[pl.ds((k - 1) * self.rows, self.rows)]
            self.go(6 + k, src, dst, p.dev(p.s, z))

    def done(self, result):
        p, step = self.p, self.step
        for k in range(1, p.chain):
            self.got(6 + k, self.zin.at[pl.ds((k - 1) * self.rows, self.rows)])
        start = p.z * self.rows

        def add(i):
            value = self.mine[pl.ds(pl.multiple_of(start + i, step), step)]
            for k in range(1, p.chain):
                value = value + self.zin[pl.ds((k - 1) * self.rows + i, step)].astype(jnp.float32)
            result[pl.ds(i, step)] = value

        by_rows(self.rows, step, add)

    def drain(self):
        for copy in self.sent:
            copy.wait_send()


SCATTER_SEMS = 10


def scatter_scratch(chain, rows, cols, flip):
    f32, bf16 = jnp.float32, jnp.bfloat16
    gr = chain * rows
    block = (cols, gr) if flip else (gr, cols)
    return [
        pltpu.VMEM((4, 2) + block, bf16),
        pltpu.VMEM((4,) + block, bf16),
        pltpu.VMEM((3,) + block, bf16),
        pltpu.VMEM((3,) + block, bf16),
        pltpu.VMEM((gr, cols), f32),
        pltpu.VMEM((gr, cols), bf16),
        pltpu.VMEM((max(1, chain - 1) * rows, cols), bf16),
    ]


class Exchange:
    def __init__(self, place, land, send, recv):
        self.p, self.land, self.send, self.recv = place, land, send, recv
        self.sent = []

    def go(self, source):
        p = self.p
        for d in range(1, 8):
            peer = lax.rem(p.s + d, 8)
            copy = remote(
                source(peer), self.land.at[p.s], self.send.at[d - 1], self.recv.at[d - 1], p.dev(peer)
            )
            copy.start()
            self.sent.append(copy)

    def wait(self):
        p = self.p
        for d in range(1, 8):
            ref = self.land.at[lax.rem(p.s + 8 - d, 8)]
            remote(ref, ref, self.send.at[d - 1], self.recv.at[d - 1], p.dev(p.sib)).wait_recv()

    def drain(self):
        for copy in self.sent:
            copy.wait_send()


def dot_nn(a, b):
    return lax.dot_general(a, b, (((1,), (0,)), ((), ())), preferred_element_type=jnp.float32)


def dot_nt(a, b):
    return lax.dot_general(a, b, (((1,), (1,)), ((), ())), preferred_element_type=jnp.float32)


def dot_tn(a, b):
    return lax.dot_general(a, b, (((0,), (0,)), ((), ())), preferred_element_type=jnp.float32)


def total_of(values):
    return jnp.sum(jnp.sum(values, 1, keepdims=True), 0, keepdims=True)


def fold_rows(values):
    rows, cols = values.shape
    return jnp.sum(values.reshape(rows // 8, 8, cols), 0)


NEG = -1e30
LEFT = math.sqrt(2.0 / math.pi)
CUBE = 0.044715


def layer_kernel(chain, names, *refs):
    r = dict(zip(names, refs))
    f32, bf16 = jnp.float32, jnp.bfloat16
    place = Place(chain)
    x_ref, dy_ref, docs_ref = r["tokens"], r["grad"], r["docs"]
    rows_all, width = x_ref.shape
    span = docs_ref.shape[1]
    spans = docs_ref.shape[0]
    pairs = width // 128
    hidden_size = r["w_up"].shape[1]
    devices = 8 * chain
    per = width // devices
    entries = 8 * spans * width
    chunk = 256
    chunks = rows_all // chunk

    gathers = {}
    for m, name in enumerate(("norm", "qkv", "out", "up", "down")):
        shard = r["s_" + name]
        g = Gather(place, r["w_" + name], shard.shape[0], r["gsend"].at[m], r["grecv"].at[m])
        g.own(place.z)[...] = shard[...].astype(bf16)
        gathers[name] = g
    scatters = {}
    for m, name in enumerate(("norm", "qkv", "out", "up", "down")):
        bufs = [r[f"c_{name}{i}"] for i in range(7)]
        scatters[name] = Scatter(
            place, r["s_" + name].shape[0], name == "down", bufs, r["csend"].at[m], r["crecv"].at[m]
        )
    first = Exchange(place, r["summ"], r["esend"].at[0], r["erecv"].at[0])
    second = Exchange(place, r["back"], r["esend"].at[1], r["erecv"].at[1])
    place.barrier()
    for name in ("norm", "qkv", "out", "up", "down"):
        gathers[name].start()

    F, mixed, heads = r["F"], r["mixed"], r["heads"]

    def norm_one(i):
        rows = pl.ds(i, 128)
        values = x_ref[rows].astype(f32)
        centre = values - jnp.mean(values, -1, keepdims=True)
        spread = jnp.mean(centre * centre, -1, keepdims=True)
        inv = lax.rsqrt(spread + 1e-05)
        F[rows] = centre * inv
        r["inv1"][rows] = jnp.broadcast_to(inv, (128, 128))

    gathers["norm"].chain_done()
    gathers["qkv"].chain_done()
    by_rows(rows_all, 128, norm_one)

    docs = docs_ref[...]
    wide = jnp.concatenate([docs] * (128 // spans), 0).T
    for p in range(spans):
        r["dcol"][pl.ds(p * span, span)] = jnp.broadcast_to(wide[:, p : p + 1], (span, 128))

    gathers["norm"].sides_done()
    gathers["qkv"].sides_done()
    for name in ("out", "up", "down"):
        gathers[name].chain_done()

    def turn_grad(i):
        rows = pl.ds(pl.multiple_of(i, 128), 128)
        r["dyT"][:, rows] = dy_ref[rows].T

    by_rows(rows_all, 128, turn_grad)
    gathers["norm"].corner_done()
    gathers["qkv"].corner_done()
    gathers["norm"].done()

    place_row = lax.broadcasted_iota(jnp.int32, (256, width), 0)
    place_col = lax.broadcasted_iota(jnp.int32, (256, width), 1)
    pick = (lax.rem(place_col, per) == place_row).astype(f32).astype(bf16)
    owner_row = lax.div(lax.broadcasted_iota(jnp.int32, (16 * devices, width), 0), 16)
    owner_col = lax.div(lax.broadcasted_iota(jnp.int32, (16 * devices, width), 1), per)
    spread_rows = dot_nn(r["w_norm"][...], pick)
    spread_rows = jnp.where(owner_row == owner_col, spread_rows, 0.0)
    norm_rows = jnp.sum(spread_rows.reshape(devices, 16, width), 0)
    r["nrows"][...] = norm_rows

    for name in ("out", "up", "down"):
        gathers[name].sides_done()
    gathers["qkv"].done()

    def project(i):
        rows = pl.ds(pl.multiple_of(i, chunk), chunk)
        act = (F[rows] * r["nrows"][0:1] + r["nrows"][1:2]).astype(bf16)
        r["act1T"][:, rows] = act.T
        mixed[rows] = dot_nn(act, r["w_qkv"][...]).astype(bf16)

    by_rows(rows_all, chunk, project)

    last_doc = docs[:, span - 1 : span]
    member = (docs == last_doc).astype(f32)
    count = jnp.sum(member, 1, keepdims=True)
    which = lax.broadcasted_iota(jnp.int32, (spans, span), 0)
    blocks = [jnp.where(which == p, member, 0.0) for p in range(spans)]
    left = jnp.concatenate(blocks, 1)
    left = jnp.concatenate([left, jnp.zeros_like(left)], 0).astype(bf16)
    means = dot_nn(left, mixed[:, width : 3 * width])[:spans] / count
    summ = r["summ"]
    summ[place.s, :, 0 : 2 * width] = means
    summ[place.s, :, 2 * width : 2 * width + 128] = jnp.broadcast_to(last_doc, (spans, 128))
    first.go(lambda peer: summ.at[place.s])
    for name in ("out", "up", "down"):
        gathers[name].corner_done()
    first.wait()

    sums = summ[...].reshape(8 * spans, 2 * width + 128)
    keys = sums[:, :width]
    stat_mean = total_of(keys) / entries
    centred = keys - stat_mean
    stat_var = total_of(centred * centred) / entries
    inv_sum = lax.rsqrt(stat_var + 1e-05)
    key_norm = centred * inv_sum
    r["knorm"][...] = key_norm
    lane = lax.broadcasted_iota(jnp.int32, (span, 128), 1)
    low_half = lane < 64
    lane_row = lax.broadcasted_iota(jnp.int32, (1, 128), 1)
    pick0 = (lane_row < 64).astype(f32).astype(bf16)
    pick1 = (lane_row >= 64).astype(f32).astype(bf16)
    for j in range(pairs):
        cols = slice(128 * j, 128 * j + 128)
        part = key_norm[:, cols].astype(bf16)
        r["KR"][j] = jnp.concatenate([part * pick0, part * pick1], 0)
        part = sums[:, width + 128 * j : width + 128 * j + 128].astype(bf16)
        r["VR"][j] = jnp.concatenate([part * pick0, part * pick1], 0)
    last = sums[:, 2 * width :]
    r["lastrow"][...] = jnp.concatenate([last, last], 0).T[0:8]

    probs = r["probs"]
    causal = lax.broadcasted_iota(jnp.int32, (span, 128), 0) >= lax.broadcasted_iota(
        jnp.int32, (span, 128), 1
    )
    span_first = place.s * spans

    def attend(p, carry):
        rows = pl.ds(pl.multiple_of(p * span, span), span)
        column = r["dcol"][rows]
        mask_local = (column == docs_ref[pl.ds(p, 1)]) & causal
        mask_remote = (column == r["lastrow"][0:1]) & (lax.rem(lane, 64) < span_first + p)
        for j in range(pairs):
            query = mixed[rows, 128 * j : 128 * j + 128]
            key = mixed[rows, width + 128 * j : width + 128 * j + 128]
            value = mixed[rows, 2 * width + 128 * j : 2 * width + 128 * j + 128]
            stack = jnp.concatenate([key * pick0, key * pick1], 0)
            local = dot_nt(query, stack) * 0.125
            far = jnp.where(mask_remote, dot_nt(query, r["KR"][j]) * 0.125, NEG)
            one = jnp.where(mask_local, local[:, :128], NEG)
            two = jnp.where(mask_local, local[:, 128:], NEG)
            peak1 = jnp.max(jnp.maximum(one, jnp.where(low_half, far, NEG)), -1, keepdims=True)
            peak2 = jnp.max(jnp.maximum(two, jnp.where(low_half, NEG, far)), -1, keepdims=True)
            one = jnp.exp(one - peak1)
            two = jnp.exp(two - peak2)
            far = jnp.exp(far - jnp.where(low_half, peak1, peak2))
            scale1 = 1.0 / jnp.sum(one + jnp.where(low_half, far, 0.0), -1, keepdims=True)
            scale2 = 1.0 / jnp.sum(two + jnp.where(low_half, 0.0, far), -1, keepdims=True)
            one = one * scale1
            two = two * scale2
            far = far * jnp.where(low_half, scale1, scale2)
            base = 384 * j
            probs[rows, base : base + 128] = one
            probs[rows, base + 128 : base + 256] = two
            probs[rows, base + 256 : base + 384] = far
            low = jnp.concatenate([one, two, far], 1).astype(bf16)
            values = jnp.concatenate([value * pick0, value * pick1, r["VR"][j]], 0)
            heads[rows, 128 * j : 128 * j + 128] = dot_nn(low, values).astype(bf16)
        return carry

    lax.fori_loop(0, spans, attend, 0)
    for name in ("out", "up", "down"):
        gathers[name].done()

    r["ngrad"][...] = jnp.zeros_like(r["ngrad"])
    tile = 256

    def feed(i):
        rows = pl.ds(pl.multiple_of(i, chunk), chunk)
        part = heads[rows]
        r["headsT"][:, rows] = part.T
        after = x_ref[rows].astype(f32) + dot_nn(part, r["w_out"][...])
        centre = after - jnp.mean(after, -1, keepdims=True)
        spread = jnp.mean(centre * centre, -1, keepdims=True)
        inv = lax.rsqrt(spread + 1e-05)
        normal = centre * inv
        F[rows] = after
        r["n2"][...] = normal
        r["inv2"][...] = jnp.broadcast_to(inv, (chunk, 128))
        act_two = (normal * r["nrows"][2:3] + r["nrows"][3:4]).astype(bf16)
        r["act2"][...] = act_two
        r["act2T"][:, rows] = act_two.T

        def mlp(c, carry):
            for half in range(2):
                cols = pl.ds(pl.multiple_of(c * 2 * tile + half * tile, tile), tile)
                h = dot_nn(r["act2"][...], r["w_up"][:, cols])
                d = dot_nt(dy_ref[rows], r["w_down"][cols])
                square = h * h
                t = jnp.tanh(h * (LEFT + (LEFT * CUBE) * square))
                halved = 0.5 * h
                r["act3"][rows, cols] = (halved + halved * t).astype(bf16)
                slope = 0.5 + 0.5 * t + halved * (1.0 - t * t) * (LEFT + (3.0 * LEFT * CUBE) * square)
                r["dhid"][rows, cols] = (d * slope).astype(bf16)
            return carry

        lax.fori_loop(0, hidden_size // (2 * tile), mlp, 0)
        result = F[rows] + dot_nn(r["act3"][rows], r["w_down"][...])
        r["block_out"][rows] = result.astype(bf16)
        d_two = dot_nt(r["dhid"][rows], r["w_up"][...])
        normal = r["n2"][...]
        r["ngrad"][2] += fold_rows(d_two * normal)
        r["ngrad"][3] += fold_rows(d_two)
        scaled = d_two * r["nrows"][2:3]
        centred = (
            scaled
            - jnp.mean(scaled, -1, keepdims=True)
            - normal * jnp.mean(scaled * normal, -1, keepdims=True)
        )
        d_after = dy_ref[rows].astype(f32) + r["inv2"][:, 0:1] * centred
        F[rows] = d_after
        low = d_after.astype(bf16)
        r["dafter"][rows] = low
        heads[rows] = dot_nt(low, r["w_out"][...]).astype(bf16)

    by_rows(rows_all, chunk, feed)

    down, up, out = scatters["down"], scatters["up"], scatters["out"]
    gw = down.cols

    def down_part(g, carry):
        cols = pl.ds(pl.multiple_of(g * 2 * gw, 2 * gw), 2 * gw)
        grad = dot_nn(r["dyT"][...], r["act3"][:, cols]).astype(bf16)
        down.full[g, 0] = grad[:, :gw]
        down.full[g, 1] = grad[:, gw:]
        return carry

    lax.fori_loop(0, 4, down_part, 0)
    down.start()

    def put(target, grad, cols):
        gr = target.gr
        for g in range(4):
            for c in range(2):
                k = (2 * g + c) * gr
                target.full[g, c, :, cols] = grad[k : k + gr]

    def up_part(c, carry):
        cols = pl.ds(pl.multiple_of(c * 512, 512), 512)
        put(up, dot_nn(r["act2T"][...], r["dhid"][:, cols]).astype(bf16), cols)
        return carry

    lax.fori_loop(0, hidden_size // 512, up_part, 0)
    up.start()
    down.core_done()
    put(out, dot_nn(r["headsT"][...], r["dafter"][...]).astype(bf16), pl.ds(0, width))
    out.start()

    r["dKR"][...] = jnp.zeros_like(r["dKR"])
    r["dVR"][...] = jnp.zeros_like(r["dVR"])
    dkey, dvalue = r["input_grad"], r["dvalue"]

    def attend_back(p, carry):
        rows = pl.ds(pl.multiple_of(p * span, span), span)
        for j in range(pairs):
            at = slice(128 * j, 128 * j + 128)
            query = mixed[rows, at]
            key = mixed[rows, width + 128 * j : width + 128 * j + 128]
            value = mixed[rows, 2 * width + 128 * j : 2 * width + 128 * j + 128]
            d_head = heads[rows, at]
            keys_all = jnp.concatenate([key * pick0, key * pick1, r["KR"][j]], 0)
            values_all = jnp.concatenate([value * pick0, value * pick1, r["VR"][j]], 0)
            d_probs = dot_nt(d_head, values_all)
            base = 384 * j
            one = probs[rows, base : base + 128]
            two = probs[rows, base + 128 : base + 256]
            far = probs[rows, base + 256 : base + 384]
            d_far = far * d_probs[:, 256:]
            sum1 = jnp.sum(one * d_probs[:, :128] + jnp.where(low_half, d_far, 0.0), -1, keepdims=True)
            sum2 = jnp.sum(two * d_probs[:, 128:256] + jnp.where(low_half, 0.0, d_far), -1, keepdims=True)
            d_one = one * (d_probs[:, :128] - sum1)
            d_two = two * (d_probs[:, 128:256] - sum2)
            d_far = far * (d_probs[:, 256:] - jnp.where(low_half, sum1, sum2))
            d_scores = jnp.concatenate([d_one, d_two, d_far], 1).astype(bf16)
            low = jnp.concatenate([one, two, far], 1).astype(bf16)
            d_keys = dot_tn(d_scores, query)
            d_values = dot_tn(low, d_head)
            mixed[rows, at] = (0.125 * dot_nn(d_scores, keys_all)).astype(bf16)
            dkey[rows, at] = 0.125 * jnp.where(low_half, d_keys[:128], d_keys[128:256])
            dvalue[rows, at] = jnp.where(low_half, d_values[:128], d_values[128:256])
            r["dKR"][j] += d_keys[256:]
            r["dVR"][j] += d_values[256:]
        return carry

    quarter = spans // 4
    lax.fori_loop(0, quarter, attend_back, 0)
    up.core_done()
    down.sides_done()
    lax.fori_loop(quarter, 2 * quarter, attend_back, 0)
    out.core_done()
    up.sides_done()
    down.mine_done()
    lax.fori_loop(2 * quarter, 3 * quarter, attend_back, 0)
    out.sides_done()
    up.mine_done()
    lax.fori_loop(3 * quarter, spans, attend_back, 0)
    out.mine_done()

    half_spans = 8 * spans
    parts = []
    for name, factor in (("dKR", 0.125), ("dVR", 1.0)):
        for j in range(pairs):
            both = r[name][j]
            low = low_half[:half_spans]
            parts.append(factor * jnp.where(low, both[:half_spans], both[half_spans:]))
    d_keys = jnp.concatenate(parts[:pairs], 1)
    d_values = jnp.concatenate(parts[pairs:], 1)
    key_norm = r["knorm"][...]
    flat = jnp.where(lane_row < 64, total_of(d_keys), total_of(d_keys * key_norm))
    send = r["sendback"]
    send[:, :, 0:width] = d_keys.reshape(8, spans, width)
    send[:, :, width : 2 * width] = d_values.reshape(8, spans, width)
    send[:, :, 2 * width :] = jnp.broadcast_to(flat.reshape(1, 1, 128), (8, spans, 128))
    back = r["back"]
    back[place.s] = send[place.s]
    second.go(lambda peer: send.at[peer])

    qkv = scatters["qkv"]
    put(qkv, dot_nn(r["act1T"][...], mixed[:, :width]).astype(bf16), pl.ds(0, width))
    second.wait()

    owned = jnp.sum(back[...], 0)
    back_sum = owned[0:1, 2 * width : 2 * width + 1]
    back_cross = owned[0:1, 2 * width + 64 : 2 * width + 65]
    mine_norm = r["knorm"][pl.ds(pl.multiple_of(place.s * spans, spans), spans)]
    d_sum_key = inv_sum * (
        owned[:, :width] - back_sum * (1.0 / entries) - mine_norm * (back_cross * (1.0 / entries))
    )
    r["dsum"][:, 0:width] = d_sum_key / count
    r["dsum"][:, width : 2 * width] = owned[:, width : 2 * width] / count
    slot = lax.broadcasted_iota(jnp.int32, (8, 128), 1)
    stats = jnp.where(slot == 0, stat_mean, stat_var)
    stats = jnp.where(slot == 2, -inv_sum * back_sum, stats)
    stats = jnp.where(slot == 3, -0.5 * inv_sum * inv_sum * back_cross, stats)
    r["stats"][...] = stats

    def join(p, carry):
        rows = pl.ds(pl.multiple_of(p * span, span), span)
        final = docs_ref[pl.ds(p, 1)][:, span - 1 : span]
        share = (r["dcol"][rows] == final).astype(f32)
        sums_row = r["dsum"][pl.ds(p, 1)]
        for j in range(pairs):
            at = slice(128 * j, 128 * j + 128)
            past = slice(width + 128 * j, width + 128 * j + 128)
            full = dkey[rows, at] + share * sums_row[:, at]
            mixed[rows, past] = full.astype(bf16)
            full = dvalue[rows, at] + share * sums_row[:, past]
            mixed[rows, 2 * width + 128 * j : 2 * width + 128 * j + 128] = full.astype(bf16)
        return carry

    lax.fori_loop(0, spans, join, 0)

    def qkv_part(c, carry):
        cols = pl.ds(pl.multiple_of(c * width, width), width)
        put(qkv, dot_nn(r["act1T"][...], mixed[:, cols]).astype(bf16), cols)
        return carry

    lax.fori_loop(1, 3, qkv_part, 0)
    qkv.start()

    def first_back(i):
        rows = pl.ds(pl.multiple_of(i, chunk), chunk)
        d_one = dot_nt(mixed[rows], r["w_qkv"][...])
        values = x_ref[rows].astype(f32)
        inv = r["inv1"][rows][:, 0:1]
        normal = (values - jnp.mean(values, -1, keepdims=True)) * inv
        r["ngrad"][0] += fold_rows(d_one * normal)
        r["ngrad"][1] += fold_rows(d_one)
        scaled = d_one * r["nrows"][0:1]
        centred = (
            scaled
            - jnp.mean(scaled, -1, keepdims=True)
            - normal * jnp.mean(scaled * normal, -1, keepdims=True)
        )
        r["input_grad"][rows] = F[rows] + inv * centred

    half_chunks = chunks // 2
    lax.fori_loop(0, half_chunks, lambda i, c: (first_back(i * chunk), c)[1], 0)
    qkv.core_done()
    lax.fori_loop(half_chunks, chunks, lambda i, c: (first_back(i * chunk), c)[1], 0)

    pieces = jnp.concatenate(
        [jnp.sum(r["ngrad"][k], 0, keepdims=True) for k in range(4)]
        + [jnp.zeros((12, width), f32)],
        0,
    )
    spread_rows = jnp.broadcast_to(pieces[None], (devices, 16, width)).reshape(16 * devices, width)
    spread_rows = jnp.where(owner_row == owner_col, spread_rows, 0.0).astype(bf16)
    norm = scatters["norm"]
    put(norm, dot_nt(spread_rows, pick).astype(bf16), pl.ds(0, 256))
    norm.start()
    qkv.sides_done()
    norm.core_done()
    norm.sides_done()
    qkv.mine_done()
    norm.mine_done()
    for name in ("down", "up", "out", "qkv", "norm"):
        scatters[name].done(r["g_" + name])
    for part in list(gathers.values()) + list(scatters.values()) + [first, second]:
        part.drain()


def fused_layer(chain, tokens, grad, docs, shards):
    f32, bf16 = jnp.float32, jnp.bfloat16
    rows, width = tokens.shape
    spans = docs.shape[0]
    order = ("norm", "qkv", "out", "up", "down")
    devices = 8 * chain
    ins = [("tokens", tokens), ("grad", grad), ("docs", docs)]
    ins += [("s_" + name, shards[name]) for name in order]
    outs = [
        ("block_out", jax.ShapeDtypeStruct((rows, width), bf16)),
        ("input_grad", jax.ShapeDtypeStruct((rows, width), f32)),
        ("stats", jax.ShapeDtypeStruct((8, 128), f32)),
    ]
    outs += [("g_" + name, jax.ShapeDtypeStruct(shards[name].shape, f32)) for name in order]
    hidden = shards["up"].shape[1]
    scratch = {}
    for name in order:
        piece, cols = shards[name].shape
        scratch["w_" + name] = pltpu.VMEM((devices * piece, cols), bf16)
        for i, buf in enumerate(scatter_scratch(chain, piece, cols, name == "down")):
            scratch[f"c_{name}{i}"] = buf
    payload = (8, spans, 2 * width + 128)
    pairs = width // 128
    scratch |= {
        "gsend": DMA((5, GATHER_SEMS)),
        "grecv": DMA((5, GATHER_SEMS)),
        "csend": DMA((5, SCATTER_SEMS)),
        "crecv": DMA((5, SCATTER_SEMS)),
        "esend": DMA((2, 7)),
        "erecv": DMA((2, 7)),
        "summ": pltpu.VMEM(payload, f32),
        "back": pltpu.VMEM(payload, f32),
        "sendback": pltpu.VMEM(payload, f32),
        "F": pltpu.VMEM((rows, width), f32),
        "inv1": pltpu.VMEM((rows, 128), f32),
        "dcol": pltpu.VMEM((rows, 128), f32),
        "nrows": pltpu.VMEM((16, width), f32),
        "ngrad": pltpu.VMEM((4, 8, width), f32),
        "act1T": pltpu.VMEM((width, rows), bf16),
        "dyT": pltpu.VMEM((width, rows), bf16),
        "act2T": pltpu.VMEM((width, rows), bf16),
        "headsT": pltpu.VMEM((width, rows), bf16),
        "mixed": pltpu.VMEM((rows, 3 * width), bf16),
        "probs": pltpu.VMEM((rows, 384 * pairs), f32),
        "heads": pltpu.VMEM((rows, width), bf16),
        "knorm": pltpu.VMEM((8 * spans, width), f32),
        "KR": pltpu.VMEM((pairs, 128, 128), bf16),
        "VR": pltpu.VMEM((pairs, 128, 128), bf16),
        "dKR": pltpu.VMEM((pairs, 128, 128), f32),
        "dVR": pltpu.VMEM((pairs, 128, 128), f32),
        "lastrow": pltpu.VMEM((8, 128), f32),
        "n2": pltpu.VMEM((256, width), f32),
        "inv2": pltpu.VMEM((256, 128), f32),
        "act2": pltpu.VMEM((256, width), bf16),
        "act3": pltpu.VMEM((rows, hidden), bf16),
        "dhid": pltpu.VMEM((rows, hidden), bf16),
        "dafter": pltpu.VMEM((rows, width), bf16),
        "dvalue": pltpu.VMEM((rows, width), f32),
        "dsum": pltpu.VMEM((spans, 2 * width), f32),
    }
    names = [n for n, _ in ins] + [n for n, _ in outs] + list(scratch)
    vmem = pl.BlockSpec(memory_space=pltpu.VMEM)
    result = pl.pallas_call(
        functools.partial(layer_kernel, chain, names),
        out_shape=[shape for _, shape in outs],
        in_specs=[vmem] * len(ins),
        out_specs=[vmem] * len(outs),
        scratch_shapes=list(scratch.values()),
        compiler_params=pltpu.CompilerParams(
            collective_id=0, has_side_effects=True, vmem_limit_bytes=63 * 2**20
        ),
    )(*[value for _, value in ins])
    return dict(zip([n for n, _ in outs], result))


def norm_forward(values, gain_row, shift_row):
    centre = values - jnp.mean(values, -1, keepdims=True)
    spread = jnp.mean(centre * centre, -1, keepdims=True)
    inv_std = lax.rsqrt(spread + 1e-05)
    normal = centre * inv_std
    return (normal * gain_row + shift_row, normal, inv_std)


def norm_backward(grad_in, normal, inv_std, gain_row):
    scaled = grad_in * gain_row
    centred = (
        scaled
        - jnp.mean(scaled, -1, keepdims=True)
        - normal * jnp.mean(scaled * normal, -1, keepdims=True)
    )
    return (inv_std * centred, jnp.sum(grad_in * normal, 0), jnp.sum(grad_in, 0))


def gelu_tanh(values):
    return jax.nn.gelu(values, approximate=True)


def span_probs(query_blk, key_blk, key_remote, doc_span, last_remote, span_first):
    span_len = doc_span.shape[2]
    local = (
        jnp.einsum("bpqhe,bpkhe->bphqk", query_blk, key_blk, preferred_element_type=jnp.float32)
        * 0.125
    )
    remote = (
        jnp.einsum("bpqhe,bnhe->bphqn", query_blk, key_remote, preferred_element_type=jnp.float32)
        * 0.125
    )
    positions = jnp.arange(span_len)
    causal = positions[:, None] >= positions[None, :]
    same_doc = doc_span[:, :, :, None] == doc_span[:, :, None, :]
    mask_local = (same_doc & causal[None, None])[:, :, None]
    span_ids = span_first + jnp.arange(doc_span.shape[1])
    earlier = jnp.arange(key_remote.shape[1])[None, :] < span_ids[:, None]
    doc_float = doc_span.astype(jnp.float32)
    match = doc_float[:, :, :, None] == last_remote.astype(jnp.float32)[:, None, None, :]
    mask_remote = (match & earlier[None, :, None, :])[:, :, None]
    allowed = jnp.concatenate([mask_local, mask_remote], -1)
    scores = jnp.where(allowed, jnp.concatenate([local, remote], -1), -1e30)
    peak_score = jnp.max(scores, -1, keepdims=True)
    raised = jnp.exp(scores - peak_score)
    return raised / jnp.sum(raised, -1, keepdims=True)


def advance(weight, moment, average, grad, rate):
    new_moment = 0.9 * moment + rate * grad
    new_weight = weight - (rate * grad + 0.9 * new_moment)
    new_average = 0.99 * average + 0.01 * new_weight
    return jnp.stack([new_weight, new_moment, new_average])


def shards_plain(
    tokens,
    grad_out,
    doc_ids,
    qkv_w,
    qkv_m,
    qkv_a,
    out_w,
    out_m,
    out_a,
    up_w,
    up_m,
    up_a,
    down_w,
    down_m,
    down_a,
    norm_w,
    norm_m,
    norm_a,
):
    seqs, seq_len, width = tokens.shape
    span_len = SPAN
    cycle_size = lax.axis_size("seq")
    cycle_rank = lax.axis_index("seq")
    spans_dev = seq_len // span_len
    spans_all = spans_dev * cycle_size
    rows_dev = seqs * seq_len
    head_size = width // H
    bf16 = jnp.bfloat16
    f32 = jnp.float32
    w_qkv, w_out, w_up, w_down, norm_low = (
        lax.all_gather(qkv_w.astype(bf16), ("seq", "dp"), axis=0, tiled=True),
        lax.all_gather(out_w.astype(bf16), ("seq", "dp"), axis=0, tiled=True),
        lax.all_gather(up_w.astype(bf16), ("seq", "dp"), axis=0, tiled=True),
        lax.all_gather(down_w.astype(bf16), ("seq", "dp"), axis=0, tiled=True),
        lax.all_gather(norm_w.astype(bf16), ("seq", "dp"), axis=1, tiled=True),
    )
    norm_rows = norm_low.astype(f32)
    inputs = tokens.reshape(rows_dev, width).astype(f32)
    normed_one, normal_one, inv_one = norm_forward(inputs, norm_rows[0], norm_rows[1])
    act_one = normed_one.astype(bf16)
    mixed = jnp.dot(act_one, w_qkv, preferred_element_type=f32)
    query = mixed[:, :width].astype(bf16)
    key_all = mixed[:, width : 2 * width].astype(bf16)
    value_all = mixed[:, 2 * width :].astype(bf16)
    block_shape = (seqs, spans_dev, span_len, H, head_size)
    query_blk = query.reshape(block_shape)
    key_blk = key_all.reshape(block_shape)
    value_blk = value_all.reshape(block_shape)
    doc_span = doc_ids.reshape(seqs, spans_dev, span_len)
    last_doc = doc_span[:, :, -1]
    member = (doc_span == last_doc[:, :, None]).astype(f32)
    counts = jnp.sum(member, -1)
    member_low = member.astype(bf16)
    key_four = key_all.reshape(seqs, spans_dev, span_len, width)
    value_four = value_all.reshape(seqs, spans_dev, span_len, width)
    sum_key = (
        jnp.einsum("bpt,bptd->bpd", member_low, key_four, preferred_element_type=f32)
        / counts[..., None]
    )
    sum_value = (
        jnp.einsum("bpt,bptd->bpd", member_low, value_four, preferred_element_type=f32)
        / counts[..., None]
    )
    total_sum, total_square = lax.psum(
        (jnp.sum(sum_key, (1, 2)), jnp.sum(sum_key * sum_key, (1, 2))), "seq"
    )
    entries = spans_all * width
    stat_mean = total_sum / entries
    stat_var = total_square / entries - stat_mean * stat_mean
    inv_sum = lax.rsqrt(stat_var + 1e-05)
    key_norm = (sum_key - stat_mean[:, None, None]) * inv_sum[:, None, None]
    key_send = key_norm.astype(bf16)
    value_send = sum_value.astype(bf16)
    last_send = last_doc.astype(bf16)
    key_remote, value_remote, last_remote = (
        lax.all_gather(key_send, "seq", axis=1, tiled=True),
        lax.all_gather(value_send, "seq", axis=1, tiled=True),
        lax.all_gather(last_send, "seq", axis=1, tiled=True),
    )
    remote_shape = (seqs, spans_all, H, head_size)
    span_first = cycle_rank * spans_dev
    probs = span_probs(
        query_blk, key_blk, key_remote.reshape(remote_shape), doc_span, last_remote, span_first
    )
    probs_low = probs.astype(bf16)
    attended = jnp.einsum(
        "bphqk,bpkhe->bpqhe", probs_low[..., :span_len], value_blk, preferred_element_type=f32
    )
    attended = attended + jnp.einsum(
        "bphqn,bnhe->bpqhe",
        probs_low[..., span_len:],
        value_remote.reshape(remote_shape),
        preferred_element_type=f32,
    )
    heads_out = attended.reshape(rows_dev, width).astype(bf16)
    after_attn = inputs + jnp.dot(heads_out, w_out, preferred_element_type=f32)
    normed_two, normal_two, inv_two = norm_forward(after_attn, norm_rows[2], norm_rows[3])
    act_two = normed_two.astype(bf16)
    hidden = jnp.dot(act_two, w_up, preferred_element_type=f32)
    act_three = gelu_tanh(hidden).astype(bf16)
    result = after_attn + jnp.dot(act_three, w_down, preferred_element_type=f32)
    block_out = result.astype(bf16).reshape(seqs, seq_len, width)
    stats_out = jnp.stack([stat_mean, stat_var], -1)
    grad_low = grad_out.reshape(rows_dev, width)
    grad_down = jnp.einsum("tf,td->fd", act_three, grad_low, preferred_element_type=f32)
    d_three = jnp.einsum("td,fd->tf", grad_low, w_down, preferred_element_type=f32)
    unused_out, gelu_pull = jax.vjp(gelu_tanh, hidden)
    d_hidden = gelu_pull(d_three)[0].astype(bf16)
    grad_up = jnp.einsum("td,tf->df", act_two, d_hidden, preferred_element_type=f32)
    d_two = jnp.einsum("tf,df->td", d_hidden, w_up, preferred_element_type=f32)
    d_norm_two, gain_two, shift_two = norm_backward(d_two, normal_two, inv_two, norm_rows[2])
    d_after = grad_low.astype(f32) + d_norm_two
    d_after_low = d_after.astype(bf16)
    grad_outw = jnp.einsum("tc,td->cd", heads_out, d_after_low, preferred_element_type=f32)
    d_heads = jnp.einsum("td,cd->tc", d_after_low, w_out, preferred_element_type=f32).astype(bf16)
    key_back, value_back, last_back = (key_remote, value_remote, last_remote)
    key_back_blk = key_back.reshape(remote_shape)
    value_back_blk = value_back.reshape(remote_shape)
    probs_back = span_probs(query_blk, key_blk, key_back_blk, doc_span, last_back, span_first)
    probs_back_low = probs_back.astype(bf16)
    d_heads_blk = d_heads.reshape(block_shape)
    d_probs = jnp.concatenate(
        [
            jnp.einsum("bpqhe,bpkhe->bphqk", d_heads_blk, value_blk, preferred_element_type=f32),
            jnp.einsum(
                "bpqhe,bnhe->bphqn", d_heads_blk, value_back_blk, preferred_element_type=f32
            ),
        ],
        -1,
    )
    row_dot = jnp.sum(probs_back * d_probs, -1, keepdims=True)
    d_scores = (probs_back * (d_probs - row_dot)).astype(bf16)
    d_local = d_scores[..., :span_len]
    d_remote = d_scores[..., span_len:]
    d_query = 0.125 * (
        jnp.einsum("bphqk,bpkhe->bpqhe", d_local, key_blk, preferred_element_type=f32)
        + jnp.einsum("bphqn,bnhe->bpqhe", d_remote, key_back_blk, preferred_element_type=f32)
    )
    d_key = 0.125 * jnp.einsum("bphqk,bpqhe->bpkhe", d_local, query_blk, preferred_element_type=f32)
    d_value = jnp.einsum(
        "bphqk,bpqhe->bpkhe",
        probs_back_low[..., :span_len],
        d_heads_blk,
        preferred_element_type=f32,
    )
    d_key_sum = (
        0.125 * jnp.einsum("bphqn,bpqhe->bnhe", d_remote, query_blk, preferred_element_type=f32)
    ).reshape(seqs, spans_all, width)
    d_value_sum = jnp.einsum(
        "bphqn,bpqhe->bnhe", probs_back_low[..., span_len:], d_heads_blk, preferred_element_type=f32
    ).reshape(seqs, spans_all, width)
    owned_key, owned_value = (
        lax.psum_scatter(
            d_key_sum.astype(jnp.bfloat16), "seq", scatter_dimension=1, tiled=True
        ).astype(jnp.float32),
        lax.psum_scatter(
            d_value_sum.astype(jnp.bfloat16), "seq", scatter_dimension=1, tiled=True
        ).astype(jnp.float32),
    )
    back_sum, back_cross = lax.psum(
        (jnp.sum(owned_key, (1, 2)), jnp.sum(owned_key * key_norm, (1, 2))), "seq"
    )
    stat_grads = jnp.stack([-inv_sum * back_sum, -0.5 * inv_sum * inv_sum * back_cross], -1)
    d_sum_key = inv_sum[:, None, None] * (
        owned_key
        - back_sum[:, None, None] / entries
        - key_norm * back_cross[:, None, None] / entries
    )
    share = member / counts[..., None]
    d_key_all = (
        d_key.reshape(seqs, spans_dev, span_len, width)
        + share[..., None] * d_sum_key[:, :, None, :]
    )
    d_value_all = (
        d_value.reshape(seqs, spans_dev, span_len, width)
        + share[..., None] * owned_value[:, :, None, :]
    )
    d_mixed = jnp.concatenate(
        [
            d_query.reshape(rows_dev, width),
            d_key_all.reshape(rows_dev, width),
            d_value_all.reshape(rows_dev, width),
        ],
        -1,
    ).astype(bf16)
    grad_qkv = jnp.einsum("td,tf->df", act_one, d_mixed, preferred_element_type=f32)
    d_one = jnp.einsum("tf,df->td", d_mixed, w_qkv, preferred_element_type=f32)
    d_norm_one, gain_one, shift_one = norm_backward(d_one, normal_one, inv_one, norm_rows[0])
    input_grad = (d_after + d_norm_one).reshape(seqs, seq_len, width)
    grad_norm = jnp.stack([gain_one, shift_one, gain_two, shift_two])
    sum_qkv, sum_outw, sum_up, sum_down, sum_norm = (
        lax.psum_scatter(grad_qkv, ("seq", "dp"), scatter_dimension=0, tiled=True),
        lax.psum_scatter(grad_outw, ("seq", "dp"), scatter_dimension=0, tiled=True),
        lax.psum_scatter(grad_up, ("seq", "dp"), scatter_dimension=0, tiled=True),
        lax.psum_scatter(grad_down, ("seq", "dp"), scatter_dimension=0, tiled=True),
        lax.psum_scatter(grad_norm, ("seq", "dp"), scatter_dimension=1, tiled=True),
    )
    tokens_all = rows_dev * cycle_size * lax.axis_size("dp")
    rate = 0.02 / math.sqrt(tokens_all)
    return (
        block_out,
        input_grad,
        stats_out,
        stat_grads,
        advance(qkv_w, qkv_m, qkv_a, sum_qkv, rate),
        advance(out_w, out_m, out_a, sum_outw, rate),
        advance(up_w, up_m, up_a, sum_up, rate),
        advance(down_w, down_m, down_a, sum_down, rate),
        advance(norm_w, norm_m, norm_a, sum_norm, rate),
    )


def shards(*args):
    tokens, grad_out, doc_ids = args[:3]
    qkv_w, norm_w = args[3], args[15]
    seqs, seq_len, width = tokens.shape
    fits = lax.axis_size("seq") == 8 and qkv_w.shape[0] % 16 == 0
    fits = fits and seqs == 1 and seq_len == 8 * SPAN and width == 512
    if not fits:
        return shards_plain(*args)
    f32 = jnp.float32
    chain = lax.axis_size("dp")
    per = norm_w.shape[1]
    pieces = {
        "norm": jnp.pad(norm_w, ((0, 12), (0, 256 - per))),
        "qkv": qkv_w,
        "out": args[6],
        "up": args[9],
        "down": args[12],
    }
    docs = doc_ids.reshape(8, SPAN).astype(f32)
    done = fused_layer(
        chain, tokens.reshape(seq_len, width), grad_out.reshape(seq_len, width), docs, pieces
    )
    rate = 0.02 / math.sqrt(seq_len * 8 * chain)
    states = []
    for name, k in (("qkv", 3), ("out", 6), ("up", 9), ("down", 12)):
        states.append(advance(args[k], args[k + 1], args[k + 2], done["g_" + name], rate))
    grad_norm = done["g_norm"][:4, :per]
    states.append(advance(args[15], args[16], args[17], grad_norm, rate))
    stats = done["stats"]
    return (
        done["block_out"].reshape(tokens.shape),
        done["input_grad"].reshape(tokens.shape),
        stats[0:1, 0:2],
        stats[0:1, 2:4],
        *states,
    )


def solution(mesh):
    placed = (
        P("dp", "seq", None),
        P("dp", "seq", None),
        P("dp", "seq"),
        P(("seq", "dp"), None),
        P(("seq", "dp"), None),
        P(("seq", "dp"), None),
        P(("seq", "dp"), None),
        P(("seq", "dp"), None),
        P(("seq", "dp"), None),
        P(("seq", "dp"), None),
        P(("seq", "dp"), None),
        P(("seq", "dp"), None),
        P(("seq", "dp"), None),
        P(("seq", "dp"), None),
        P(("seq", "dp"), None),
        P(None, ("seq", "dp")),
        P(None, ("seq", "dp")),
        P(None, ("seq", "dp")),
    )
    return jax.shard_map(
        shards,
        mesh=mesh,
        in_specs=placed,
        out_specs=(
            P("dp", "seq", None),
            P("dp", "seq", None),
            P("dp", None),
            P("dp", None),
            P(None, ("seq", "dp"), None),
            P(None, ("seq", "dp"), None),
            P(None, ("seq", "dp"), None),
            P(None, ("seq", "dp"), None),
            P(None, None, ("seq", "dp")),
        ),
        check_vma=False,
    )
```

```python
import functools
import math

import jax
import jax.numpy as jnp
from jax import lax
from jax.experimental import pallas as pl
from jax.experimental.pallas import tpu as pltpu
from jax.sharding import PartitionSpec as P

H = 8
SPAN = 128
MESH = pl.DeviceIdType.MESH
DMA = pltpu.SemaphoreType.DMA


class Place:
    def __init__(self, chain):
        self.chain = chain
        self.s = lax.axis_index("seq")
        self.z = lax.axis_index("dp")
        self.core = lax.rem(self.s, 2)
        self.group = lax.div(self.s, 2)
        self.sib = self.flip(self.s, 1)
        self.xs = self.flip(self.s, 2)
        self.ys = self.flip(self.s, 4)
        self.ds = self.flip(self.xs, 4)

    @staticmethod
    def flip(value, bit):
        return value + bit - 2 * bit * lax.rem(lax.div(value, bit), 2)

    def dev(self, s, z=None):
        return {"seq": s, "dp": self.z if z is None else z}

    def zpeer(self, step):
        return lax.rem(self.z + step, self.chain)

    def barrier(self, extra=()):
        sem = pltpu.get_barrier_semaphore()
        peers = [self.dev(self.sib), self.dev(self.xs), self.dev(self.ys)]
        peers += [self.dev(self.s, self.zpeer(k)) for k in range(1, self.chain)]
        peers += list(extra)
        for peer in peers:
            pl.semaphore_signal(sem, inc=1, device_id=peer, device_id_type=MESH)
        pl.semaphore_wait(sem, len(peers))


def remote(src, dst, send, recv, peer):
    return pltpu.make_async_remote_copy(
        src_ref=src, dst_ref=dst, send_sem=send, recv_sem=recv, device_id=peer, device_id_type=MESH
    )


class Gather:
    def __init__(self, place, full, rows, send, recv):
        self.p, self.full, self.rows = place, full, rows
        self.send, self.recv = send, recv
        self.gr = place.chain * rows
        self.half = full.shape[1] // 2
        self.sent = []

    def region(self, s, cols=None):
        rows = pl.ds(pl.multiple_of(s * self.gr, self.gr), self.gr)
        if cols is None:
            return self.full.at[rows]
        return self.full.at[rows, cols]

    def own(self, z):
        start = pl.multiple_of(self.p.s * self.gr + z * self.rows, self.rows)
        return self.full.at[pl.ds(start, self.rows)]

    def go(self, k, ref, peer):
        copy = remote(ref, ref, self.send.at[k], self.recv.at[k], peer)
        copy.start()
        self.sent.append(copy)

    def got(self, k, ref):
        remote(ref, ref, self.send.at[k], self.recv.at[k], self.p.dev(self.p.sib)).wait_recv()

    def start(self):
        p = self.p
        for k in range(1, p.chain):
            self.go(k - 1, self.own(p.z), p.dev(p.s, p.zpeer(k)))

    def chain_done(self):
        p = self.p
        for k in range(1, p.chain):
            self.got(k - 1, self.own(p.zpeer(p.chain - k)))
        self.go(3, self.region(p.s), p.dev(p.xs))
        self.go(4, self.region(p.s), p.dev(p.ys))
        self.go(7, self.region(p.s), p.dev(p.sib))

    def sides_done(self):
        p = self.p
        first, second = pl.ds(0, self.half), pl.ds(self.half, self.half)
        self.got(3, self.region(p.xs))
        self.go(5, self.region(p.xs, first), p.dev(p.ys))
        self.go(8, self.region(p.xs), p.dev(p.sib))
        self.got(4, self.region(p.ys))
        self.go(6, self.region(p.ys, second), p.dev(p.xs))
        self.go(9, self.region(p.ys), p.dev(p.sib))

    def corner_done(self):
        p = self.p
        first, second = pl.ds(0, self.half), pl.ds(self.half, self.half)
        self.got(5, self.region(p.ds, first))
        self.got(6, self.region(p.ds, second))
        self.go(10, self.region(p.ds), p.dev(p.sib))

    def done(self):
        p = self.p
        for k, s in ((7, p.s), (8, p.xs), (9, p.ys), (10, p.ds)):
            self.got(k, self.region(p.flip(s, 1)))

    def drain(self):
        for copy in self.sent:
            copy.wait_send()


GATHER_SEMS = 11


def by_rows(count, step, body):
    def trip(i, carry):
        body(pl.multiple_of(i * step, step))
        return carry

    lax.fori_loop(0, count // step, trip, 0)


class Scatter:
    def __init__(self, place, rows, flip, bufs, send, recv):
        self.p, self.rows, self.turned = place, rows, flip
        self.full, self.in2, self.stage, self.land, self.mine, self.zout, self.zin = bufs
        self.gr, self.cols = self.full.shape[2], self.full.shape[3]
        self.half = self.cols // 2
        self.step = 16
        self.send, self.recv = send, recv
        self.sent = []

    def go(self, k, src, dst, peer):
        copy = remote(src, dst, self.send.at[k], self.recv.at[k], peer)
        copy.start()
        self.sent.append(copy)

    def got(self, k, ref):
        remote(ref, ref, self.send.at[k], self.recv.at[k], self.p.dev(self.p.sib)).wait_recv()

    def near(self, bits):
        g = self.p.group
        for bit in (1, 2):
            if bits & bit:
                g = Place.flip(g, bit)
        return g

    def cut(self, ref, slot, which):
        return ref.at[slot, :, pl.ds(which * self.half, self.half)]

    def both(self, g, rows, cols):
        mine = self.full[g, self.p.core, rows, cols].astype(jnp.float32)
        return mine + self.in2[g, rows, cols].astype(jnp.float32)

    def start(self):
        self.go(0, self.full.at[:, 1 - self.p.core], self.in2, self.p.dev(self.p.sib))

    def core_done(self):
        p, step = self.p, self.step
        self.got(0, self.in2)
        far, xg, yg = self.near(3), self.near(1), self.near(2)
        whole = pl.ds(0, self.cols)
        first, second = pl.ds(0, self.half), pl.ds(self.half, self.half)

        def sum_far(i):
            rows = pl.ds(i, step)
            self.stage[0, rows] = self.both(far, rows, whole).astype(jnp.bfloat16)

        by_rows(self.gr, step, sum_far)
        self.go(1, self.cut(self.stage, 0, 0), self.cut(self.land, 0, 0), p.dev(p.xs))
        self.go(2, self.cut(self.stage, 0, 1), self.cut(self.land, 0, 1), p.dev(p.ys))

        def sum_sides(i):
            rows = pl.ds(i, step)
            self.stage[1, rows, first] = self.both(xg, rows, first).astype(jnp.bfloat16)
            self.stage[2, rows, second] = self.both(yg, rows, second).astype(jnp.bfloat16)

        by_rows(self.gr, step, sum_sides)
        self.go(3, self.cut(self.stage, 1, 0), self.cut(self.land, 1, 0), p.dev(p.xs))
        self.go(4, self.cut(self.stage, 2, 1), self.cut(self.land, 2, 1), p.dev(p.ys))

    def sides_done(self):
        p, step = self.p, self.step
        for k, slot, which, bits, peer in ((5, 2, 0, 2, p.ys), (6, 1, 1, 1, p.xs)):
            self.got(k - 4, self.cut(self.land, 0, which))
            cols = pl.ds(which * self.half, self.half)
            g = self.near(bits)

            def add(i, slot=slot, cols=cols, g=g):
                rows = pl.ds(i, step)
                total = self.both(g, rows, cols) + self.land[0, rows, cols].astype(jnp.float32)
                self.stage[slot, rows, cols] = total.astype(jnp.bfloat16)

            by_rows(self.gr, step, add)
            self.go(k, self.cut(self.stage, slot, which), self.cut(self.land, slot, which), p.dev(peer))

    def mine_done(self):
        p, step = self.p, self.step
        me = p.group
        for k, slot, which in ((3, 1, 0), (4, 2, 1), (5, 2, 0), (6, 1, 1)):
            self.got(k, self.cut(self.land, slot, which))

        def total(rows, cols):
            sides = self.land[1, rows, cols].astype(jnp.float32)
            sides = sides + self.land[2, rows, cols].astype(jnp.float32)
            return self.both(me, rows, cols) + sides

        if self.turned:

            def turn(i):
                cols = pl.ds(pl.multiple_of(i, 128), 128)
                value = total(pl.ds(0, self.gr), cols).T
                self.mine[cols] = value
                self.zout[cols] = value.astype(jnp.bfloat16)

            by_rows(self.cols, 128, turn)
        else:

            def add(i):
                rows = pl.ds(i, step)
                value = total(rows, pl.ds(0, self.cols))
                self.mine[rows] = value
                self.zout[rows] = value.astype(jnp.bfloat16)

            by_rows(self.gr, step, add)
        for k in range(1, p.chain):
            z = p.zpeer(k)
            src = self.zout.at[pl.ds(pl.multiple_of(z * self.rows, self.rows), self.rows)]
            dst = self.zin.at[pl.ds((k - 1) * self.rows, self.rows)]
            self.go(6 + k, src, dst, p.dev(p.s, z))

    def done(self, result):
        p, step = self.p, self.step
        for k in range(1, p.chain):
            self.got(6 + k, self.zin.at[pl.ds((k - 1) * self.rows, self.rows)])
        start = p.z * self.rows

        def add(i):
            value = self.mine[pl.ds(pl.multiple_of(start + i, step), step)]
            for k in range(1, p.chain):
                value = value + self.zin[pl.ds((k - 1) * self.rows + i, step)].astype(jnp.float32)
            result(i, value)

        by_rows(self.rows, step, add)

    def drain(self):
        for copy in self.sent:
            copy.wait_send()


SCATTER_SEMS = 10


def scatter_scratch(chain, rows, cols, flip):
    f32, bf16 = jnp.float32, jnp.bfloat16
    gr = chain * rows
    block = (cols, gr) if flip else (gr, cols)
    return [
        pltpu.VMEM((4, 2) + block, bf16),
        pltpu.VMEM((4,) + block, bf16),
        pltpu.VMEM((3,) + block, bf16),
        pltpu.VMEM((3,) + block, bf16),
        pltpu.VMEM((gr, cols), f32),
        pltpu.VMEM((gr, cols), bf16),
        pltpu.VMEM((max(1, chain - 1) * rows, cols), bf16),
    ]


class Exchange:
    def __init__(self, place, land, send, recv):
        self.p, self.land, self.send, self.recv = place, land, send, recv
        self.sent = []

    def go(self, source):
        p = self.p
        for d in range(1, 8):
            peer = lax.rem(p.s + d, 8)
            copy = remote(
                source(peer), self.land.at[p.s], self.send.at[d - 1], self.recv.at[d - 1], p.dev(peer)
            )
            copy.start()
            self.sent.append(copy)

    def wait(self):
        p = self.p
        for d in range(1, 8):
            ref = self.land.at[lax.rem(p.s + 8 - d, 8)]
            remote(ref, ref, self.send.at[d - 1], self.recv.at[d - 1], p.dev(p.sib)).wait_recv()

    def drain(self):
        for copy in self.sent:
            copy.wait_send()


def dot_nn(a, b):
    return lax.dot_general(a, b, (((1,), (0,)), ((), ())), preferred_element_type=jnp.float32)


def dot_nt(a, b):
    return lax.dot_general(a, b, (((1,), (1,)), ((), ())), preferred_element_type=jnp.float32)


def dot_tn(a, b):
    return lax.dot_general(a, b, (((0,), (0,)), ((), ())), preferred_element_type=jnp.float32)


def total_of(values):
    return jnp.sum(jnp.sum(values, 1, keepdims=True), 0, keepdims=True)


def fold_rows(values):
    rows, cols = values.shape
    return jnp.sum(values.reshape(rows // 8, 8, cols), 0)


NEG = -1e30
ORDER = ("norm", "qkv", "out", "up", "down")
SUMS = (("norm", 16, 256), ("q", 16, 512), ("kv", 16, 1024), ("out", 16, 512), ("up", 16, 2048), ("down", 64, 512))
LEFT = math.sqrt(2.0 / math.pi)
CUBE = 0.044715


def layer_kernel(chain, rate, names, *refs):
    r = dict(zip(names, refs))
    f32, bf16 = jnp.float32, jnp.bfloat16
    place = Place(chain)
    x_ref, dy_ref, docs_ref = r["tokens"], r["grad"], r["docs"]
    rows_all, width = x_ref.shape
    span, spans = SPAN, rows_all // SPAN
    pairs = width // 128
    hidden_size = r["w_up"].shape[1]
    devices = 8 * chain
    per = width // devices
    entries = 8 * spans * width
    chunk = 256
    chunks = rows_all // chunk

    gathers = {}
    for m, name in enumerate(("norm", "qkv", "out", "up", "down")):
        shard = r["s_" + name]
        piece = 16 if name == "norm" else shard.shape[0]
        g = Gather(place, r["w_" + name], piece, r["gsend"].at[m], r["grecv"].at[m])
        if name == "norm":
            r["npad"][...] = jnp.zeros_like(r["npad"])
            r["npad"][0:4, 0:per] = shard[...]
            shard = r["npad"]
        g.own(place.z)[...] = shard[...].astype(bf16)
        gathers[name] = g
    scatters = {}
    for m, (name, piece, _) in enumerate(SUMS):
        bufs = [r[f"c_{name}{i}"] for i in range(7)]
        scatters[name] = Scatter(
            place, piece, name == "down", bufs, r["csend"].at[m], r["crecv"].at[m]
        )
    first = Exchange(place, r["summ"], r["esend"].at[0], r["erecv"].at[0])
    second = Exchange(place, r["back"], r["esend"].at[1], r["erecv"].at[1])
    place.barrier()
    for name in ("norm", "qkv"):
        gathers[name].start()

    F, mixed, heads = r["F"], r["mixed"], r["heads"]
    loads = []
    for name in ORDER:
        for kind in ("m_", "a_"):
            sem = r["lsem"].at[len(loads)]
            loads.append(pltpu.make_async_copy(r[kind + name], r["v" + kind + name], sem))
            loads[-1].start()

    def advance_rows(name, rows, cols, total):
        scaled = rate * total
        moment = 0.9 * r["vm_" + name][rows, cols] + scaled
        weight = r["s_" + name][rows, cols] - (scaled + 0.9 * moment)
        average = 0.99 * r["va_" + name][rows, cols] + 0.01 * weight
        for k, value in enumerate((weight, moment, average)):
            r["t_" + name][k, rows, cols] = value

    def update(name, start):
        def rows_done(i, total):
            advance_rows(name, pl.ds(i, 16), slice(start, start + total.shape[1]), total)

        return rows_done

    def update_norm(i, total):
        advance_rows("norm", slice(0, 4), slice(0, per), total[0:4, 0:per])

    def norm_one(i):
        rows = pl.ds(i, 128)
        values = x_ref[rows].astype(f32)
        centre = values - jnp.mean(values, -1, keepdims=True)
        spread = jnp.mean(centre * centre, -1, keepdims=True)
        inv = lax.rsqrt(spread + 1e-05)
        F[rows] = centre * inv
        r["inv1"][rows] = jnp.broadcast_to(inv, (128, 128))

    by_rows(rows_all // 2, 128, norm_one)
    gathers["norm"].chain_done()
    gathers["qkv"].chain_done()
    for name in ("out", "up", "down"):
        gathers[name].start()
    lax.fori_loop(rows_all // 256, rows_all // 128, lambda i, c: (norm_one(i * 128), c)[1], 0)

    ids = r["doc_ids"]
    docs = jnp.concatenate([ids[0:1, p * span : p * span + span] for p in range(spans)], 0).astype(f32)
    docs_ref[...] = docs
    wide = jnp.concatenate([docs] * (128 // spans), 0).T
    for p in range(spans):
        r["dcol"][pl.ds(p * span, span)] = jnp.broadcast_to(wide[:, p : p + 1], (span, 128))

    gathers["norm"].sides_done()
    gathers["qkv"].sides_done()
    gathers["out"].chain_done()

    def turn_grad(i):
        rows = pl.ds(pl.multiple_of(i, 128), 128)
        r["dyT"][:, rows] = dy_ref[rows].T

    by_rows(rows_all, 128, turn_grad)
    gathers["norm"].corner_done()
    gathers["qkv"].corner_done()
    gathers["norm"].done()

    place_row = lax.broadcasted_iota(jnp.int32, (256, width), 0)
    place_col = lax.broadcasted_iota(jnp.int32, (256, width), 1)
    pick = (lax.rem(place_col, per) == place_row).astype(f32).astype(bf16)
    owner_row = lax.div(lax.broadcasted_iota(jnp.int32, (16 * devices, width), 0), 16)
    owner_col = lax.div(lax.broadcasted_iota(jnp.int32, (16 * devices, width), 1), per)
    spread_rows = dot_nn(r["w_norm"][...], pick)
    spread_rows = jnp.where(owner_row == owner_col, spread_rows, 0.0)
    norm_rows = jnp.sum(spread_rows.reshape(devices, 16, width), 0)
    r["nrows"][...] = norm_rows

    gathers["up"].chain_done()
    gathers["qkv"].done()

    def project(i):
        rows = pl.ds(pl.multiple_of(i, chunk), chunk)
        act = (F[rows] * r["nrows"][0:1] + r["nrows"][1:2]).astype(bf16)
        r["act1T"][:, rows] = act.T
        result = dot_nn(act, r["w_qkv"][...])
        mixed[rows, 0:width] = (result[:, :width] * 0.125).astype(bf16)
        mixed[rows, width : 3 * width] = result[:, width:].astype(bf16)

    by_rows(rows_all, chunk, project)
    gathers["down"].chain_done()

    last_doc = docs[:, span - 1 : span]
    member = (docs == last_doc).astype(f32)
    count = jnp.sum(member, 1, keepdims=True)
    which = lax.broadcasted_iota(jnp.int32, (spans, span), 0)
    blocks = [jnp.where(which == p, member, 0.0) for p in range(spans)]
    left = jnp.concatenate(blocks, 1)
    left = jnp.concatenate([left, jnp.zeros_like(left)], 0).astype(bf16)
    means = dot_nn(left, mixed[:, width : 3 * width])[:spans] / count
    summ = r["summ"]
    summ[place.s, :, 0 : 2 * width] = means
    summ[place.s, :, 2 * width : 2 * width + 128] = jnp.broadcast_to(last_doc, (spans, 128))
    first.go(lambda peer: summ.at[place.s])
    gathers["out"].sides_done()
    first.wait()

    sums = summ[...].reshape(8 * spans, 2 * width + 128)
    keys = sums[:, :width]
    stat_mean = total_of(keys) / entries
    centred = keys - stat_mean
    stat_var = total_of(centred * centred) / entries
    inv_sum = lax.rsqrt(stat_var + 1e-05)
    key_norm = centred * inv_sum
    r["knorm"][...] = key_norm
    lane = lax.broadcasted_iota(jnp.int32, (span, 128), 1)
    low_half = lane < 64
    lane_row = lax.broadcasted_iota(jnp.int32, (1, 128), 1)
    pick0 = (lane_row < 64).astype(f32).astype(bf16)
    pick1 = (lane_row >= 64).astype(f32).astype(bf16)
    for j in range(pairs):
        cols = slice(128 * j, 128 * j + 128)
        part = key_norm[:, cols].astype(bf16)
        r["KR"][j] = jnp.concatenate([part * pick0, part * pick1], 0)
        part = sums[:, width + 128 * j : width + 128 * j + 128].astype(bf16)
        r["VR"][j] = jnp.concatenate([part * pick0, part * pick1], 0)
    last = sums[:, 2 * width :]
    r["lastrow"][...] = jnp.concatenate([last, last], 0).T[0:8]

    probs = r["probs"]
    causal = lax.broadcasted_iota(jnp.int32, (span, 128), 0) >= lax.broadcasted_iota(
        jnp.int32, (span, 128), 1
    )
    span_first = place.s * spans
    quarter = spans // 4

    def attend(p, carry):
        rows = pl.ds(pl.multiple_of(p * span, span), span)
        column = r["dcol"][rows]
        mask_local = (column == docs_ref[pl.ds(p, 1)]) & causal
        mask_remote = (column == r["lastrow"][0:1]) & (lax.rem(lane, 64) < span_first + p)
        scores, lows = [], []
        for j in range(pairs):
            query = mixed[rows, 128 * j : 128 * j + 128]
            key = mixed[rows, width + 128 * j : width + 128 * j + 128]
            scores.append(dot_nt(query, jnp.concatenate([key * pick0, key * pick1, r["KR"][j]], 0)))
        for j in range(pairs):
            one = jnp.where(mask_local, scores[j][:, :128], NEG)
            two = jnp.where(mask_local, scores[j][:, 128:256], NEG)
            far = jnp.where(mask_remote, scores[j][:, 256:], NEG)
            peak1 = jnp.max(jnp.maximum(one, jnp.where(low_half, far, NEG)), -1, keepdims=True)
            peak2 = jnp.max(jnp.maximum(two, jnp.where(low_half, NEG, far)), -1, keepdims=True)
            one = jnp.exp(one - peak1)
            two = jnp.exp(two - peak2)
            far = jnp.exp(far - jnp.where(low_half, peak1, peak2))
            scale1 = 1.0 / jnp.sum(one + jnp.where(low_half, far, 0.0), -1, keepdims=True)
            scale2 = 1.0 / jnp.sum(two + jnp.where(low_half, 0.0, far), -1, keepdims=True)
            one = one * scale1
            two = two * scale2
            far = far * jnp.where(low_half, scale1, scale2)
            base = 384 * j
            probs[rows, base : base + 128] = one
            probs[rows, base + 128 : base + 256] = two
            probs[rows, base + 256 : base + 384] = far
            lows.append(jnp.concatenate([one, two, far], 1).astype(bf16))
        for j in range(pairs):
            value = mixed[rows, 2 * width + 128 * j : 2 * width + 128 * j + 128]
            values = jnp.concatenate([value * pick0, value * pick1, r["VR"][j]], 0)
            heads[rows, 128 * j : 128 * j + 128] = dot_nn(lows[j], values).astype(bf16)
        return carry

    lax.fori_loop(0, quarter, attend, 0)
    gathers["up"].sides_done()
    gathers["out"].corner_done()
    lax.fori_loop(quarter, 2 * quarter, attend, 0)
    gathers["down"].sides_done()
    lax.fori_loop(2 * quarter, 3 * quarter, attend, 0)
    gathers["up"].corner_done()
    lax.fori_loop(3 * quarter, spans, attend, 0)
    gathers["down"].corner_done()
    for name in ("out", "up", "down"):
        gathers[name].done()

    r["ngrad"][...] = jnp.zeros_like(r["ngrad"])
    tile = 256

    def feed(i):
        rows = pl.ds(pl.multiple_of(i, chunk), chunk)
        part = heads[rows]
        r["headsT"][:, rows] = part.T
        after = x_ref[rows].astype(f32) + dot_nn(part, r["w_out"][...])
        centre = after - jnp.mean(after, -1, keepdims=True)
        spread = jnp.mean(centre * centre, -1, keepdims=True)
        inv = lax.rsqrt(spread + 1e-05)
        normal = centre * inv
        F[rows] = after
        r["dvalue"][rows] = normal
        r["inv2"][rows] = jnp.broadcast_to(inv, (chunk, 128))
        act_two = (normal * r["nrows"][2:3] + r["nrows"][3:4]).astype(bf16)
        r["act2"][...] = act_two
        r["act2T"][:, rows] = act_two.T

        def mlp(c, carry):
            for half in range(2):
                cols = pl.ds(pl.multiple_of(c * 2 * tile + half * tile, tile), tile)
                h = dot_nn(r["act2"][...], r["w_up"][:, cols])
                d = dot_nt(dy_ref[rows], r["w_down"][cols])
                square = h * h
                gate = 0.5 + 0.5 * jnp.tanh(h * (LEFT + (LEFT * CUBE) * square))
                act = h * gate
                r["act3"][rows, cols] = act.astype(bf16)
                slope = gate + act * (2.0 * LEFT + (6.0 * LEFT * CUBE) * square) * (1.0 - gate)
                r["dhid"][rows, cols] = (d * slope).astype(bf16)
            return carry

        lax.fori_loop(0, hidden_size // (2 * tile), mlp, 0)

    by_rows(rows_all, chunk, feed)

    down, up, out = scatters["down"], scatters["up"], scatters["out"]
    gw = down.cols

    def down_part(g, carry):
        cols = pl.ds(pl.multiple_of(g * 2 * gw, 2 * gw), 2 * gw)
        grad = dot_nn(r["dyT"][...], r["act3"][:, cols]).astype(bf16)
        down.full[g, 0] = grad[:, :gw]
        down.full[g, 1] = grad[:, gw:]
        return carry

    lax.fori_loop(0, 4, down_part, 0)
    down.start()

    def put(target, grad, cols):
        gr = target.gr
        for g in range(4):
            for c in range(2):
                k = (2 * g + c) * gr
                target.full[g, c, :, cols] = grad[k : k + gr]

    def up_part(c, carry):
        cols = pl.ds(pl.multiple_of(c * 512, 512), 512)
        put(up, dot_nn(r["act2T"][...], r["dhid"][:, cols]).astype(bf16), cols)
        return carry

    lax.fori_loop(0, hidden_size // 512, up_part, 0)
    up.start()

    def feed_back(i):
        rows = pl.ds(pl.multiple_of(i, chunk), chunk)
        result = F[rows] + dot_nn(r["act3"][rows], r["w_down"][...])
        r["block_out"][rows] = result.astype(bf16)
        d_two = dot_nt(r["dhid"][rows], r["w_up"][...])
        normal = r["dvalue"][rows]
        r["ngrad"][2] += fold_rows(d_two * normal)
        r["ngrad"][3] += fold_rows(d_two)
        scaled = d_two * r["nrows"][2:3]
        centred = (
            scaled
            - jnp.mean(scaled, -1, keepdims=True)
            - normal * jnp.mean(scaled * normal, -1, keepdims=True)
        )
        d_after = dy_ref[rows].astype(f32) + r["inv2"][rows][:, 0:1] * centred
        F[rows] = d_after
        low = d_after.astype(bf16)
        r["dafter"][rows] = low
        heads[rows] = dot_nt(low, r["w_out"][...]).astype(bf16)

    lax.fori_loop(0, chunks // 2, lambda i, c: (feed_back(i * chunk), c)[1], 0)
    down.core_done()
    lax.fori_loop(chunks // 2, chunks, lambda i, c: (feed_back(i * chunk), c)[1], 0)
    up.core_done()
    put(out, dot_nn(r["headsT"][...], r["dafter"][...]).astype(bf16), pl.ds(0, width))
    out.start()

    r["dKR"][...] = jnp.zeros_like(r["dKR"])
    r["dVR"][...] = jnp.zeros_like(r["dVR"])
    dkey, dvalue = r["input_grad"], r["dvalue"]

    def attend_back(p, carry):
        rows = pl.ds(pl.multiple_of(p * span, span), span)
        wide_probs, d_scores, lows, stacks = [], [], [], []
        for j in range(pairs):
            key = mixed[rows, width + 128 * j : width + 128 * j + 128]
            value = mixed[rows, 2 * width + 128 * j : 2 * width + 128 * j + 128]
            stacks.append(jnp.concatenate([key * pick0, key * pick1, r["KR"][j]], 0))
            values_all = jnp.concatenate([value * pick0, value * pick1, r["VR"][j]], 0)
            wide_probs.append(dot_nt(heads[rows, 128 * j : 128 * j + 128], values_all))
        for j in range(pairs):
            d_probs = wide_probs[j]
            base = 384 * j
            one = probs[rows, base : base + 128]
            two = probs[rows, base + 128 : base + 256]
            far = probs[rows, base + 256 : base + 384]
            d_far = far * d_probs[:, 256:]
            sum1 = jnp.sum(one * d_probs[:, :128] + jnp.where(low_half, d_far, 0.0), -1, keepdims=True)
            sum2 = jnp.sum(two * d_probs[:, 128:256] + jnp.where(low_half, 0.0, d_far), -1, keepdims=True)
            d_one = one * (d_probs[:, :128] - sum1)
            d_two = two * (d_probs[:, 128:256] - sum2)
            d_far = far * (d_probs[:, 256:] - jnp.where(low_half, sum1, sum2))
            d_scores.append(jnp.concatenate([d_one, d_two, d_far], 1).astype(bf16))
            lows.append(jnp.concatenate([one, two, far], 1).astype(bf16))
        for j in range(pairs):
            at = slice(128 * j, 128 * j + 128)
            d_keys = dot_tn(d_scores[j], mixed[rows, at])
            d_values = dot_tn(lows[j], heads[rows, at])
            dkey[rows, at] = jnp.where(low_half, d_keys[:128], d_keys[128:256])
            dvalue[rows, at] = jnp.where(low_half, d_values[:128], d_values[128:256])
            r["dKR"][j] += d_keys[256:]
            r["dVR"][j] += d_values[256:]
        for j in range(pairs):
            at = slice(128 * j, 128 * j + 128)
            mixed[rows, at] = (0.125 * dot_nn(d_scores[j], stacks[j])).astype(bf16)
        return carry

    lax.fori_loop(0, quarter, attend_back, 0)
    down.sides_done()
    out.core_done()
    lax.fori_loop(quarter, 2 * quarter, attend_back, 0)
    up.sides_done()
    lax.fori_loop(2 * quarter, 3 * quarter, attend_back, 0)
    out.sides_done()
    down.mine_done()
    lax.fori_loop(3 * quarter, spans, attend_back, 0)

    half_spans = 8 * spans
    parts = []
    for name in ("dKR", "dVR"):
        for j in range(pairs):
            both = r[name][j]
            low = low_half[:half_spans]
            parts.append(jnp.where(low, both[:half_spans], both[half_spans:]))
    d_keys = jnp.concatenate(parts[:pairs], 1)
    d_values = jnp.concatenate(parts[pairs:], 1)
    key_norm = r["knorm"][...]
    flat = jnp.where(lane_row < 64, total_of(d_keys), total_of(d_keys * key_norm))
    send = r["sendback"]
    send[:, :, 0:width] = d_keys.reshape(8, spans, width)
    send[:, :, width : 2 * width] = d_values.reshape(8, spans, width)
    send[:, :, 2 * width :] = jnp.broadcast_to(flat.reshape(1, 1, 128), (8, spans, 128))
    back = r["back"]
    back[place.s] = send[place.s]
    second.go(lambda peer: send.at[peer])

    first_part, rest = scatters["q"], scatters["kv"]
    put(first_part, dot_nn(r["act1T"][...], mixed[:, :width]).astype(bf16), pl.ds(0, width))
    first_part.start()
    up.mine_done()
    out.mine_done()
    second.wait()

    owned = jnp.sum(back[...], 0)
    back_sum = owned[0:1, 2 * width : 2 * width + 1]
    back_cross = owned[0:1, 2 * width + 64 : 2 * width + 65]
    mine_norm = r["knorm"][pl.ds(pl.multiple_of(place.s * spans, spans), spans)]
    d_sum_key = inv_sum * (
        owned[:, :width] - back_sum * (1.0 / entries) - mine_norm * (back_cross * (1.0 / entries))
    )
    r["dsum"][:, 0:width] = d_sum_key / count
    r["dsum"][:, width : 2 * width] = owned[:, width : 2 * width] / count
    slot = lax.broadcasted_iota(jnp.int32, (8, 128), 1)
    stats = jnp.where(slot == 0, stat_mean, stat_var)
    stats = jnp.where(slot == 2, -inv_sum * back_sum, stats)
    stats = jnp.where(slot == 3, -0.5 * inv_sum * inv_sum * back_cross, stats)
    r["stats"][...] = stats

    def join(p, carry):
        rows = pl.ds(pl.multiple_of(p * span, span), span)
        final = docs_ref[pl.ds(p, 1)][:, span - 1 : span]
        share = (r["dcol"][rows] == final).astype(f32)
        sums_row = r["dsum"][pl.ds(p, 1)]
        for j in range(pairs):
            at = slice(128 * j, 128 * j + 128)
            past = slice(width + 128 * j, width + 128 * j + 128)
            full = dkey[rows, at] + share * sums_row[:, at]
            mixed[rows, past] = full.astype(bf16)
            full = dvalue[rows, at] + share * sums_row[:, past]
            mixed[rows, 2 * width + 128 * j : 2 * width + 128 * j + 128] = full.astype(bf16)
        return carry

    lax.fori_loop(0, spans, join, 0)

    first_part.core_done()

    def rest_part(c, carry):
        cols = pl.ds(pl.multiple_of(c * width, width), width)
        past = pl.ds(pl.multiple_of(c * width + width, width), width)
        put(rest, dot_nn(r["act1T"][...], mixed[:, past]).astype(bf16), cols)
        return carry

    lax.fori_loop(0, 2, rest_part, 0)
    rest.start()

    def first_back(i):
        rows = pl.ds(pl.multiple_of(i, chunk), chunk)
        d_one = dot_nt(mixed[rows], r["w_qkv"][...])
        values = x_ref[rows].astype(f32)
        inv = r["inv1"][rows][:, 0:1]
        normal = (values - jnp.mean(values, -1, keepdims=True)) * inv
        r["ngrad"][0] += fold_rows(d_one * normal)
        r["ngrad"][1] += fold_rows(d_one)
        scaled = d_one * r["nrows"][0:1]
        centred = (
            scaled
            - jnp.mean(scaled, -1, keepdims=True)
            - normal * jnp.mean(scaled * normal, -1, keepdims=True)
        )
        r["input_grad"][rows] = F[rows] + inv * centred

    half_chunks = chunks // 2
    lax.fori_loop(0, half_chunks, lambda i, c: (first_back(i * chunk), c)[1], 0)
    first_part.sides_done()
    rest.core_done()
    lax.fori_loop(half_chunks, chunks, lambda i, c: (first_back(i * chunk), c)[1], 0)

    pieces = jnp.concatenate(
        [jnp.sum(r["ngrad"][k], 0, keepdims=True) for k in range(4)]
        + [jnp.zeros((12, width), f32)],
        0,
    )
    spread_rows = jnp.broadcast_to(pieces[None], (devices, 16, width)).reshape(16 * devices, width)
    spread_rows = jnp.where(owner_row == owner_col, spread_rows, 0.0).astype(bf16)
    norm = scatters["norm"]
    put(norm, dot_nt(spread_rows, pick).astype(bf16), pl.ds(0, 256))
    norm.start()
    first_part.mine_done()
    rest.sides_done()
    norm.core_done()
    norm.sides_done()
    rest.mine_done()
    norm.mine_done()
    for copy in loads:
        copy.wait()
    for name in ("down", "up", "out"):
        scatters[name].done(update(name, 0))
    first_part.done(update("qkv", 0))
    rest.done(update("qkv", width))
    norm.done(update_norm)
    for part in list(gathers.values()) + list(scatters.values()) + [first, second]:
        part.drain()


def fused_layer(chain, rate, tokens, grad, doc_ids, shards, moments, averages):
    f32, bf16 = jnp.float32, jnp.bfloat16
    rows, width = tokens.shape
    spans = rows // SPAN
    order = ORDER
    devices = 8 * chain
    ins = [("tokens", tokens), ("grad", grad), ("doc_ids", doc_ids)]
    ins += [("s_" + name, shards[name]) for name in order]
    ins += [("m_" + name, moments[name]) for name in order]
    ins += [("a_" + name, averages[name]) for name in order]
    outs = [
        ("block_out", pltpu.VMEM((rows, width), bf16)),
        ("input_grad", pltpu.VMEM((rows, width), f32)),
        ("stats", pltpu.VMEM((8, 128), f32)),
    ]
    outs += [("t_" + name, pltpu.VMEM((3,) + shards[name].shape, f32)) for name in order]
    hidden = shards["up"].shape[1]
    scratch = {}
    for name in order:
        piece, cols = (16, 256) if name == "norm" else shards[name].shape
        scratch["w_" + name] = pltpu.VMEM((devices * piece, cols), bf16)
    for name, piece, cols in SUMS:
        for i, buf in enumerate(scatter_scratch(chain, piece, cols, name == "down")):
            scratch[f"c_{name}{i}"] = buf
    for name in order:
        scratch["vm_" + name] = pltpu.VMEM(shards[name].shape, f32)
        scratch["va_" + name] = pltpu.VMEM(shards[name].shape, f32)
    scratch["lsem"] = DMA((10,))
    payload = (8, spans, 2 * width + 128)
    pairs = width // 128
    scratch |= {
        "gsend": DMA((5, GATHER_SEMS)),
        "grecv": DMA((5, GATHER_SEMS)),
        "csend": DMA((6, SCATTER_SEMS)),
        "crecv": DMA((6, SCATTER_SEMS)),
        "esend": DMA((2, 7)),
        "erecv": DMA((2, 7)),
        "summ": pltpu.VMEM(payload, f32),
        "back": pltpu.VMEM(payload, f32),
        "sendback": pltpu.VMEM(payload, f32),
        "F": pltpu.VMEM((rows, width), f32),
        "inv1": pltpu.VMEM((rows, 128), f32),
        "dcol": pltpu.VMEM((rows, 128), f32),
        "nrows": pltpu.VMEM((16, width), f32),
        "ngrad": pltpu.VMEM((4, 8, width), f32),
        "act1T": pltpu.VMEM((width, rows), bf16),
        "dyT": pltpu.VMEM((width, rows), bf16),
        "act2T": pltpu.VMEM((width, rows), bf16),
        "headsT": pltpu.VMEM((width, rows), bf16),
        "mixed": pltpu.VMEM((rows, 3 * width), bf16),
        "probs": pltpu.VMEM((rows, 384 * pairs), f32),
        "heads": pltpu.VMEM((rows, width), bf16),
        "knorm": pltpu.VMEM((8 * spans, width), f32),
        "KR": pltpu.VMEM((pairs, 128, 128), bf16),
        "VR": pltpu.VMEM((pairs, 128, 128), bf16),
        "dKR": pltpu.VMEM((pairs, 128, 128), f32),
        "dVR": pltpu.VMEM((pairs, 128, 128), f32),
        "lastrow": pltpu.VMEM((8, 128), f32),
        "docs": pltpu.VMEM((spans, SPAN), f32),
        "npad": pltpu.VMEM((16, 256), f32),
        "inv2": pltpu.VMEM((rows, 128), f32),
        "act2": pltpu.VMEM((256, width), bf16),
        "act3": pltpu.VMEM((rows, hidden), bf16),
        "dhid": pltpu.VMEM((rows, hidden), bf16),
        "dafter": pltpu.VMEM((rows, width), bf16),
        "dvalue": pltpu.VMEM((rows, width), f32),
        "dsum": pltpu.VMEM((spans, 2 * width), f32),
    }
    names = [n for n, _ in ins] + [n for n, _ in outs] + list(scratch)
    vmem = pl.BlockSpec(memory_space=pltpu.VMEM)
    result = pl.pallas_call(
        functools.partial(layer_kernel, chain, rate, names),
        out_shape=[shape for _, shape in outs],
        in_specs=[vmem] * (len(ins) - 10) + [pl.BlockSpec(memory_space=pltpu.HBM)] * 10,
        out_specs=[vmem] * len(outs),
        scratch_shapes=list(scratch.values()),
        compiler_params=pltpu.CompilerParams(
            collective_id=0, has_side_effects=True, vmem_limit_bytes=59 * 2**20
        ),
    )(*[value for _, value in ins])
    return dict(zip([n for n, _ in outs], result))


def finish_kernel(count, *refs):
    ins, outs, sems = refs[:count], refs[count:-1], refs[-1]
    stats, two = ins[-1], outs[count - 1 :]
    copies = [pltpu.make_async_copy(ins[k], outs[k], sems.at[k]) for k in range(count - 1)]
    for copy in copies:
        copy.start()
    two[0][...] = stats[0:1, 0:2]
    two[1][...] = stats[0:1, 2:4]
    for copy in copies:
        copy.wait()


def finish(arrays, stats):
    vmem = pl.BlockSpec(memory_space=pltpu.VMEM)
    two = jax.ShapeDtypeStruct((1, 2), jnp.float32)
    count = len(arrays) + 1
    return pl.pallas_call(
        functools.partial(finish_kernel, count),
        out_shape=[jax.ShapeDtypeStruct(a.shape, a.dtype) for a in arrays] + [two, two],
        in_specs=[pl.BlockSpec(memory_space=pl.ANY)] * (count - 1) + [vmem],
        out_specs=[pl.BlockSpec(memory_space=pltpu.HBM)] * (count - 1) + [vmem] * 2,
        scratch_shapes=[DMA((count - 1,))],
        compiler_params=pltpu.CompilerParams(vmem_limit_bytes=2 * 2**20),
    )(*(pltpu.with_memory_space_constraint(a, pltpu.VMEM) for a in arrays), stats)


def norm_forward(values, gain_row, shift_row):
    centre = values - jnp.mean(values, -1, keepdims=True)
    spread = jnp.mean(centre * centre, -1, keepdims=True)
    inv_std = lax.rsqrt(spread + 1e-05)
    normal = centre * inv_std
    return (normal * gain_row + shift_row, normal, inv_std)


def norm_backward(grad_in, normal, inv_std, gain_row):
    scaled = grad_in * gain_row
    centred = (
        scaled
        - jnp.mean(scaled, -1, keepdims=True)
        - normal * jnp.mean(scaled * normal, -1, keepdims=True)
    )
    return (inv_std * centred, jnp.sum(grad_in * normal, 0), jnp.sum(grad_in, 0))


def gelu_tanh(values):
    return jax.nn.gelu(values, approximate=True)


def span_probs(query_blk, key_blk, key_remote, doc_span, last_remote, span_first):
    span_len = doc_span.shape[2]
    local = (
        jnp.einsum("bpqhe,bpkhe->bphqk", query_blk, key_blk, preferred_element_type=jnp.float32)
        * 0.125
    )
    remote = (
        jnp.einsum("bpqhe,bnhe->bphqn", query_blk, key_remote, preferred_element_type=jnp.float32)
        * 0.125
    )
    positions = jnp.arange(span_len)
    causal = positions[:, None] >= positions[None, :]
    same_doc = doc_span[:, :, :, None] == doc_span[:, :, None, :]
    mask_local = (same_doc & causal[None, None])[:, :, None]
    span_ids = span_first + jnp.arange(doc_span.shape[1])
    earlier = jnp.arange(key_remote.shape[1])[None, :] < span_ids[:, None]
    doc_float = doc_span.astype(jnp.float32)
    match = doc_float[:, :, :, None] == last_remote.astype(jnp.float32)[:, None, None, :]
    mask_remote = (match & earlier[None, :, None, :])[:, :, None]
    allowed = jnp.concatenate([mask_local, mask_remote], -1)
    scores = jnp.where(allowed, jnp.concatenate([local, remote], -1), -1e30)
    peak_score = jnp.max(scores, -1, keepdims=True)
    raised = jnp.exp(scores - peak_score)
    return raised / jnp.sum(raised, -1, keepdims=True)


def advance(weight, moment, average, grad, rate):
    new_moment = 0.9 * moment + rate * grad
    new_weight = weight - (rate * grad + 0.9 * new_moment)
    new_average = 0.99 * average + 0.01 * new_weight
    return jnp.stack([new_weight, new_moment, new_average])


def shards_plain(
    tokens,
    grad_out,
    doc_ids,
    qkv_w,
    qkv_m,
    qkv_a,
    out_w,
    out_m,
    out_a,
    up_w,
    up_m,
    up_a,
    down_w,
    down_m,
    down_a,
    norm_w,
    norm_m,
    norm_a,
):
    seqs, seq_len, width = tokens.shape
    span_len = SPAN
    cycle_size = lax.axis_size("seq")
    cycle_rank = lax.axis_index("seq")
    spans_dev = seq_len // span_len
    spans_all = spans_dev * cycle_size
    rows_dev = seqs * seq_len
    head_size = width // H
    bf16 = jnp.bfloat16
    f32 = jnp.float32
    w_qkv, w_out, w_up, w_down, norm_low = (
        lax.all_gather(qkv_w.astype(bf16), ("seq", "dp"), axis=0, tiled=True),
        lax.all_gather(out_w.astype(bf16), ("seq", "dp"), axis=0, tiled=True),
        lax.all_gather(up_w.astype(bf16), ("seq", "dp"), axis=0, tiled=True),
        lax.all_gather(down_w.astype(bf16), ("seq", "dp"), axis=0, tiled=True),
        lax.all_gather(norm_w.astype(bf16), ("seq", "dp"), axis=1, tiled=True),
    )
    norm_rows = norm_low.astype(f32)
    inputs = tokens.reshape(rows_dev, width).astype(f32)
    normed_one, normal_one, inv_one = norm_forward(inputs, norm_rows[0], norm_rows[1])
    act_one = normed_one.astype(bf16)
    mixed = jnp.dot(act_one, w_qkv, preferred_element_type=f32)
    query = mixed[:, :width].astype(bf16)
    key_all = mixed[:, width : 2 * width].astype(bf16)
    value_all = mixed[:, 2 * width :].astype(bf16)
    block_shape = (seqs, spans_dev, span_len, H, head_size)
    query_blk = query.reshape(block_shape)
    key_blk = key_all.reshape(block_shape)
    value_blk = value_all.reshape(block_shape)
    doc_span = doc_ids.reshape(seqs, spans_dev, span_len)
    last_doc = doc_span[:, :, -1]
    member = (doc_span == last_doc[:, :, None]).astype(f32)
    counts = jnp.sum(member, -1)
    member_low = member.astype(bf16)
    key_four = key_all.reshape(seqs, spans_dev, span_len, width)
    value_four = value_all.reshape(seqs, spans_dev, span_len, width)
    sum_key = (
        jnp.einsum("bpt,bptd->bpd", member_low, key_four, preferred_element_type=f32)
        / counts[..., None]
    )
    sum_value = (
        jnp.einsum("bpt,bptd->bpd", member_low, value_four, preferred_element_type=f32)
        / counts[..., None]
    )
    total_sum, total_square = lax.psum(
        (jnp.sum(sum_key, (1, 2)), jnp.sum(sum_key * sum_key, (1, 2))), "seq"
    )
    entries = spans_all * width
    stat_mean = total_sum / entries
    stat_var = total_square / entries - stat_mean * stat_mean
    inv_sum = lax.rsqrt(stat_var + 1e-05)
    key_norm = (sum_key - stat_mean[:, None, None]) * inv_sum[:, None, None]
    key_send = key_norm.astype(bf16)
    value_send = sum_value.astype(bf16)
    last_send = last_doc.astype(bf16)
    key_remote, value_remote, last_remote = (
        lax.all_gather(key_send, "seq", axis=1, tiled=True),
        lax.all_gather(value_send, "seq", axis=1, tiled=True),
        lax.all_gather(last_send, "seq", axis=1, tiled=True),
    )
    remote_shape = (seqs, spans_all, H, head_size)
    span_first = cycle_rank * spans_dev
    probs = span_probs(
        query_blk, key_blk, key_remote.reshape(remote_shape), doc_span, last_remote, span_first
    )
    probs_low = probs.astype(bf16)
    attended = jnp.einsum(
        "bphqk,bpkhe->bpqhe", probs_low[..., :span_len], value_blk, preferred_element_type=f32
    )
    attended = attended + jnp.einsum(
        "bphqn,bnhe->bpqhe",
        probs_low[..., span_len:],
        value_remote.reshape(remote_shape),
        preferred_element_type=f32,
    )
    heads_out = attended.reshape(rows_dev, width).astype(bf16)
    after_attn = inputs + jnp.dot(heads_out, w_out, preferred_element_type=f32)
    normed_two, normal_two, inv_two = norm_forward(after_attn, norm_rows[2], norm_rows[3])
    act_two = normed_two.astype(bf16)
    hidden = jnp.dot(act_two, w_up, preferred_element_type=f32)
    act_three = gelu_tanh(hidden).astype(bf16)
    result = after_attn + jnp.dot(act_three, w_down, preferred_element_type=f32)
    block_out = result.astype(bf16).reshape(seqs, seq_len, width)
    stats_out = jnp.stack([stat_mean, stat_var], -1)
    grad_low = grad_out.reshape(rows_dev, width)
    grad_down = jnp.einsum("tf,td->fd", act_three, grad_low, preferred_element_type=f32)
    d_three = jnp.einsum("td,fd->tf", grad_low, w_down, preferred_element_type=f32)
    unused_out, gelu_pull = jax.vjp(gelu_tanh, hidden)
    d_hidden = gelu_pull(d_three)[0].astype(bf16)
    grad_up = jnp.einsum("td,tf->df", act_two, d_hidden, preferred_element_type=f32)
    d_two = jnp.einsum("tf,df->td", d_hidden, w_up, preferred_element_type=f32)
    d_norm_two, gain_two, shift_two = norm_backward(d_two, normal_two, inv_two, norm_rows[2])
    d_after = grad_low.astype(f32) + d_norm_two
    d_after_low = d_after.astype(bf16)
    grad_outw = jnp.einsum("tc,td->cd", heads_out, d_after_low, preferred_element_type=f32)
    d_heads = jnp.einsum("td,cd->tc", d_after_low, w_out, preferred_element_type=f32).astype(bf16)
    key_back, value_back, last_back = (key_remote, value_remote, last_remote)
    key_back_blk = key_back.reshape(remote_shape)
    value_back_blk = value_back.reshape(remote_shape)
    probs_back = span_probs(query_blk, key_blk, key_back_blk, doc_span, last_back, span_first)
    probs_back_low = probs_back.astype(bf16)
    d_heads_blk = d_heads.reshape(block_shape)
    d_probs = jnp.concatenate(
        [
            jnp.einsum("bpqhe,bpkhe->bphqk", d_heads_blk, value_blk, preferred_element_type=f32),
            jnp.einsum(
                "bpqhe,bnhe->bphqn", d_heads_blk, value_back_blk, preferred_element_type=f32
            ),
        ],
        -1,
    )
    row_dot = jnp.sum(probs_back * d_probs, -1, keepdims=True)
    d_scores = (probs_back * (d_probs - row_dot)).astype(bf16)
    d_local = d_scores[..., :span_len]
    d_remote = d_scores[..., span_len:]
    d_query = 0.125 * (
        jnp.einsum("bphqk,bpkhe->bpqhe", d_local, key_blk, preferred_element_type=f32)
        + jnp.einsum("bphqn,bnhe->bpqhe", d_remote, key_back_blk, preferred_element_type=f32)
    )
    d_key = 0.125 * jnp.einsum("bphqk,bpqhe->bpkhe", d_local, query_blk, preferred_element_type=f32)
    d_value = jnp.einsum(
        "bphqk,bpqhe->bpkhe",
        probs_back_low[..., :span_len],
        d_heads_blk,
        preferred_element_type=f32,
    )
    d_key_sum = (
        0.125 * jnp.einsum("bphqn,bpqhe->bnhe", d_remote, query_blk, preferred_element_type=f32)
    ).reshape(seqs, spans_all, width)
    d_value_sum = jnp.einsum(
        "bphqn,bpqhe->bnhe", probs_back_low[..., span_len:], d_heads_blk, preferred_element_type=f32
    ).reshape(seqs, spans_all, width)
    owned_key, owned_value = (
        lax.psum_scatter(
            d_key_sum.astype(jnp.bfloat16), "seq", scatter_dimension=1, tiled=True
        ).astype(jnp.float32),
        lax.psum_scatter(
            d_value_sum.astype(jnp.bfloat16), "seq", scatter_dimension=1, tiled=True
        ).astype(jnp.float32),
    )
    back_sum, back_cross = lax.psum(
        (jnp.sum(owned_key, (1, 2)), jnp.sum(owned_key * key_norm, (1, 2))), "seq"
    )
    stat_grads = jnp.stack([-inv_sum * back_sum, -0.5 * inv_sum * inv_sum * back_cross], -1)
    d_sum_key = inv_sum[:, None, None] * (
        owned_key
        - back_sum[:, None, None] / entries
        - key_norm * back_cross[:, None, None] / entries
    )
    share = member / counts[..., None]
    d_key_all = (
        d_key.reshape(seqs, spans_dev, span_len, width)
        + share[..., None] * d_sum_key[:, :, None, :]
    )
    d_value_all = (
        d_value.reshape(seqs, spans_dev, span_len, width)
        + share[..., None] * owned_value[:, :, None, :]
    )
    d_mixed = jnp.concatenate(
        [
            d_query.reshape(rows_dev, width),
            d_key_all.reshape(rows_dev, width),
            d_value_all.reshape(rows_dev, width),
        ],
        -1,
    ).astype(bf16)
    grad_qkv = jnp.einsum("td,tf->df", act_one, d_mixed, preferred_element_type=f32)
    d_one = jnp.einsum("tf,df->td", d_mixed, w_qkv, preferred_element_type=f32)
    d_norm_one, gain_one, shift_one = norm_backward(d_one, normal_one, inv_one, norm_rows[0])
    input_grad = (d_after + d_norm_one).reshape(seqs, seq_len, width)
    grad_norm = jnp.stack([gain_one, shift_one, gain_two, shift_two])
    sum_qkv, sum_outw, sum_up, sum_down, sum_norm = (
        lax.psum_scatter(grad_qkv, ("seq", "dp"), scatter_dimension=0, tiled=True),
        lax.psum_scatter(grad_outw, ("seq", "dp"), scatter_dimension=0, tiled=True),
        lax.psum_scatter(grad_up, ("seq", "dp"), scatter_dimension=0, tiled=True),
        lax.psum_scatter(grad_down, ("seq", "dp"), scatter_dimension=0, tiled=True),
        lax.psum_scatter(grad_norm, ("seq", "dp"), scatter_dimension=1, tiled=True),
    )
    tokens_all = rows_dev * cycle_size * lax.axis_size("dp")
    rate = 0.02 / math.sqrt(tokens_all)
    return (
        block_out,
        input_grad,
        stats_out,
        stat_grads,
        advance(qkv_w, qkv_m, qkv_a, sum_qkv, rate),
        advance(out_w, out_m, out_a, sum_outw, rate),
        advance(up_w, up_m, up_a, sum_up, rate),
        advance(down_w, down_m, down_a, sum_down, rate),
        advance(norm_w, norm_m, norm_a, sum_norm, rate),
    )


def shards(*args):
    tokens, grad_out, doc_ids = args[:3]
    qkv_w = args[3]
    seqs, seq_len, width = tokens.shape
    fits = lax.axis_size("seq") == 8 and qkv_w.shape[0] % 16 == 0
    fits = fits and seqs == 1 and seq_len == 8 * SPAN and width == 512
    if not fits:
        return shards_plain(*args)
    chain = lax.axis_size("dp")
    names = {"qkv": 3, "out": 6, "up": 9, "down": 12, "norm": 15}
    done = fused_layer(
        chain,
        0.02 / math.sqrt(seq_len * 8 * chain),
        tokens.reshape(seq_len, width),
        grad_out.reshape(seq_len, width),
        doc_ids,
        *({name: args[k + j] for name, k in names.items()} for j in range(3)),
    )
    order = ["block_out", "input_grad"] + ["t_" + name for name in names]
    result = finish([done[name] for name in order], done["stats"])
    return (
        result[0].reshape(tokens.shape),
        result[1].reshape(tokens.shape),
        *result[7:],
        *result[2:7],
    )


def solution(mesh):
    placed = (
        P("dp", "seq", None),
        P("dp", "seq", None),
        P("dp", "seq"),
        P(("seq", "dp"), None),
        P(("seq", "dp"), None),
        P(("seq", "dp"), None),
        P(("seq", "dp"), None),
        P(("seq", "dp"), None),
        P(("seq", "dp"), None),
        P(("seq", "dp"), None),
        P(("seq", "dp"), None),
        P(("seq", "dp"), None),
        P(("seq", "dp"), None),
        P(("seq", "dp"), None),
        P(("seq", "dp"), None),
        P(None, ("seq", "dp")),
        P(None, ("seq", "dp")),
        P(None, ("seq", "dp")),
    )
    return jax.shard_map(
        shards,
        mesh=mesh,
        in_specs=placed,
        out_specs=(
            P("dp", "seq", None),
            P("dp", "seq", None),
            P("dp", None),
            P("dp", None),
            P(None, ("seq", "dp"), None),
            P(None, ("seq", "dp"), None),
            P(None, ("seq", "dp"), None),
            P(None, ("seq", "dp"), None),
            P(None, None, ("seq", "dp")),
        ),
        check_vma=False,
    )
```

```python
import functools
import math

import jax
import jax.numpy as jnp
from jax import lax
from jax.experimental import pallas as pl
from jax.experimental.pallas import tpu as pltpu
from jax.sharding import PartitionSpec as P

H = 8
SPAN = 128
MESH = pl.DeviceIdType.MESH
DMA = pltpu.SemaphoreType.DMA


class Place:
    def __init__(self, chain):
        self.chain = chain
        self.s = lax.axis_index("seq")
        self.z = lax.axis_index("dp")
        self.core = lax.rem(self.s, 2)
        self.group = lax.div(self.s, 2)
        self.sib = self.flip(self.s, 1)
        self.xs = self.flip(self.s, 2)
        self.ys = self.flip(self.s, 4)
        self.ds = self.flip(self.xs, 4)

    @staticmethod
    def flip(value, bit):
        return value + bit - 2 * bit * lax.rem(lax.div(value, bit), 2)

    def dev(self, s, z=None):
        return {"seq": s, "dp": self.z if z is None else z}

    def zflip(self, bits):
        z = self.z
        for bit in (1, 2):
            if bits & bit:
                z = self.flip(z, bit)
        return z

    def zpeer(self, step):
        return lax.rem(self.z + step, self.chain)

    def barrier(self, extra=()):
        sem = pltpu.get_barrier_semaphore()
        peers = [self.dev(self.sib), self.dev(self.xs), self.dev(self.ys)]
        peers += [self.dev(self.s, self.zpeer(k)) for k in range(1, self.chain)]
        peers += list(extra)
        for peer in peers:
            pl.semaphore_signal(sem, inc=1, device_id=peer, device_id_type=MESH)
        pl.semaphore_wait(sem, len(peers))


def remote(src, dst, send, recv, peer):
    return pltpu.make_async_remote_copy(
        src_ref=src, dst_ref=dst, send_sem=send, recv_sem=recv, device_id=peer, device_id_type=MESH
    )


class Gather:
    def __init__(self, place, full, rows, send, recv):
        self.p, self.full, self.rows = place, full, rows
        self.send, self.recv = send, recv
        self.gr = place.chain * rows
        self.sent = []

    def region(self, s):
        return self.full.at[pl.ds(pl.multiple_of(s * self.gr, self.gr), self.gr)]

    def piece(self, s, z):
        start = pl.multiple_of(s * self.gr + z * self.rows, self.rows)
        return self.full.at[pl.ds(start, self.rows)]

    def go(self, k, ref, peer):
        copy = remote(ref, ref, self.send.at[k], self.recv.at[k], peer)
        copy.start()
        self.sent.append(copy)

    def got(self, k, ref):
        remote(ref, ref, self.send.at[k], self.recv.at[k], self.p.dev(self.p.sib)).wait_recv()

    def sides(self, k):
        p = self.p
        piece = self.piece(p.s, p.zflip(k))
        self.go(3 + k, piece, p.dev(p.xs))
        self.go(7 + k, piece, p.dev(p.ys))

    def start(self):
        p = self.p
        for k in range(1, p.chain):
            self.go(k - 1, self.piece(p.s, p.z), p.dev(p.s, p.zflip(k)))

    def chain_done(self):
        p = self.p
        for k in range(1, p.chain):
            self.got(k - 1, self.piece(p.s, p.zflip(k)))
            self.sides(k)
        self.go(19, self.region(p.s), p.dev(p.sib))

    def sides_done(self):
        p = self.p
        for k in range(p.chain):
            self.got(3 + k, self.piece(p.xs, p.zflip(k)))
            if k < (p.chain + 1) // 2:
                self.go(11 + k, self.piece(p.xs, p.zflip(k)), p.dev(p.ys))
            self.got(7 + k, self.piece(p.ys, p.zflip(k)))
            if k >= (p.chain + 1) // 2:
                self.go(11 + k, self.piece(p.ys, p.zflip(k)), p.dev(p.xs))
        self.go(20, self.region(p.xs), p.dev(p.sib))
        self.go(21, self.region(p.ys), p.dev(p.sib))

    def corner_done(self):
        p = self.p
        for k in range(p.chain):
            self.got(11 + k, self.piece(p.ds, p.zflip(k)))
        self.go(22, self.region(p.ds), p.dev(p.sib))

    def done(self):
        p = self.p
        for k, s in ((19, p.s), (20, p.xs), (21, p.ys), (22, p.ds)):
            self.got(k, self.region(p.flip(s, 1)))

    def drain(self):
        for copy in self.sent:
            copy.wait_send()


GATHER_SEMS = 23


def by_rows(count, step, body):
    def trip(i, carry):
        body(pl.multiple_of(i * step, step))
        return carry

    lax.fori_loop(0, count // step, trip, 0)


class Scatter:
    def __init__(self, place, rows, flip, bufs, send, recv):
        self.p, self.rows, self.turned = place, rows, flip
        self.full, self.in2, self.stage, self.land, self.mine, self.zout, self.zin = bufs
        self.gr, self.cols = self.full.shape[2], self.full.shape[3]
        self.half = self.cols // 2
        self.step = 16
        self.send, self.recv = send, recv
        self.sent = []

    def go(self, k, src, dst, peer):
        copy = remote(src, dst, self.send.at[k], self.recv.at[k], peer)
        copy.start()
        self.sent.append(copy)

    def got(self, k, ref):
        remote(ref, ref, self.send.at[k], self.recv.at[k], self.p.dev(self.p.sib)).wait_recv()

    def near(self, bits):
        g = self.p.group
        for bit in (1, 2):
            if bits & bit:
                g = Place.flip(g, bit)
        return g

    def cut(self, ref, slot, which):
        return ref.at[slot, :, pl.ds(which * self.half, self.half)]

    def both(self, g, rows, cols):
        mine = self.full[g, self.p.core, rows, cols].astype(jnp.float32)
        return mine + self.in2[g, rows, cols].astype(jnp.float32)

    def start(self):
        self.go(0, self.full.at[:, 1 - self.p.core], self.in2, self.p.dev(self.p.sib))

    def start_group(self, g):
        self.go(10 + g, self.full.at[g, 1 - self.p.core], self.in2.at[g], self.p.dev(self.p.sib))

    def core_done(self):
        p, step = self.p, self.step
        if self.turned:
            for g in range(4):
                self.got(10 + g, self.in2.at[g])
        else:
            self.got(0, self.in2)
        far, xg, yg = self.near(3), self.near(1), self.near(2)
        whole = pl.ds(0, self.cols)
        first, second = pl.ds(0, self.half), pl.ds(self.half, self.half)

        def sum_far(i):
            rows = pl.ds(i, step)
            self.stage[0, rows] = self.both(far, rows, whole).astype(jnp.bfloat16)

        by_rows(self.gr, step, sum_far)
        self.go(1, self.cut(self.stage, 0, 0), self.cut(self.land, 0, 0), p.dev(p.xs))
        self.go(2, self.cut(self.stage, 0, 1), self.cut(self.land, 0, 1), p.dev(p.ys))

        def sum_sides(i):
            rows = pl.ds(i, step)
            self.stage[1, rows, first] = self.both(xg, rows, first).astype(jnp.bfloat16)
            self.stage[2, rows, second] = self.both(yg, rows, second).astype(jnp.bfloat16)

        by_rows(self.gr, step, sum_sides)
        self.go(3, self.cut(self.stage, 1, 0), self.cut(self.land, 1, 0), p.dev(p.xs))
        self.go(4, self.cut(self.stage, 2, 1), self.cut(self.land, 2, 1), p.dev(p.ys))

    def sides_done(self):
        p, step = self.p, self.step
        for k, slot, which, bits, peer in ((5, 2, 0, 2, p.ys), (6, 1, 1, 1, p.xs)):
            self.got(k - 4, self.cut(self.land, 0, which))
            cols = pl.ds(which * self.half, self.half)
            g = self.near(bits)

            def add(i, slot=slot, cols=cols, g=g):
                rows = pl.ds(i, step)
                total = self.both(g, rows, cols) + self.land[0, rows, cols].astype(jnp.float32)
                self.stage[slot, rows, cols] = total.astype(jnp.bfloat16)

            by_rows(self.gr, step, add)
            self.go(k, self.cut(self.stage, slot, which), self.cut(self.land, slot, which), p.dev(peer))

    def mine_done(self):
        p, step = self.p, self.step
        me = p.group
        for k, slot, which in ((3, 1, 0), (4, 2, 1), (5, 2, 0), (6, 1, 1)):
            self.got(k, self.cut(self.land, slot, which))

        def total(rows, cols):
            sides = self.land[1, rows, cols].astype(jnp.float32)
            sides = sides + self.land[2, rows, cols].astype(jnp.float32)
            return self.both(me, rows, cols) + sides

        if self.turned:

            def turn(i):
                cols = pl.ds(pl.multiple_of(i, 128), 128)
                value = total(pl.ds(0, self.gr), cols).T
                self.mine[cols] = value
                self.zout[cols] = value.astype(jnp.bfloat16)

            by_rows(self.cols, 128, turn)
        else:

            def add(i):
                rows = pl.ds(i, step)
                value = total(rows, pl.ds(0, self.cols))
                self.mine[rows] = value
                self.zout[rows] = value.astype(jnp.bfloat16)

            by_rows(self.gr, step, add)
        for k in range(1, p.chain):
            z = p.zpeer(k)
            src = self.zout.at[pl.ds(pl.multiple_of(z * self.rows, self.rows), self.rows)]
            dst = self.zin.at[pl.ds((k - 1) * self.rows, self.rows)]
            self.go(6 + k, src, dst, p.dev(p.s, z))

    def done(self, result):
        p, step = self.p, self.step
        for k in range(1, p.chain):
            self.got(6 + k, self.zin.at[pl.ds((k - 1) * self.rows, self.rows)])
        start = p.z * self.rows

        def add(i):
            value = self.mine[pl.ds(pl.multiple_of(start + i, step), step)]
            for k in range(1, p.chain):
                value = value + self.zin[pl.ds((k - 1) * self.rows + i, step)].astype(jnp.float32)
            result(i, value)

        by_rows(self.rows, step, add)

    def drain(self):
        for copy in self.sent:
            copy.wait_send()


SCATTER_SEMS = 14


def scatter_scratch(chain, rows, cols, flip):
    f32, bf16 = jnp.float32, jnp.bfloat16
    gr = chain * rows
    block = (cols, gr) if flip else (gr, cols)
    return [
        pltpu.VMEM((4, 2) + block, bf16),
        pltpu.VMEM((4,) + block, bf16),
        pltpu.VMEM((3,) + block, bf16),
        pltpu.VMEM((3,) + block, bf16),
        pltpu.VMEM((gr, cols), f32),
        pltpu.VMEM((gr, cols), bf16),
        pltpu.VMEM((max(1, chain - 1) * rows, cols), bf16),
    ]


class Exchange:
    def __init__(self, place, land, send, recv):
        self.p, self.land, self.send, self.recv = place, land, send, recv
        self.sent = []

    def go(self, source):
        p = self.p
        for d in range(1, 8):
            peer = lax.rem(p.s + d, 8)
            copy = remote(
                source(peer), self.land.at[p.s], self.send.at[d - 1], self.recv.at[d - 1], p.dev(peer)
            )
            copy.start()
            self.sent.append(copy)

    def wait(self):
        p = self.p
        for d in range(1, 8):
            ref = self.land.at[lax.rem(p.s + 8 - d, 8)]
            remote(ref, ref, self.send.at[d - 1], self.recv.at[d - 1], p.dev(p.sib)).wait_recv()

    def drain(self):
        for copy in self.sent:
            copy.wait_send()


def dot_nn(a, b):
    return lax.dot_general(a, b, (((1,), (0,)), ((), ())), preferred_element_type=jnp.float32)


def dot_nt(a, b):
    return lax.dot_general(a, b, (((1,), (1,)), ((), ())), preferred_element_type=jnp.float32)


def dot_tn(a, b):
    return lax.dot_general(a, b, (((0,), (0,)), ((), ())), preferred_element_type=jnp.float32)


def total_of(values):
    return jnp.sum(jnp.sum(values, 1, keepdims=True), 0, keepdims=True)


def fold_rows(values):
    rows, cols = values.shape
    return jnp.sum(values.reshape(rows // 8, 8, cols), 0)


NEG = -1e30
ORDER = ("norm", "qkv", "out", "up", "down")
SUMS = (("norm", 16, 256), ("q", 16, 512), ("k", 16, 512), ("v", 16, 512), ("out", 16, 512), ("up0", 16, 512), ("up1", 16, 512), ("up2", 16, 512), ("up3", 16, 512), ("down", 64, 512))
LEFT = math.sqrt(2.0 / math.pi)
CUBE = 0.044715


def layer_kernel(chain, rate, names, *refs):
    r = dict(zip(names, refs))
    f32, bf16 = jnp.float32, jnp.bfloat16
    place = Place(chain)
    x_ref, dy_ref, docs_ref = r["tokens"], r["grad"], r["docs"]
    rows_all, width = x_ref.shape
    span, spans = SPAN, rows_all // SPAN
    pairs = width // 128
    hidden_size = r["s_up"].shape[1]
    devices = 8 * chain
    per = width // devices
    entries = 8 * spans * width
    chunk = 256
    chunks = rows_all // chunk

    gathers = {}
    r["npad"][...] = jnp.zeros_like(r["npad"])
    r["npad"][0:4, 0:per] = r["s_norm"][...]
    qkv_cols, mid_cols = 3 * width, width
    w_qkv, w_norm = r["w_first"].at[:, 0:qkv_cols], r["w_first"].at[:, qkv_cols : qkv_cols + 128]
    w_out, w_up = r["w_mid"].at[:, 0:mid_cols], r["w_mid"].at[:, mid_cols : mid_cols + hidden_size]
    w_down = r["w_down"]
    for m, (name, parts) in enumerate(
        (("first", ("s_qkv", "npad")), ("mid", ("s_out", "s_up")), ("down", ("s_down",)))
    ):
        piece = r[parts[0]].shape[0]
        g = Gather(place, r["w_" + name], piece, r["gsend"].at[m], r["grecv"].at[m])
        own, start = g.piece(place.s, place.z), 0
        for part in parts:
            cols = r[part].shape[1]
            own[:, start : start + cols] = r[part][...].astype(bf16)
            start += cols
        gathers[name] = g
    scatters = {}
    for m, (name, piece, _) in enumerate(SUMS):
        bufs = [r[f"c_{name}{i}"] for i in range(7)]
        scatters[name] = Scatter(
            place, piece, name == "down", bufs, r["csend"].at[m], r["crecv"].at[m]
        )
    first = Exchange(place, r["summ"], r["esend"].at[0], r["erecv"].at[0])
    second = Exchange(place, r["back"], r["esend"].at[1], r["erecv"].at[1])
    place.barrier()
    gathers["first"].start()
    for name in ("first", "mid", "down"):
        gathers[name].sides(0)

    F, D, mixed, heads = r["F"], r["D"], r["mixed"], r["heads"]
    loads = []
    for name in ORDER:
        for kind in ("m_", "a_"):
            sem = r["lsem"].at[len(loads)]
            loads.append(pltpu.make_async_copy(r[kind + name], r["v" + kind + name], sem))
            loads[-1].start()

    def advance_rows(name, rows, cols, total):
        scaled = rate * total
        moment = 0.9 * r["vm_" + name][rows, cols] + scaled
        weight = r["s_" + name][rows, cols] - (scaled + 0.9 * moment)
        average = 0.99 * r["va_" + name][rows, cols] + 0.01 * weight
        for k, value in enumerate((weight, moment, average)):
            r["t_" + name][k, rows, cols] = value

    def update(name, start):
        def rows_done(i, total):
            advance_rows(name, pl.ds(i, 16), slice(start, start + total.shape[1]), total)

        return rows_done

    def update_norm(i, total):
        advance_rows("norm", slice(0, 4), slice(0, per), total[0:4, 0:per])

    def norm_one(i):
        rows = pl.ds(i, 128)
        values = x_ref[rows].astype(f32)
        centre = values - jnp.mean(values, -1, keepdims=True)
        spread = jnp.mean(centre * centre, -1, keepdims=True)
        inv = lax.rsqrt(spread + 1e-05)
        F[rows] = centre * inv
        r["inv1"][rows] = jnp.broadcast_to(inv, (128, 128))

    by_rows(rows_all // 2, 128, norm_one)
    gathers["first"].chain_done()
    gathers["mid"].start()
    gathers["down"].start()
    lax.fori_loop(rows_all // 256, rows_all // 128, lambda i, c: (norm_one(i * 128), c)[1], 0)

    ids = r["doc_ids"]
    docs = jnp.concatenate([ids[0:1, p * span : p * span + span] for p in range(spans)], 0).astype(f32)
    docs_ref[...] = docs
    wide = jnp.concatenate([docs] * (128 // spans), 0).T
    for p in range(spans):
        r["dcol"][pl.ds(p * span, span)] = jnp.broadcast_to(wide[:, p : p + 1], (span, 128))

    gathers["first"].sides_done()

    def turn_grad(i):
        rows = pl.ds(pl.multiple_of(i, 128), 128)
        r["dyT"][:, rows] = dy_ref[rows].T

    gathers["first"].corner_done()
    gathers["mid"].chain_done()
    gathers["first"].done()

    place_row = lax.broadcasted_iota(jnp.int32, (128, width), 0)
    place_col = lax.broadcasted_iota(jnp.int32, (128, width), 1)
    pick = (lax.rem(place_col, per) == place_row).astype(f32).astype(bf16)
    owner_row = lax.div(lax.broadcasted_iota(jnp.int32, (16 * devices, width), 0), 16)
    owner_col = lax.div(lax.broadcasted_iota(jnp.int32, (16 * devices, width), 1), per)
    spread_rows = dot_nn(w_norm[...], pick)
    spread_rows = jnp.where(owner_row == owner_col, spread_rows, 0.0)
    norm_rows = jnp.sum(spread_rows.reshape(devices, 16, width), 0)
    r["nrows"][...] = norm_rows


    def project(i):
        rows = pl.ds(pl.multiple_of(i, chunk), chunk)
        act = (F[rows] * r["nrows"][0:1] + r["nrows"][1:2]).astype(bf16)
        r["act1T"][:, rows] = act.T
        result = dot_nn(act, w_qkv[...])
        mixed[rows, 0:width] = (result[:, :width] * 0.125).astype(bf16)
        mixed[rows, width : 3 * width] = result[:, width:].astype(bf16)

    by_rows(rows_all, chunk, project)

    last_doc = docs[:, span - 1 : span]
    member = (docs == last_doc).astype(f32)
    count = jnp.sum(member, 1, keepdims=True)
    which = lax.broadcasted_iota(jnp.int32, (spans, span), 0)
    blocks = [jnp.where(which == p, member, 0.0) for p in range(spans)]
    left = jnp.concatenate(blocks, 1)
    left = jnp.concatenate([left, jnp.zeros_like(left)], 0).astype(bf16)
    means = dot_nn(left, mixed[:, width : 3 * width])[:spans] / count
    summ = r["summ"]
    summ[place.s, :, 0 : 2 * width] = means
    summ[place.s, :, 2 * width : 2 * width + 128] = jnp.broadcast_to(last_doc, (spans, 128))
    first.go(lambda peer: summ.at[place.s])
    by_rows(rows_all, 128, turn_grad)
    gathers["down"].chain_done()
    first.wait()

    sums = summ[...].reshape(8 * spans, 2 * width + 128)
    keys = sums[:, :width]
    stat_mean = total_of(keys) / entries
    centred = keys - stat_mean
    stat_var = total_of(centred * centred) / entries
    inv_sum = lax.rsqrt(stat_var + 1e-05)
    key_norm = centred * inv_sum
    r["knorm"][...] = key_norm
    lane = lax.broadcasted_iota(jnp.int32, (span, 128), 1)
    low_half = lane < 64
    lane_row = lax.broadcasted_iota(jnp.int32, (1, 128), 1)
    pick0 = (lane_row < 64).astype(f32).astype(bf16)
    pick1 = (lane_row >= 64).astype(f32).astype(bf16)
    for j in range(pairs):
        cols = slice(128 * j, 128 * j + 128)
        part = key_norm[:, cols].astype(bf16)
        r["KR"][j] = jnp.concatenate([part * pick0, part * pick1], 0)
        part = sums[:, width + 128 * j : width + 128 * j + 128].astype(bf16)
        r["VR"][j] = jnp.concatenate([part * pick0, part * pick1], 0)
    last = sums[:, 2 * width :]
    r["lastrow"][...] = jnp.concatenate([last, last], 0).T[0:8]

    probs = r["probs"]
    causal = lax.broadcasted_iota(jnp.int32, (span, 128), 0) >= lax.broadcasted_iota(
        jnp.int32, (span, 128), 1
    )
    span_first = place.s * spans
    quarter = spans // 4

    def attend(p, carry):
        rows = pl.ds(pl.multiple_of(p * span, span), span)
        column = r["dcol"][rows]
        mask_local = (column == docs_ref[pl.ds(p, 1)]) & causal
        mask_remote = (column == r["lastrow"][0:1]) & (lax.rem(lane, 64) < span_first + p)
        scores, lows = [], []
        for j in range(pairs):
            query = mixed[rows, 128 * j : 128 * j + 128]
            key = mixed[rows, width + 128 * j : width + 128 * j + 128]
            scores.append(dot_nt(query, jnp.concatenate([key * pick0, key * pick1, r["KR"][j]], 0)))
        for j in range(pairs):
            one = jnp.where(mask_local, scores[j][:, :128], NEG)
            two = jnp.where(mask_local, scores[j][:, 128:256], NEG)
            far = jnp.where(mask_remote, scores[j][:, 256:], NEG)
            peak1 = jnp.max(jnp.maximum(one, jnp.where(low_half, far, NEG)), -1, keepdims=True)
            peak2 = jnp.max(jnp.maximum(two, jnp.where(low_half, NEG, far)), -1, keepdims=True)
            one = jnp.exp(one - peak1)
            two = jnp.exp(two - peak2)
            far = jnp.exp(far - jnp.where(low_half, peak1, peak2))
            scale1 = 1.0 / jnp.sum(one + jnp.where(low_half, far, 0.0), -1, keepdims=True)
            scale2 = 1.0 / jnp.sum(two + jnp.where(low_half, 0.0, far), -1, keepdims=True)
            one = one * scale1
            two = two * scale2
            far = far * jnp.where(low_half, scale1, scale2)
            base = 384 * j
            probs[rows, base : base + 128] = one
            probs[rows, base + 128 : base + 256] = two
            probs[rows, base + 256 : base + 384] = far
            lows.append(jnp.concatenate([one, two, far], 1).astype(bf16))
        for j in range(pairs):
            value = mixed[rows, 2 * width + 128 * j : 2 * width + 128 * j + 128]
            values = jnp.concatenate([value * pick0, value * pick1, r["VR"][j]], 0)
            heads[rows, 128 * j : 128 * j + 128] = dot_nn(lows[j], values).astype(bf16)
        return carry

    lax.fori_loop(0, quarter, attend, 0)
    gathers["mid"].sides_done()
    lax.fori_loop(quarter, 2 * quarter, attend, 0)
    gathers["down"].sides_done()
    gathers["mid"].corner_done()
    lax.fori_loop(2 * quarter, 3 * quarter, attend, 0)
    lax.fori_loop(3 * quarter, spans, attend, 0)
    gathers["mid"].done()

    r["ngrad"][...] = jnp.zeros_like(r["ngrad"])
    tile = 256

    def feed(i):
        rows = pl.ds(pl.multiple_of(i, chunk), chunk)
        part = heads[rows]
        r["headsT"][:, rows] = part.T
        after = x_ref[rows].astype(f32) + dot_nn(part, w_out[...])
        centre = after - jnp.mean(after, -1, keepdims=True)
        spread = jnp.mean(centre * centre, -1, keepdims=True)
        inv = lax.rsqrt(spread + 1e-05)
        normal = centre * inv
        F[rows] = after
        D[rows] = normal
        r["inv2"][rows] = jnp.broadcast_to(inv, (chunk, 128))
        act_two = (normal * r["nrows"][2:3] + r["nrows"][3:4]).astype(bf16)
        r["act2"][rows] = act_two
        r["act2T"][:, rows] = act_two.T

    by_rows(rows_all, chunk, feed)
    for name in ("down",):
        gathers[name].corner_done()
        gathers[name].done()

    down, out = scatters["down"], scatters["out"]
    ups = [scatters[f"up{g}"] for g in range(4)]
    quad = hidden_size // 4

    def put(target, grad, cols):
        gr = target.gr
        for g in range(4):
            for c in range(2):
                k = (2 * g + c) * gr
                target.full[g, c, :, cols] = grad[k : k + gr]

    for g in range(4):

        def mlp(i, g=g):
            rows = pl.ds(pl.multiple_of(i, chunk), chunk)
            for start in range(g * quad, g * quad + quad, tile):
                cols = slice(start, start + tile)
                h = dot_nn(r["act2"][rows], w_up[:, cols])
                d = dot_nt(dy_ref[rows], w_down[cols])
                square = h * h
                gate = 0.5 + 0.5 * jnp.tanh(h * (LEFT + (LEFT * CUBE) * square))
                act = h * gate
                r["act3"][rows, cols] = act.astype(bf16)
                slope = gate + act * (2.0 * LEFT + (6.0 * LEFT * CUBE) * square) * (1.0 - gate)
                r["dhid"][rows, cols] = (d * slope).astype(bf16)

        by_rows(rows_all, chunk, mlp)
        if g:
            ups[g - 1].core_done()
        grad = dot_nn(r["dyT"][...], r["act3"][:, g * quad : g * quad + quad]).astype(bf16)
        down.full[g, 0] = grad[:, : quad // 2]
        down.full[g, 1] = grad[:, quad // 2 :]
        down.start_group(g)
        grad = dot_nn(r["act2T"][...], r["dhid"][:, g * quad : g * quad + quad]).astype(bf16)
        put(ups[g], grad, pl.ds(0, quad))
        ups[g].start()

    def feed_back(i):
        rows = pl.ds(pl.multiple_of(i, chunk), chunk)
        d_two = dot_nt(r["dhid"][rows], w_up[...])
        normal = D[rows]
        r["ngrad"][2] += fold_rows(d_two * normal)
        r["ngrad"][3] += fold_rows(d_two)
        scaled = d_two * r["nrows"][2:3]
        centred = (
            scaled
            - jnp.mean(scaled, -1, keepdims=True)
            - normal * jnp.mean(scaled * normal, -1, keepdims=True)
        )
        d_after = dy_ref[rows].astype(f32) + r["inv2"][rows][:, 0:1] * centred
        D[rows] = d_after
        low = d_after.astype(bf16)
        r["dafter"][rows] = low
        heads[rows] = dot_nt(low, w_out[...]).astype(bf16)

    lax.fori_loop(0, chunks // 2, lambda i, c: (feed_back(i * chunk), c)[1], 0)
    ups[3].core_done()
    ups[0].sides_done()
    down.core_done()
    lax.fori_loop(chunks // 2, chunks, lambda i, c: (feed_back(i * chunk), c)[1], 0)
    ups[1].sides_done()
    put(out, dot_nn(r["headsT"][...], r["dafter"][...]).astype(bf16), pl.ds(0, width))
    out.start()
    ups[2].sides_done()

    kept = r["dhid"]
    side = 384 * pairs

    def attend_back(p, carry):
        rows = pl.ds(pl.multiple_of(p * span, span), span)
        wide_probs, d_scores, stacks = [], [], []
        for j in range(pairs):
            key = mixed[rows, width + 128 * j : width + 128 * j + 128]
            value = mixed[rows, 2 * width + 128 * j : 2 * width + 128 * j + 128]
            stacks.append(jnp.concatenate([key * pick0, key * pick1, r["KR"][j]], 0))
            values_all = jnp.concatenate([value * pick0, value * pick1, r["VR"][j]], 0)
            wide_probs.append(dot_nt(heads[rows, 128 * j : 128 * j + 128], values_all))
        for j in range(pairs):
            d_probs = wide_probs[j]
            base = 384 * j
            one = probs[rows, base : base + 128]
            two = probs[rows, base + 128 : base + 256]
            far = probs[rows, base + 256 : base + 384]
            d_far = far * d_probs[:, 256:]
            sum1 = jnp.sum(one * d_probs[:, :128] + jnp.where(low_half, d_far, 0.0), -1, keepdims=True)
            sum2 = jnp.sum(two * d_probs[:, 128:256] + jnp.where(low_half, 0.0, d_far), -1, keepdims=True)
            d_one = one * (d_probs[:, :128] - sum1)
            d_two = two * (d_probs[:, 128:256] - sum2)
            d_far = far * (d_probs[:, 256:] - jnp.where(low_half, sum1, sum2))
            d_scores.append(jnp.concatenate([d_one, d_two, d_far], 1).astype(bf16))
            kept[rows, base : base + 384] = d_scores[j]
            kept[rows, side + 128 * j : side + 128 * j + 128] = far.astype(bf16)
        for j in range(pairs):
            at = slice(128 * j, 128 * j + 128)
            r["act2"][rows, at] = (0.125 * dot_nn(d_scores[j], stacks[j])).astype(bf16)
        return carry

    lax.fori_loop(0, quarter, attend_back, 0)
    ups[3].sides_done()
    out.core_done()
    lax.fori_loop(quarter, 2 * quarter, attend_back, 0)
    down.sides_done()
    ups[0].mine_done()
    lax.fori_loop(2 * quarter, 3 * quarter, attend_back, 0)
    out.sides_done()
    ups[1].mine_done()
    lax.fori_loop(3 * quarter, spans, attend_back, 0)
    ups[2].mine_done()

    half_spans = 8 * spans
    parts = []
    for name in ("key", "value"):
        for j in range(pairs):
            at = slice(128 * j, 128 * j + 128)
            if name == "key":
                both = dot_tn(kept[:, 384 * j + 256 : 384 * j + 384], mixed[:, at])
            else:
                both = dot_tn(kept[:, side + 128 * j : side + 128 * j + 128], heads[:, at])
            low = low_half[:half_spans]
            parts.append(jnp.where(low, both[:half_spans], both[half_spans:]))
    d_keys = jnp.concatenate(parts[:pairs], 1)
    d_values = jnp.concatenate(parts[pairs:], 1)
    key_norm = r["knorm"][...]
    flat = jnp.where(lane_row < 64, total_of(d_keys), total_of(d_keys * key_norm))
    send = r["sendback"]
    send[:, :, 0:width] = d_keys.reshape(8, spans, width)
    send[:, :, width : 2 * width] = d_values.reshape(8, spans, width)
    send[:, :, 2 * width :] = jnp.broadcast_to(flat.reshape(1, 1, 128), (8, spans, 128))
    back = r["back"]
    back[place.s] = send[place.s]
    second.go(lambda peer: send.at[peer])

    q_sum, k_sum, v_sum = scatters["q"], scatters["k"], scatters["v"]
    put(q_sum, dot_nn(r["act1T"][...], r["act2"][...]).astype(bf16), pl.ds(0, width))
    q_sum.start()
    ups[3].mine_done()
    down.mine_done()

    def local_back(p, carry):
        rows = pl.ds(pl.multiple_of(p * span, span), span)
        d_keys, d_values = [], []
        for j in range(pairs):
            at = slice(128 * j, 128 * j + 128)
            low = probs[rows, 384 * j : 384 * j + 256].astype(bf16)
            d_keys.append(dot_tn(kept[rows, 384 * j : 384 * j + 256], mixed[rows, at]))
            d_values.append(dot_tn(low, heads[rows, at]))
        for j in range(pairs):
            at = slice(128 * j, 128 * j + 128)
            probs[rows, at] = jnp.where(low_half, d_keys[j][:128], d_keys[j][128:])
            past = slice(width + 128 * j, width + 128 * j + 128)
            probs[rows, past] = jnp.where(low_half, d_values[j][:128], d_values[j][128:])
        return carry

    lax.fori_loop(0, 2 * quarter, local_back, 0)
    q_sum.core_done()
    out.mine_done()
    lax.fori_loop(2 * quarter, spans, local_back, 0)
    second.wait()

    owned = jnp.sum(back[...], 0)
    back_sum = owned[0:1, 2 * width : 2 * width + 1]
    back_cross = owned[0:1, 2 * width + 64 : 2 * width + 65]
    mine_norm = r["knorm"][pl.ds(pl.multiple_of(place.s * spans, spans), spans)]
    d_sum_key = inv_sum * (
        owned[:, :width] - back_sum * (1.0 / entries) - mine_norm * (back_cross * (1.0 / entries))
    )
    r["dsum"][:, 0:width] = d_sum_key / count
    r["dsum"][:, width : 2 * width] = owned[:, width : 2 * width] / count
    slot = lax.broadcasted_iota(jnp.int32, (8, 128), 1)
    stats = jnp.where(slot == 0, stat_mean, stat_var)
    stats = jnp.where(slot == 2, -inv_sum * back_sum, stats)
    stats = jnp.where(slot == 3, -0.5 * inv_sum * inv_sum * back_cross, stats)
    r["stats"][...] = stats

    def join(p, carry):
        rows = pl.ds(pl.multiple_of(p * span, span), span)
        final = docs_ref[pl.ds(p, 1)][:, span - 1 : span]
        share = (r["dcol"][rows] == final).astype(f32)
        sums_row = r["dsum"][pl.ds(p, 1)]
        for j in range(pairs):
            at = slice(128 * j, 128 * j + 128)
            past = slice(width + 128 * j, width + 128 * j + 128)
            full = probs[rows, at] + share * sums_row[:, at]
            mixed[rows, past] = full.astype(bf16)
            full = probs[rows, past] + share * sums_row[:, past]
            mixed[rows, 2 * width + 128 * j : 2 * width + 128 * j + 128] = full.astype(bf16)
        return carry

    lax.fori_loop(0, spans, join, 0)

    put(k_sum, dot_nn(r["act1T"][...], mixed[:, width : 2 * width]).astype(bf16), pl.ds(0, width))
    k_sum.start()
    put(v_sum, dot_nn(r["act1T"][...], mixed[:, 2 * width :]).astype(bf16), pl.ds(0, width))
    v_sum.start()
    q_sum.sides_done()

    def first_back(i):
        rows = pl.ds(pl.multiple_of(i, chunk), chunk)
        d_one = dot_nt(r["act2"][rows], w_qkv[:, 0:width])
        d_one = d_one + dot_nt(mixed[rows, width : 3 * width], w_qkv[:, width : 3 * width])
        values = x_ref[rows].astype(f32)
        inv = r["inv1"][rows][:, 0:1]
        normal = (values - jnp.mean(values, -1, keepdims=True)) * inv
        r["ngrad"][0] += fold_rows(d_one * normal)
        r["ngrad"][1] += fold_rows(d_one)
        scaled = d_one * r["nrows"][0:1]
        centred = (
            scaled
            - jnp.mean(scaled, -1, keepdims=True)
            - normal * jnp.mean(scaled * normal, -1, keepdims=True)
        )
        r["input_grad"][rows] = D[rows] + inv * centred

    half_chunks = chunks // 2
    lax.fori_loop(0, half_chunks, lambda i, c: (first_back(i * chunk), c)[1], 0)
    k_sum.core_done()
    v_sum.core_done()
    lax.fori_loop(half_chunks, chunks, lambda i, c: (first_back(i * chunk), c)[1], 0)

    pieces = jnp.concatenate(
        [jnp.sum(r["ngrad"][k], 0, keepdims=True) for k in range(4)]
        + [jnp.zeros((12, width), f32)],
        0,
    )
    spread_rows = jnp.broadcast_to(pieces[None], (devices, 16, width)).reshape(16 * devices, width)
    spread_rows = jnp.where(owner_row == owner_col, spread_rows, 0.0).astype(bf16)
    norm = scatters["norm"]
    narrow = dot_nt(spread_rows, pick).astype(bf16)
    put(norm, jnp.concatenate([narrow, jnp.zeros_like(narrow)], 1), pl.ds(0, 256))
    norm.start()
    k_sum.sides_done()
    v_sum.sides_done()
    norm.core_done()
    q_sum.mine_done()

    def output(i):
        rows = pl.ds(pl.multiple_of(i, chunk), chunk)
        result = F[rows] + dot_nn(r["act3"][rows], w_down[...])
        r["block_out"][rows] = result.astype(bf16)

    lax.fori_loop(0, half_chunks, lambda i, c: (output(i * chunk), c)[1], 0)
    k_sum.mine_done()
    v_sum.mine_done()
    norm.sides_done()
    lax.fori_loop(half_chunks, chunks, lambda i, c: (output(i * chunk), c)[1], 0)
    norm.mine_done()
    for copy in loads:
        copy.wait()
    for name in ("down", "out"):
        scatters[name].done(update(name, 0))
    for g in range(4):
        ups[g].done(update("up", g * quad))
    q_sum.done(update("qkv", 0))
    k_sum.done(update("qkv", width))
    v_sum.done(update("qkv", 2 * width))
    norm.done(update_norm)
    for part in list(gathers.values()) + list(scatters.values()) + [first, second]:
        part.drain()


def fused_layer(chain, rate, tokens, grad, doc_ids, shards, moments, averages):
    f32, bf16 = jnp.float32, jnp.bfloat16
    rows, width = tokens.shape
    spans = rows // SPAN
    order = ORDER
    devices = 8 * chain
    ins = [("tokens", tokens), ("grad", grad), ("doc_ids", doc_ids)]
    ins += [("s_" + name, shards[name]) for name in order]
    ins += [("m_" + name, moments[name]) for name in order]
    ins += [("a_" + name, averages[name]) for name in order]
    outs = [
        ("block_out", pltpu.VMEM((rows, width), bf16)),
        ("input_grad", pltpu.VMEM((rows, width), f32)),
        ("stats", pltpu.VMEM((8, 128), f32)),
    ]
    outs += [("t_" + name, pltpu.VMEM((3,) + shards[name].shape, f32)) for name in order]
    hidden = shards["up"].shape[1]
    scratch = {}
    down_rows = shards["down"].shape[0]
    scratch["w_first"] = pltpu.VMEM((devices * 16, 3 * width + 128), bf16)
    scratch["w_mid"] = pltpu.VMEM((devices * 16, width + hidden), bf16)
    scratch["w_down"] = pltpu.VMEM((devices * down_rows, width), bf16)
    for name, piece, cols in SUMS:
        for i, buf in enumerate(scatter_scratch(chain, piece, cols, name == "down")):
            scratch[f"c_{name}{i}"] = buf
    for name in order:
        scratch["vm_" + name] = pltpu.VMEM(shards[name].shape, f32)
        scratch["va_" + name] = pltpu.VMEM(shards[name].shape, f32)
    scratch["lsem"] = DMA((10,))
    payload = (8, spans, 2 * width + 128)
    pairs = width // 128
    scratch |= {
        "gsend": DMA((3, GATHER_SEMS)),
        "grecv": DMA((3, GATHER_SEMS)),
        "csend": DMA((10, SCATTER_SEMS)),
        "crecv": DMA((10, SCATTER_SEMS)),
        "esend": DMA((2, 7)),
        "erecv": DMA((2, 7)),
        "summ": pltpu.VMEM(payload, f32),
        "back": pltpu.VMEM(payload, f32),
        "sendback": pltpu.VMEM(payload, f32),
        "F": pltpu.VMEM((rows, width), f32),
        "inv1": pltpu.VMEM((rows, 128), f32),
        "dcol": pltpu.VMEM((rows, 128), f32),
        "nrows": pltpu.VMEM((16, width), f32),
        "ngrad": pltpu.VMEM((4, 8, width), f32),
        "act1T": pltpu.VMEM((width, rows), bf16),
        "dyT": pltpu.VMEM((width, rows), bf16),
        "act2T": pltpu.VMEM((width, rows), bf16),
        "headsT": pltpu.VMEM((width, rows), bf16),
        "mixed": pltpu.VMEM((rows, 3 * width), bf16),
        "probs": pltpu.VMEM((rows, 384 * pairs), f32),
        "heads": pltpu.VMEM((rows, width), bf16),
        "knorm": pltpu.VMEM((8 * spans, width), f32),
        "KR": pltpu.VMEM((pairs, 128, 128), bf16),
        "VR": pltpu.VMEM((pairs, 128, 128), bf16),
        "lastrow": pltpu.VMEM((8, 128), f32),
        "docs": pltpu.VMEM((spans, SPAN), f32),
        "npad": pltpu.VMEM((16, 128), f32),
        "inv2": pltpu.VMEM((rows, 128), f32),
        "act2": pltpu.VMEM((rows, width), bf16),
        "act3": pltpu.VMEM((rows, hidden), bf16),
        "dhid": pltpu.VMEM((rows, hidden), bf16),
        "dafter": pltpu.VMEM((rows, width), bf16),
        "D": pltpu.VMEM((rows, width), f32),
        "dsum": pltpu.VMEM((spans, 2 * width), f32),
    }
    names = [n for n, _ in ins] + [n for n, _ in outs] + list(scratch)
    vmem = pl.BlockSpec(memory_space=pltpu.VMEM)
    result = pl.pallas_call(
        functools.partial(layer_kernel, chain, rate, names),
        out_shape=[shape for _, shape in outs],
        in_specs=[vmem] * (len(ins) - 10) + [pl.BlockSpec(memory_space=pltpu.HBM)] * 10,
        out_specs=[vmem] * len(outs),
        scratch_shapes=list(scratch.values()),
        compiler_params=pltpu.CompilerParams(
            collective_id=0, has_side_effects=True, vmem_limit_bytes=59 * 2**20
        ),
    )(*[value for _, value in ins])
    return dict(zip([n for n, _ in outs], result))


def finish_kernel(count, *refs):
    ins, outs, sems = refs[:count], refs[count:-1], refs[-1]
    stats, two = ins[-1], outs[count - 1 :]
    copies = [pltpu.make_async_copy(ins[k], outs[k], sems.at[k]) for k in range(count - 1)]
    for copy in copies:
        copy.start()
    two[0][...] = stats[0:1, 0:2]
    two[1][...] = stats[0:1, 2:4]
    for copy in copies:
        copy.wait()


def finish(arrays, stats):
    vmem = pl.BlockSpec(memory_space=pltpu.VMEM)
    two = jax.ShapeDtypeStruct((1, 2), jnp.float32)
    count = len(arrays) + 1
    return pl.pallas_call(
        functools.partial(finish_kernel, count),
        out_shape=[jax.ShapeDtypeStruct(a.shape, a.dtype) for a in arrays] + [two, two],
        in_specs=[pl.BlockSpec(memory_space=pl.ANY)] * (count - 1) + [vmem],
        out_specs=[pl.BlockSpec(memory_space=pltpu.HBM)] * (count - 1) + [vmem] * 2,
        scratch_shapes=[DMA((count - 1,))],
        compiler_params=pltpu.CompilerParams(vmem_limit_bytes=2 * 2**20),
    )(*(pltpu.with_memory_space_constraint(a, pltpu.VMEM) for a in arrays), stats)


def norm_forward(values, gain_row, shift_row):
    centre = values - jnp.mean(values, -1, keepdims=True)
    spread = jnp.mean(centre * centre, -1, keepdims=True)
    inv_std = lax.rsqrt(spread + 1e-05)
    normal = centre * inv_std
    return (normal * gain_row + shift_row, normal, inv_std)


def norm_backward(grad_in, normal, inv_std, gain_row):
    scaled = grad_in * gain_row
    centred = (
        scaled
        - jnp.mean(scaled, -1, keepdims=True)
        - normal * jnp.mean(scaled * normal, -1, keepdims=True)
    )
    return (inv_std * centred, jnp.sum(grad_in * normal, 0), jnp.sum(grad_in, 0))


def gelu_tanh(values):
    return jax.nn.gelu(values, approximate=True)


def span_probs(query_blk, key_blk, key_remote, doc_span, last_remote, span_first):
    span_len = doc_span.shape[2]
    local = (
        jnp.einsum("bpqhe,bpkhe->bphqk", query_blk, key_blk, preferred_element_type=jnp.float32)
        * 0.125
    )
    remote = (
        jnp.einsum("bpqhe,bnhe->bphqn", query_blk, key_remote, preferred_element_type=jnp.float32)
        * 0.125
    )
    positions = jnp.arange(span_len)
    causal = positions[:, None] >= positions[None, :]
    same_doc = doc_span[:, :, :, None] == doc_span[:, :, None, :]
    mask_local = (same_doc & causal[None, None])[:, :, None]
    span_ids = span_first + jnp.arange(doc_span.shape[1])
    earlier = jnp.arange(key_remote.shape[1])[None, :] < span_ids[:, None]
    doc_float = doc_span.astype(jnp.float32)
    match = doc_float[:, :, :, None] == last_remote.astype(jnp.float32)[:, None, None, :]
    mask_remote = (match & earlier[None, :, None, :])[:, :, None]
    allowed = jnp.concatenate([mask_local, mask_remote], -1)
    scores = jnp.where(allowed, jnp.concatenate([local, remote], -1), -1e30)
    peak_score = jnp.max(scores, -1, keepdims=True)
    raised = jnp.exp(scores - peak_score)
    return raised / jnp.sum(raised, -1, keepdims=True)


def advance(weight, moment, average, grad, rate):
    new_moment = 0.9 * moment + rate * grad
    new_weight = weight - (rate * grad + 0.9 * new_moment)
    new_average = 0.99 * average + 0.01 * new_weight
    return jnp.stack([new_weight, new_moment, new_average])


def shards_plain(
    tokens,
    grad_out,
    doc_ids,
    qkv_w,
    qkv_m,
    qkv_a,
    out_w,
    out_m,
    out_a,
    up_w,
    up_m,
    up_a,
    down_w,
    down_m,
    down_a,
    norm_w,
    norm_m,
    norm_a,
):
    seqs, seq_len, width = tokens.shape
    span_len = SPAN
    cycle_size = lax.axis_size("seq")
    cycle_rank = lax.axis_index("seq")
    spans_dev = seq_len // span_len
    spans_all = spans_dev * cycle_size
    rows_dev = seqs * seq_len
    head_size = width // H
    bf16 = jnp.bfloat16
    f32 = jnp.float32
    w_qkv, w_out, w_up, w_down, norm_low = (
        lax.all_gather(qkv_w.astype(bf16), ("seq", "dp"), axis=0, tiled=True),
        lax.all_gather(out_w.astype(bf16), ("seq", "dp"), axis=0, tiled=True),
        lax.all_gather(up_w.astype(bf16), ("seq", "dp"), axis=0, tiled=True),
        lax.all_gather(down_w.astype(bf16), ("seq", "dp"), axis=0, tiled=True),
        lax.all_gather(norm_w.astype(bf16), ("seq", "dp"), axis=1, tiled=True),
    )
    norm_rows = norm_low.astype(f32)
    inputs = tokens.reshape(rows_dev, width).astype(f32)
    normed_one, normal_one, inv_one = norm_forward(inputs, norm_rows[0], norm_rows[1])
    act_one = normed_one.astype(bf16)
    mixed = jnp.dot(act_one, w_qkv, preferred_element_type=f32)
    query = mixed[:, :width].astype(bf16)
    key_all = mixed[:, width : 2 * width].astype(bf16)
    value_all = mixed[:, 2 * width :].astype(bf16)
    block_shape = (seqs, spans_dev, span_len, H, head_size)
    query_blk = query.reshape(block_shape)
    key_blk = key_all.reshape(block_shape)
    value_blk = value_all.reshape(block_shape)
    doc_span = doc_ids.reshape(seqs, spans_dev, span_len)
    last_doc = doc_span[:, :, -1]
    member = (doc_span == last_doc[:, :, None]).astype(f32)
    counts = jnp.sum(member, -1)
    member_low = member.astype(bf16)
    key_four = key_all.reshape(seqs, spans_dev, span_len, width)
    value_four = value_all.reshape(seqs, spans_dev, span_len, width)
    sum_key = (
        jnp.einsum("bpt,bptd->bpd", member_low, key_four, preferred_element_type=f32)
        / counts[..., None]
    )
    sum_value = (
        jnp.einsum("bpt,bptd->bpd", member_low, value_four, preferred_element_type=f32)
        / counts[..., None]
    )
    total_sum, total_square = lax.psum(
        (jnp.sum(sum_key, (1, 2)), jnp.sum(sum_key * sum_key, (1, 2))), "seq"
    )
    entries = spans_all * width
    stat_mean = total_sum / entries
    stat_var = total_square / entries - stat_mean * stat_mean
    inv_sum = lax.rsqrt(stat_var + 1e-05)
    key_norm = (sum_key - stat_mean[:, None, None]) * inv_sum[:, None, None]
    key_send = key_norm.astype(bf16)
    value_send = sum_value.astype(bf16)
    last_send = last_doc.astype(bf16)
    key_remote, value_remote, last_remote = (
        lax.all_gather(key_send, "seq", axis=1, tiled=True),
        lax.all_gather(value_send, "seq", axis=1, tiled=True),
        lax.all_gather(last_send, "seq", axis=1, tiled=True),
    )
    remote_shape = (seqs, spans_all, H, head_size)
    span_first = cycle_rank * spans_dev
    probs = span_probs(
        query_blk, key_blk, key_remote.reshape(remote_shape), doc_span, last_remote, span_first
    )
    probs_low = probs.astype(bf16)
    attended = jnp.einsum(
        "bphqk,bpkhe->bpqhe", probs_low[..., :span_len], value_blk, preferred_element_type=f32
    )
    attended = attended + jnp.einsum(
        "bphqn,bnhe->bpqhe",
        probs_low[..., span_len:],
        value_remote.reshape(remote_shape),
        preferred_element_type=f32,
    )
    heads_out = attended.reshape(rows_dev, width).astype(bf16)
    after_attn = inputs + jnp.dot(heads_out, w_out, preferred_element_type=f32)
    normed_two, normal_two, inv_two = norm_forward(after_attn, norm_rows[2], norm_rows[3])
    act_two = normed_two.astype(bf16)
    hidden = jnp.dot(act_two, w_up, preferred_element_type=f32)
    act_three = gelu_tanh(hidden).astype(bf16)
    result = after_attn + jnp.dot(act_three, w_down, preferred_element_type=f32)
    block_out = result.astype(bf16).reshape(seqs, seq_len, width)
    stats_out = jnp.stack([stat_mean, stat_var], -1)
    grad_low = grad_out.reshape(rows_dev, width)
    grad_down = jnp.einsum("tf,td->fd", act_three, grad_low, preferred_element_type=f32)
    d_three = jnp.einsum("td,fd->tf", grad_low, w_down, preferred_element_type=f32)
    unused_out, gelu_pull = jax.vjp(gelu_tanh, hidden)
    d_hidden = gelu_pull(d_three)[0].astype(bf16)
    grad_up = jnp.einsum("td,tf->df", act_two, d_hidden, preferred_element_type=f32)
    d_two = jnp.einsum("tf,df->td", d_hidden, w_up, preferred_element_type=f32)
    d_norm_two, gain_two, shift_two = norm_backward(d_two, normal_two, inv_two, norm_rows[2])
    d_after = grad_low.astype(f32) + d_norm_two
    d_after_low = d_after.astype(bf16)
    grad_outw = jnp.einsum("tc,td->cd", heads_out, d_after_low, preferred_element_type=f32)
    d_heads = jnp.einsum("td,cd->tc", d_after_low, w_out, preferred_element_type=f32).astype(bf16)
    key_back, value_back, last_back = (key_remote, value_remote, last_remote)
    key_back_blk = key_back.reshape(remote_shape)
    value_back_blk = value_back.reshape(remote_shape)
    probs_back = span_probs(query_blk, key_blk, key_back_blk, doc_span, last_back, span_first)
    probs_back_low = probs_back.astype(bf16)
    d_heads_blk = d_heads.reshape(block_shape)
    d_probs = jnp.concatenate(
        [
            jnp.einsum("bpqhe,bpkhe->bphqk", d_heads_blk, value_blk, preferred_element_type=f32),
            jnp.einsum(
                "bpqhe,bnhe->bphqn", d_heads_blk, value_back_blk, preferred_element_type=f32
            ),
        ],
        -1,
    )
    row_dot = jnp.sum(probs_back * d_probs, -1, keepdims=True)
    d_scores = (probs_back * (d_probs - row_dot)).astype(bf16)
    d_local = d_scores[..., :span_len]
    d_remote = d_scores[..., span_len:]
    d_query = 0.125 * (
        jnp.einsum("bphqk,bpkhe->bpqhe", d_local, key_blk, preferred_element_type=f32)
        + jnp.einsum("bphqn,bnhe->bpqhe", d_remote, key_back_blk, preferred_element_type=f32)
    )
    d_key = 0.125 * jnp.einsum("bphqk,bpqhe->bpkhe", d_local, query_blk, preferred_element_type=f32)
    d_value = jnp.einsum(
        "bphqk,bpqhe->bpkhe",
        probs_back_low[..., :span_len],
        d_heads_blk,
        preferred_element_type=f32,
    )
    d_key_sum = (
        0.125 * jnp.einsum("bphqn,bpqhe->bnhe", d_remote, query_blk, preferred_element_type=f32)
    ).reshape(seqs, spans_all, width)
    d_value_sum = jnp.einsum(
        "bphqn,bpqhe->bnhe", probs_back_low[..., span_len:], d_heads_blk, preferred_element_type=f32
    ).reshape(seqs, spans_all, width)
    owned_key, owned_value = (
        lax.psum_scatter(
            d_key_sum.astype(jnp.bfloat16), "seq", scatter_dimension=1, tiled=True
        ).astype(jnp.float32),
        lax.psum_scatter(
            d_value_sum.astype(jnp.bfloat16), "seq", scatter_dimension=1, tiled=True
        ).astype(jnp.float32),
    )
    back_sum, back_cross = lax.psum(
        (jnp.sum(owned_key, (1, 2)), jnp.sum(owned_key * key_norm, (1, 2))), "seq"
    )
    stat_grads = jnp.stack([-inv_sum * back_sum, -0.5 * inv_sum * inv_sum * back_cross], -1)
    d_sum_key = inv_sum[:, None, None] * (
        owned_key
        - back_sum[:, None, None] / entries
        - key_norm * back_cross[:, None, None] / entries
    )
    share = member / counts[..., None]
    d_key_all = (
        d_key.reshape(seqs, spans_dev, span_len, width)
        + share[..., None] * d_sum_key[:, :, None, :]
    )
    d_value_all = (
        d_value.reshape(seqs, spans_dev, span_len, width)
        + share[..., None] * owned_value[:, :, None, :]
    )
    d_mixed = jnp.concatenate(
        [
            d_query.reshape(rows_dev, width),
            d_key_all.reshape(rows_dev, width),
            d_value_all.reshape(rows_dev, width),
        ],
        -1,
    ).astype(bf16)
    grad_qkv = jnp.einsum("td,tf->df", act_one, d_mixed, preferred_element_type=f32)
    d_one = jnp.einsum("tf,df->td", d_mixed, w_qkv, preferred_element_type=f32)
    d_norm_one, gain_one, shift_one = norm_backward(d_one, normal_one, inv_one, norm_rows[0])
    input_grad = (d_after + d_norm_one).reshape(seqs, seq_len, width)
    grad_norm = jnp.stack([gain_one, shift_one, gain_two, shift_two])
    sum_qkv, sum_outw, sum_up, sum_down, sum_norm = (
        lax.psum_scatter(grad_qkv, ("seq", "dp"), scatter_dimension=0, tiled=True),
        lax.psum_scatter(grad_outw, ("seq", "dp"), scatter_dimension=0, tiled=True),
        lax.psum_scatter(grad_up, ("seq", "dp"), scatter_dimension=0, tiled=True),
        lax.psum_scatter(grad_down, ("seq", "dp"), scatter_dimension=0, tiled=True),
        lax.psum_scatter(grad_norm, ("seq", "dp"), scatter_dimension=1, tiled=True),
    )
    tokens_all = rows_dev * cycle_size * lax.axis_size("dp")
    rate = 0.02 / math.sqrt(tokens_all)
    return (
        block_out,
        input_grad,
        stats_out,
        stat_grads,
        advance(qkv_w, qkv_m, qkv_a, sum_qkv, rate),
        advance(out_w, out_m, out_a, sum_outw, rate),
        advance(up_w, up_m, up_a, sum_up, rate),
        advance(down_w, down_m, down_a, sum_down, rate),
        advance(norm_w, norm_m, norm_a, sum_norm, rate),
    )


def shards(*args):
    tokens, grad_out, doc_ids = args[:3]
    qkv_w = args[3]
    seqs, seq_len, width = tokens.shape
    fits = lax.axis_size("seq") == 8 and qkv_w.shape[0] % 16 == 0
    fits = fits and seqs == 1 and seq_len == 8 * SPAN and width == 512
    if not fits:
        return shards_plain(*args)
    chain = lax.axis_size("dp")
    names = {"qkv": 3, "out": 6, "up": 9, "down": 12, "norm": 15}
    done = fused_layer(
        chain,
        0.02 / math.sqrt(seq_len * 8 * chain),
        tokens.reshape(seq_len, width),
        grad_out.reshape(seq_len, width),
        doc_ids,
        *({name: args[k + j] for name, k in names.items()} for j in range(3)),
    )
    order = ["block_out", "input_grad"] + ["t_" + name for name in names]
    result = finish([done[name] for name in order], done["stats"])
    return (
        result[0].reshape(tokens.shape),
        result[1].reshape(tokens.shape),
        *result[7:],
        *result[2:7],
    )


def solution(mesh):
    placed = (
        P("dp", "seq", None),
        P("dp", "seq", None),
        P("dp", "seq"),
        P(("seq", "dp"), None),
        P(("seq", "dp"), None),
        P(("seq", "dp"), None),
        P(("seq", "dp"), None),
        P(("seq", "dp"), None),
        P(("seq", "dp"), None),
        P(("seq", "dp"), None),
        P(("seq", "dp"), None),
        P(("seq", "dp"), None),
        P(("seq", "dp"), None),
        P(("seq", "dp"), None),
        P(("seq", "dp"), None),
        P(None, ("seq", "dp")),
        P(None, ("seq", "dp")),
        P(None, ("seq", "dp")),
    )
    return jax.shard_map(
        shards,
        mesh=mesh,
        in_specs=placed,
        out_specs=(
            P("dp", "seq", None),
            P("dp", "seq", None),
            P("dp", None),
            P("dp", None),
            P(None, ("seq", "dp"), None),
            P(None, ("seq", "dp"), None),
            P(None, ("seq", "dp"), None),
            P(None, ("seq", "dp"), None),
            P(None, None, ("seq", "dp")),
        ),
        check_vma=False,
    )
```

```python
import functools
import math

import jax
import jax.numpy as jnp
from jax import lax
from jax.experimental import pallas as pl
from jax.experimental.pallas import tpu as pltpu
from jax.sharding import PartitionSpec as P

H = 8
SPAN = 128
MESH = pl.DeviceIdType.MESH
DMA = pltpu.SemaphoreType.DMA


class Place:
    def __init__(self, chain):
        self.chain = chain
        self.s = lax.axis_index("seq")
        self.z = lax.axis_index("dp")
        self.core = lax.rem(self.s, 2)
        self.group = lax.div(self.s, 2)
        self.sib = self.flip(self.s, 1)
        self.xs = self.flip(self.s, 2)
        self.ys = self.flip(self.s, 4)
        self.ds = self.flip(self.xs, 4)

    @staticmethod
    def flip(value, bit):
        return value + bit - 2 * bit * lax.rem(lax.div(value, bit), 2)

    def dev(self, s, z=None):
        return {"seq": s, "dp": self.z if z is None else z}

    def zflip(self, bits):
        z = self.z
        for bit in (1, 2):
            if bits & bit:
                z = self.flip(z, bit)
        return z

    def zpeer(self, step):
        return lax.rem(self.z + step, self.chain)

    def barrier(self, extra=()):
        sem = pltpu.get_barrier_semaphore()
        peers = [self.dev(self.sib), self.dev(self.xs), self.dev(self.ys)]
        peers += [self.dev(self.s, self.zpeer(k)) for k in range(1, self.chain)]
        peers += list(extra)
        for peer in peers:
            pl.semaphore_signal(sem, inc=1, device_id=peer, device_id_type=MESH)
        pl.semaphore_wait(sem, len(peers))


def remote(src, dst, send, recv, peer):
    return pltpu.make_async_remote_copy(
        src_ref=src, dst_ref=dst, send_sem=send, recv_sem=recv, device_id=peer, device_id_type=MESH
    )


class Gather:
    def __init__(self, place, full, rows, send, recv):
        self.p, self.full, self.rows = place, full, rows
        self.send, self.recv = send, recv
        self.gr = place.chain * rows
        self.sent = []

    def region(self, s):
        return self.full.at[pl.ds(pl.multiple_of(s * self.gr, self.gr), self.gr)]

    def piece(self, s, z):
        start = pl.multiple_of(s * self.gr + z * self.rows, self.rows)
        return self.full.at[pl.ds(start, self.rows)]

    def go(self, k, ref, peer):
        copy = remote(ref, ref, self.send.at[k], self.recv.at[k], peer)
        copy.start()
        self.sent.append(copy)

    def got(self, k, ref):
        remote(ref, ref, self.send.at[k], self.recv.at[k], self.p.dev(self.p.sib)).wait_recv()

    def sides(self, k):
        p = self.p
        piece = self.piece(p.s, p.zflip(k))
        self.go(3 + k, piece, p.dev(p.xs))
        self.go(7 + k, piece, p.dev(p.ys))

    def start(self):
        p = self.p
        for k in range(1, p.chain):
            self.go(k - 1, self.piece(p.s, p.z), p.dev(p.s, p.zflip(k)))

    def chain_piece(self, k):
        p = self.p
        if 0 < k < p.chain:
            self.got(k - 1, self.piece(p.s, p.zflip(k)))
            self.sides(k)
        if k == 3:
            self.go(19, self.region(p.s), p.dev(p.sib))

    def chain_done(self):
        for k in range(1, 4):
            self.chain_piece(k)

    def sides_done(self, part=(0, 1)):
        p = self.p
        middle = (p.chain + 1) // 2
        steps = [range(middle), range(middle, p.chain)]
        for k in [k for one in part for k in steps[one]]:
            self.got(3 + k, self.piece(p.xs, p.zflip(k)))
            if k < middle:
                self.go(11 + k, self.piece(p.xs, p.zflip(k)), p.dev(p.ys))
            self.got(7 + k, self.piece(p.ys, p.zflip(k)))
            if k >= middle:
                self.go(11 + k, self.piece(p.ys, p.zflip(k)), p.dev(p.xs))
        if part[-1] == 1:
            self.go(20, self.region(p.xs), p.dev(p.sib))
            self.go(21, self.region(p.ys), p.dev(p.sib))

    def corner_done(self):
        p = self.p
        for k in range(p.chain):
            self.got(11 + k, self.piece(p.ds, p.zflip(k)))
        self.go(22, self.region(p.ds), p.dev(p.sib))

    def done(self):
        p = self.p
        for k, s in ((19, p.s), (20, p.xs), (21, p.ys), (22, p.ds)):
            self.got(k, self.region(p.flip(s, 1)))

    def drain(self):
        for copy in self.sent:
            copy.wait_send()


GATHER_SEMS = 23


def by_rows(count, step, body):
    def trip(i, carry):
        body(pl.multiple_of(i * step, step))
        return carry

    lax.fori_loop(0, count // step, trip, 0)


class Scatter:
    def __init__(self, place, rows, flip, bufs, send, recv):
        self.p, self.rows, self.turned = place, rows, flip
        self.full, self.in2, self.stage, self.land, self.mine, self.zout, self.zin = bufs
        self.gr, self.cols = self.full.shape[2], self.full.shape[3]
        self.half = self.cols // 2
        self.step = 16
        self.send, self.recv = send, recv
        self.sent = []

    def go(self, k, src, dst, peer):
        copy = remote(src, dst, self.send.at[k], self.recv.at[k], peer)
        copy.start()
        self.sent.append(copy)

    def got(self, k, ref):
        remote(ref, ref, self.send.at[k], self.recv.at[k], self.p.dev(self.p.sib)).wait_recv()

    def near(self, bits):
        g = self.p.group
        for bit in (1, 2):
            if bits & bit:
                g = Place.flip(g, bit)
        return g

    def cut(self, ref, slot, which):
        return ref.at[slot, :, pl.ds(which * self.half, self.half)]

    def both(self, g, rows, cols):
        mine = self.full[g, self.p.core, rows, cols].astype(jnp.float32)
        return mine + self.in2[g, rows, cols].astype(jnp.float32)

    def start(self):
        self.go(0, self.full.at[:, 1 - self.p.core], self.in2, self.p.dev(self.p.sib))

    def start_group(self, g):
        self.go(10 + g, self.full.at[g, 1 - self.p.core], self.in2.at[g], self.p.dev(self.p.sib))

    def core_done(self):
        p, step = self.p, self.step
        if self.turned:
            for g in range(4):
                self.got(10 + g, self.in2.at[g])
        else:
            self.got(0, self.in2)
        far, xg, yg = self.near(3), self.near(1), self.near(2)
        whole = pl.ds(0, self.cols)
        first, second = pl.ds(0, self.half), pl.ds(self.half, self.half)

        def sum_far(i):
            rows = pl.ds(i, step)
            self.stage[0, rows] = self.both(far, rows, whole).astype(jnp.bfloat16)

        by_rows(self.gr, step, sum_far)
        self.go(1, self.cut(self.stage, 0, 0), self.cut(self.land, 0, 0), p.dev(p.xs))
        self.go(2, self.cut(self.stage, 0, 1), self.cut(self.land, 0, 1), p.dev(p.ys))

        def sum_sides(i):
            rows = pl.ds(i, step)
            self.stage[1, rows, first] = self.both(xg, rows, first).astype(jnp.bfloat16)
            self.stage[2, rows, second] = self.both(yg, rows, second).astype(jnp.bfloat16)

        by_rows(self.gr, step, sum_sides)
        self.go(3, self.cut(self.stage, 1, 0), self.cut(self.land, 1, 0), p.dev(p.xs))
        self.go(4, self.cut(self.stage, 2, 1), self.cut(self.land, 2, 1), p.dev(p.ys))

    def sides_done(self):
        p, step = self.p, self.step
        for k, slot, which, bits, peer in ((5, 2, 0, 2, p.ys), (6, 1, 1, 1, p.xs)):
            self.got(k - 4, self.cut(self.land, 0, which))
            cols = pl.ds(which * self.half, self.half)
            g = self.near(bits)

            def add(i, slot=slot, cols=cols, g=g):
                rows = pl.ds(i, step)
                total = self.both(g, rows, cols) + self.land[0, rows, cols].astype(jnp.float32)
                self.stage[slot, rows, cols] = total.astype(jnp.bfloat16)

            by_rows(self.gr, step, add)
            self.go(k, self.cut(self.stage, slot, which), self.cut(self.land, slot, which), p.dev(peer))

    def mine_done(self):
        p, step = self.p, self.step
        me = p.group
        for k, slot, which in ((3, 1, 0), (4, 2, 1), (5, 2, 0), (6, 1, 1)):
            self.got(k, self.cut(self.land, slot, which))

        def total(rows, cols):
            sides = self.land[1, rows, cols].astype(jnp.float32)
            sides = sides + self.land[2, rows, cols].astype(jnp.float32)
            return self.both(me, rows, cols) + sides

        if self.turned:

            def turn(i):
                cols = pl.ds(pl.multiple_of(i, 128), 128)
                value = total(pl.ds(0, self.gr), cols).T
                self.mine[cols] = value
                self.zout[cols] = value.astype(jnp.bfloat16)

            by_rows(self.cols, 128, turn)
        else:

            def add(i):
                rows = pl.ds(i, step)
                value = total(rows, pl.ds(0, self.cols))
                self.mine[rows] = value
                self.zout[rows] = value.astype(jnp.bfloat16)

            by_rows(self.gr, step, add)
        for k in range(1, p.chain):
            z = p.zpeer(k)
            src = self.zout.at[pl.ds(pl.multiple_of(z * self.rows, self.rows), self.rows)]
            dst = self.zin.at[pl.ds((k - 1) * self.rows, self.rows)]
            self.go(6 + k, src, dst, p.dev(p.s, z))

    def done(self, result):
        p, step = self.p, self.step
        for k in range(1, p.chain):
            self.got(6 + k, self.zin.at[pl.ds((k - 1) * self.rows, self.rows)])
        start = p.z * self.rows

        def add(i):
            value = self.mine[pl.ds(pl.multiple_of(start + i, step), step)]
            for k in range(1, p.chain):
                value = value + self.zin[pl.ds((k - 1) * self.rows + i, step)].astype(jnp.float32)
            result(i, value)

        by_rows(self.rows, step, add)

    def drain(self):
        for copy in self.sent:
            copy.wait_send()


SCATTER_SEMS = 14


def scatter_scratch(chain, rows, cols, flip):
    f32, bf16 = jnp.float32, jnp.bfloat16
    gr = chain * rows
    block = (cols, gr) if flip else (gr, cols)
    return [
        pltpu.VMEM((4, 2) + block, bf16),
        pltpu.VMEM((4,) + block, bf16),
        pltpu.VMEM((3,) + block, bf16),
        pltpu.VMEM((3,) + block, bf16),
        pltpu.VMEM((gr, cols), f32),
        pltpu.VMEM((gr, cols), bf16),
        pltpu.VMEM((max(1, chain - 1) * rows, cols), bf16),
    ]


class Exchange:
    def __init__(self, place, land, send, recv):
        self.p, self.land, self.send, self.recv = place, land, send, recv
        self.sent = []

    def go(self, source):
        p = self.p
        for d in range(1, 8):
            peer = lax.rem(p.s + d, 8)
            copy = remote(
                source(peer), self.land.at[p.s], self.send.at[d - 1], self.recv.at[d - 1], p.dev(peer)
            )
            copy.start()
            self.sent.append(copy)

    def wait(self):
        p = self.p
        for d in range(1, 8):
            ref = self.land.at[lax.rem(p.s + 8 - d, 8)]
            remote(ref, ref, self.send.at[d - 1], self.recv.at[d - 1], p.dev(p.sib)).wait_recv()

    def drain(self):
        for copy in self.sent:
            copy.wait_send()


def dot_nn(a, b):
    return lax.dot_general(a, b, (((1,), (0,)), ((), ())), preferred_element_type=jnp.float32)


def dot_nt(a, b):
    return lax.dot_general(a, b, (((1,), (1,)), ((), ())), preferred_element_type=jnp.float32)


def dot_tn(a, b):
    return lax.dot_general(a, b, (((0,), (0,)), ((), ())), preferred_element_type=jnp.float32)


def total_of(values):
    return jnp.sum(jnp.sum(values, 1, keepdims=True), 0, keepdims=True)


def fold_rows(values):
    rows, cols = values.shape
    return jnp.sum(values.reshape(rows // 8, 8, cols), 0)


NEG = -1e30
ORDER = ("norm", "qkv", "out", "up", "down")
SUMS = (("norm", 16, 256), ("q", 16, 512), ("k", 16, 512), ("v", 16, 512), ("out", 16, 512), ("up0", 16, 512), ("up1", 16, 512), ("up2", 16, 512), ("up3", 16, 512), ("down", 64, 512))
LEFT = math.sqrt(2.0 / math.pi)
CUBE = 0.044715


def layer_kernel(chain, rate, names, *refs):
    r = dict(zip(names, refs))
    f32, bf16 = jnp.float32, jnp.bfloat16
    place = Place(chain)
    x_ref, dy_ref, docs_ref = r["tokens"], r["grad"], r["docs"]
    rows_all, width = x_ref.shape
    span, spans = SPAN, rows_all // SPAN
    pairs = width // 128
    hidden_size = r["s_up"].shape[1]
    devices = 8 * chain
    per = width // devices
    entries = 8 * spans * width
    chunk = 256
    chunks = rows_all // chunk

    gathers = {}
    r["npad"][...] = jnp.zeros_like(r["npad"])
    r["npad"][0:4, 0:per] = r["s_norm"][...]
    past_cols, mid_cols = 2 * width, width
    w_past = r["w_first"].at[:, 0:past_cols]
    w_norm = r["w_first"].at[:, past_cols : past_cols + 128]
    w_query = r["w_query"]
    w_out, w_up = r["w_mid"].at[:, 0:mid_cols], r["w_mid"].at[:, mid_cols : mid_cols + hidden_size]
    w_down = r["w_down"]
    r["past"] = r["s_qkv"].at[:, width : 3 * width]
    r["query"] = r["s_qkv"].at[:, 0:width]
    for m, (name, parts) in enumerate(
        (
            ("first", ("past", "npad")),
            ("query", ("query",)),
            ("mid", ("s_out", "s_up")),
            ("down", ("s_down",)),
        )
    ):
        piece = r[parts[0]].shape[0]
        g = Gather(place, r["w_" + name], piece, r["gsend"].at[m], r["grecv"].at[m])
        own, start = g.piece(place.s, place.z), 0
        for part in parts:
            cols = r[part].shape[1]
            own[:, start : start + cols] = r[part][...].astype(bf16)
            start += cols
        gathers[name] = g
    scatters = {}
    for m, (name, piece, _) in enumerate(SUMS):
        bufs = [r[f"c_{name}{i}"] for i in range(7)]
        scatters[name] = Scatter(
            place, piece, name == "down", bufs, r["csend"].at[m], r["crecv"].at[m]
        )
    first = Exchange(place, r["summ"], r["esend"].at[0], r["erecv"].at[0])
    second = Exchange(place, r["back"], r["esend"].at[1], r["erecv"].at[1])
    place.barrier()
    for name in ("first", "query"):
        gathers[name].start()
    for name in ("first", "query", "mid"):
        gathers[name].sides(0)

    F, D, mixed, heads = r["F"], r["D"], r["mixed"], r["heads"]
    loads = []
    for name in ORDER:
        for kind in ("m_", "a_"):
            sem = r["lsem"].at[len(loads)]
            loads.append(pltpu.make_async_copy(r[kind + name], r["v" + kind + name], sem))
            loads[-1].start()

    def advance_rows(name, rows, cols, total):
        scaled = rate * total
        moment = 0.9 * r["vm_" + name][rows, cols] + scaled
        weight = r["s_" + name][rows, cols] - (scaled + 0.9 * moment)
        average = 0.99 * r["va_" + name][rows, cols] + 0.01 * weight
        for k, value in enumerate((weight, moment, average)):
            r["t_" + name][k, rows, cols] = value

    def update(name, start):
        def rows_done(i, total):
            advance_rows(name, pl.ds(i, 16), slice(start, start + total.shape[1]), total)

        return rows_done

    def update_norm(i, total):
        advance_rows("norm", slice(0, 4), slice(0, per), total[0:4, 0:per])

    def norm_one(i):
        rows = pl.ds(i, 128)
        values = x_ref[rows].astype(f32)
        centre = values - jnp.mean(values, -1, keepdims=True)
        spread = jnp.mean(centre * centre, -1, keepdims=True)
        inv = lax.rsqrt(spread + 1e-05)
        F[rows] = centre * inv
        r["inv1"][rows] = jnp.broadcast_to(inv, (128, 128))

    by_rows(rows_all // 2, 128, norm_one)
    gathers["first"].chain_done()
    gathers["mid"].start()
    lax.fori_loop(rows_all // 256, rows_all // 128, lambda i, c: (norm_one(i * 128), c)[1], 0)

    ids = r["doc_ids"]
    docs = jnp.concatenate([ids[0:1, p * span : p * span + span] for p in range(spans)], 0).astype(f32)
    docs_ref[...] = docs
    wide = jnp.concatenate([docs] * (128 // spans), 0).T
    for p in range(spans):
        r["dcol"][pl.ds(p * span, span)] = jnp.broadcast_to(wide[:, p : p + 1], (span, 128))

    gathers["query"].chain_done()
    gathers["down"].start()
    gathers["first"].sides_done()
    gathers["query"].sides_done()
    gathers["mid"].chain_piece(1)

    def turn_grad(i):
        rows = pl.ds(pl.multiple_of(i, 128), 128)
        r["dyT"][:, rows] = dy_ref[rows].T

    gathers["first"].corner_done()
    gathers["first"].done()
    gathers["mid"].chain_piece(2)

    place_row = lax.broadcasted_iota(jnp.int32, (128, width), 0)
    place_col = lax.broadcasted_iota(jnp.int32, (128, width), 1)
    pick = (lax.rem(place_col, per) == place_row).astype(f32).astype(bf16)
    owner_row = lax.div(lax.broadcasted_iota(jnp.int32, (16 * devices, width), 0), 16)
    owner_col = lax.div(lax.broadcasted_iota(jnp.int32, (16 * devices, width), 1), per)
    spread_rows = dot_nn(w_norm[...], pick)
    spread_rows = jnp.where(owner_row == owner_col, spread_rows, 0.0)
    norm_rows = jnp.sum(spread_rows.reshape(devices, 16, width), 0)
    r["nrows"][...] = norm_rows


    def project(i):
        rows = pl.ds(pl.multiple_of(i, chunk), chunk)
        act = (F[rows] * r["nrows"][0:1] + r["nrows"][1:2]).astype(bf16)
        r["act1T"][:, rows] = act.T
        mixed[rows, width : 3 * width] = dot_nn(act, w_past[...]).astype(bf16)
        r["act2"][rows] = act

    by_rows(rows_all, chunk, project)

    last_doc = docs[:, span - 1 : span]
    member = (docs == last_doc).astype(f32)
    count = jnp.sum(member, 1, keepdims=True)
    which = lax.broadcasted_iota(jnp.int32, (spans, span), 0)
    blocks = [jnp.where(which == p, member, 0.0) for p in range(spans)]
    left = jnp.concatenate(blocks, 1)
    left = jnp.concatenate([left, jnp.zeros_like(left)], 0).astype(bf16)
    means = dot_nn(left, mixed[:, width : 3 * width])[:spans] / count
    summ = r["summ"]
    summ[place.s, :, 0 : 2 * width] = means
    summ[place.s, :, 2 * width : 2 * width + 128] = jnp.broadcast_to(last_doc, (spans, 128))
    first.go(lambda peer: summ.at[place.s])
    gathers["query"].corner_done()
    gathers["mid"].chain_piece(3)
    gathers["mid"].sides_done((0,))
    gathers["query"].done()

    def project_query(i):
        rows = pl.ds(pl.multiple_of(i, chunk), chunk)
        mixed[rows, 0:width] = (dot_nn(r["act2"][rows], w_query[...]) * 0.125).astype(bf16)

    by_rows(rows_all, chunk, project_query)
    by_rows(rows_all, 128, turn_grad)
    first.wait()
    gathers["mid"].sides_done((1,))
    gathers["down"].sides(0)

    sums = summ[...].reshape(8 * spans, 2 * width + 128)
    keys = sums[:, :width]
    stat_mean = total_of(keys) / entries
    centred = keys - stat_mean
    stat_var = total_of(centred * centred) / entries
    inv_sum = lax.rsqrt(stat_var + 1e-05)
    key_norm = centred * inv_sum
    r["knorm"][...] = key_norm
    lane = lax.broadcasted_iota(jnp.int32, (span, 128), 1)
    low_half = lane < 64
    lane_row = lax.broadcasted_iota(jnp.int32, (1, 128), 1)
    pick0 = (lane_row < 64).astype(f32).astype(bf16)
    pick1 = (lane_row >= 64).astype(f32).astype(bf16)
    for j in range(pairs):
        cols = slice(128 * j, 128 * j + 128)
        part = key_norm[:, cols].astype(bf16)
        r["KR"][j] = jnp.concatenate([part * pick0, part * pick1], 0)
        part = sums[:, width + 128 * j : width + 128 * j + 128].astype(bf16)
        r["VR"][j] = jnp.concatenate([part * pick0, part * pick1], 0)
    last = sums[:, 2 * width :]
    r["lastrow"][...] = jnp.concatenate([last, last], 0).T[0:8]

    probs = r["probs"]
    causal = lax.broadcasted_iota(jnp.int32, (span, 128), 0) >= lax.broadcasted_iota(
        jnp.int32, (span, 128), 1
    )
    span_first = place.s * spans
    quarter = spans // 4

    def attend(p, carry):
        rows = pl.ds(pl.multiple_of(p * span, span), span)
        column = r["dcol"][rows]
        mask_local = (column == docs_ref[pl.ds(p, 1)]) & causal
        mask_remote = (column == r["lastrow"][0:1]) & (lax.rem(lane, 64) < span_first + p)
        scores, lows = [], []
        for j in range(pairs):
            query = mixed[rows, 128 * j : 128 * j + 128]
            key = mixed[rows, width + 128 * j : width + 128 * j + 128]
            scores.append(dot_nt(query, jnp.concatenate([key * pick0, key * pick1, r["KR"][j]], 0)))
        for j in range(pairs):
            one = jnp.where(mask_local, scores[j][:, :128], NEG)
            two = jnp.where(mask_local, scores[j][:, 128:256], NEG)
            far = jnp.where(mask_remote, scores[j][:, 256:], NEG)
            peak1 = jnp.max(jnp.maximum(one, jnp.where(low_half, far, NEG)), -1, keepdims=True)
            peak2 = jnp.max(jnp.maximum(two, jnp.where(low_half, NEG, far)), -1, keepdims=True)
            one = jnp.exp(one - peak1)
            two = jnp.exp(two - peak2)
            far = jnp.exp(far - jnp.where(low_half, peak1, peak2))
            scale1 = 1.0 / jnp.sum(one + jnp.where(low_half, far, 0.0), -1, keepdims=True)
            scale2 = 1.0 / jnp.sum(two + jnp.where(low_half, 0.0, far), -1, keepdims=True)
            one = one * scale1
            two = two * scale2
            far = far * jnp.where(low_half, scale1, scale2)
            base = 384 * j
            probs[rows, base : base + 128] = one
            probs[rows, base + 128 : base + 256] = two
            probs[rows, base + 256 : base + 384] = far
            lows.append(jnp.concatenate([one, two, far], 1).astype(bf16))
        for j in range(pairs):
            value = mixed[rows, 2 * width + 128 * j : 2 * width + 128 * j + 128]
            values = jnp.concatenate([value * pick0, value * pick1, r["VR"][j]], 0)
            heads[rows, 128 * j : 128 * j + 128] = dot_nn(lows[j], values).astype(bf16)
        return carry

    gathers["down"].chain_done()
    lax.fori_loop(0, 3 * quarter, attend, 0)
    gathers["mid"].corner_done()
    lax.fori_loop(3 * quarter, spans, attend, 0)
    gathers["mid"].done()

    r["ngrad"][...] = jnp.zeros_like(r["ngrad"])
    tile = 256

    def feed(i):
        rows = pl.ds(pl.multiple_of(i, chunk), chunk)
        part = heads[rows]
        r["headsT"][:, rows] = part.T
        after = x_ref[rows].astype(f32) + dot_nn(part, w_out[...])
        centre = after - jnp.mean(after, -1, keepdims=True)
        spread = jnp.mean(centre * centre, -1, keepdims=True)
        inv = lax.rsqrt(spread + 1e-05)
        normal = centre * inv
        F[rows] = after
        D[rows] = normal
        r["inv2"][rows] = jnp.broadcast_to(inv, (chunk, 128))
        act_two = (normal * r["nrows"][2:3] + r["nrows"][3:4]).astype(bf16)
        r["act2"][rows] = act_two
        r["act2T"][:, rows] = act_two.T

    lax.fori_loop(0, chunks // 2, lambda i, c: (feed(i * chunk), c)[1], 0)
    gathers["down"].sides_done()
    lax.fori_loop(chunks // 2, chunks, lambda i, c: (feed(i * chunk), c)[1], 0)
    gathers["down"].corner_done()
    gathers["down"].done()

    down, out = scatters["down"], scatters["out"]
    ups = [scatters[f"up{g}"] for g in range(4)]
    quad = hidden_size // 4

    def put(target, grad, cols):
        gr = target.gr
        for g in range(4):
            for c in range(2):
                k = (2 * g + c) * gr
                target.full[g, c, :, cols] = grad[k : k + gr]

    for g in range(4):

        def mlp(i, g=g):
            parts = [
                (pl.ds(pl.multiple_of(i + top, chunk), chunk), slice(start, start + tile))
                for top in (0, chunk)
                for start in range(g * quad, g * quad + quad, tile)
            ]
            waiting = []
            for step in range(len(parts) + 1):
                if step < len(parts):
                    rows, cols = parts[step]
                    h = dot_nn(r["act2"][rows], w_up[:, cols])
                    d = dot_nt(dy_ref[rows], w_down[cols])
                    waiting.append((rows, cols, h, d))
                if step:
                    rows, cols, h, d = waiting[step - 1]
                    square = h * h
                    gate = 0.5 + 0.5 * jnp.tanh(h * (LEFT + (LEFT * CUBE) * square))
                    act = h * gate
                    r["act3"][rows, cols] = act.astype(bf16)
                    slope = gate + act * (2.0 * LEFT + (6.0 * LEFT * CUBE) * square) * (1.0 - gate)
                    r["dhid"][rows, cols] = (d * slope).astype(bf16)

        by_rows(rows_all, 2 * chunk, mlp)
        if g:
            ups[g - 1].core_done()
        if g > 1:
            ups[g - 2].sides_done()
        grad = dot_nn(r["dyT"][...], r["act3"][:, g * quad : g * quad + quad]).astype(bf16)
        down.full[g, 0] = grad[:, : quad // 2]
        down.full[g, 1] = grad[:, quad // 2 :]
        down.start_group(g)
        grad = dot_nn(r["act2T"][...], r["dhid"][:, g * quad : g * quad + quad]).astype(bf16)
        put(ups[g], grad, pl.ds(0, quad))
        ups[g].start()

    def feed_back(i):
        rows = pl.ds(pl.multiple_of(i, chunk), chunk)
        d_two = dot_nt(r["dhid"][rows], w_up[...])
        normal = D[rows]
        r["ngrad"][2] += fold_rows(d_two * normal)
        r["ngrad"][3] += fold_rows(d_two)
        scaled = d_two * r["nrows"][2:3]
        centred = (
            scaled
            - jnp.mean(scaled, -1, keepdims=True)
            - normal * jnp.mean(scaled * normal, -1, keepdims=True)
        )
        d_after = dy_ref[rows].astype(f32) + r["inv2"][rows][:, 0:1] * centred
        D[rows] = d_after
        low = d_after.astype(bf16)
        r["dafter"][rows] = low
        heads[rows] = dot_nt(low, w_out[...]).astype(bf16)

    lax.fori_loop(0, chunks // 2, lambda i, c: (feed_back(i * chunk), c)[1], 0)
    ups[3].core_done()
    ups[2].sides_done()
    down.core_done()
    lax.fori_loop(chunks // 2, chunks, lambda i, c: (feed_back(i * chunk), c)[1], 0)
    ups[3].sides_done()
    put(out, dot_nn(r["headsT"][...], r["dafter"][...]).astype(bf16), pl.ds(0, width))
    out.start()

    kept = r["dhid"]
    side = 384 * pairs

    def attend_back(p, carry):
        rows = pl.ds(pl.multiple_of(p * span, span), span)
        wide_probs, d_scores, stacks = [], [], []
        for j in range(pairs):
            key = mixed[rows, width + 128 * j : width + 128 * j + 128]
            value = mixed[rows, 2 * width + 128 * j : 2 * width + 128 * j + 128]
            stacks.append(jnp.concatenate([key * pick0, key * pick1, r["KR"][j]], 0))
            values_all = jnp.concatenate([value * pick0, value * pick1, r["VR"][j]], 0)
            wide_probs.append(dot_nt(heads[rows, 128 * j : 128 * j + 128], values_all))
        for j in range(pairs):
            d_probs = wide_probs[j]
            base = 384 * j
            one = probs[rows, base : base + 128]
            two = probs[rows, base + 128 : base + 256]
            far = probs[rows, base + 256 : base + 384]
            d_far = far * d_probs[:, 256:]
            sum1 = jnp.sum(one * d_probs[:, :128] + jnp.where(low_half, d_far, 0.0), -1, keepdims=True)
            sum2 = jnp.sum(two * d_probs[:, 128:256] + jnp.where(low_half, 0.0, d_far), -1, keepdims=True)
            d_one = one * (d_probs[:, :128] - sum1)
            d_two = two * (d_probs[:, 128:256] - sum2)
            d_far = far * (d_probs[:, 256:] - jnp.where(low_half, sum1, sum2))
            d_scores.append(jnp.concatenate([d_one, d_two, d_far], 1).astype(bf16))
            kept[rows, base : base + 384] = d_scores[j]
            kept[rows, side + 128 * j : side + 128 * j + 128] = far.astype(bf16)
        for j in range(pairs):
            at = slice(128 * j, 128 * j + 128)
            r["act2"][rows, at] = (0.125 * dot_nn(d_scores[j], stacks[j])).astype(bf16)
        return carry

    lax.fori_loop(0, quarter, attend_back, 0)
    ups[0].mine_done()
    out.core_done()
    lax.fori_loop(quarter, 2 * quarter, attend_back, 0)
    ups[1].mine_done()
    lax.fori_loop(2 * quarter, 3 * quarter, attend_back, 0)
    ups[2].mine_done()
    lax.fori_loop(3 * quarter, spans, attend_back, 0)

    half_spans = 8 * spans
    parts = []
    for name in ("key", "value"):
        for j in range(pairs):
            at = slice(128 * j, 128 * j + 128)
            if name == "key":
                both = dot_tn(kept[:, 384 * j + 256 : 384 * j + 384], mixed[:, at])
            else:
                both = dot_tn(kept[:, side + 128 * j : side + 128 * j + 128], heads[:, at])
            low = low_half[:half_spans]
            parts.append(jnp.where(low, both[:half_spans], both[half_spans:]))
    d_keys = jnp.concatenate(parts[:pairs], 1)
    d_values = jnp.concatenate(parts[pairs:], 1)
    key_norm = r["knorm"][...]
    flat = jnp.where(lane_row < 64, total_of(d_keys), total_of(d_keys * key_norm))
    send = r["sendback"]
    send[:, :, 0:width] = d_keys.reshape(8, spans, width)
    send[:, :, width : 2 * width] = d_values.reshape(8, spans, width)
    send[:, :, 2 * width :] = jnp.broadcast_to(flat.reshape(1, 1, 128), (8, spans, 128))
    back = r["back"]
    back[place.s] = send[place.s]
    second.go(lambda peer: send.at[peer])

    q_sum, k_sum, v_sum = scatters["q"], scatters["k"], scatters["v"]
    put(q_sum, dot_nn(r["act1T"][...], r["act2"][...]).astype(bf16), pl.ds(0, width))
    q_sum.start()
    down.sides_done()
    ups[3].mine_done()

    def local_back(p, carry):
        rows = pl.ds(pl.multiple_of(p * span, span), span)
        d_keys, d_values = [], []
        for j in range(pairs):
            at = slice(128 * j, 128 * j + 128)
            low = probs[rows, 384 * j : 384 * j + 256].astype(bf16)
            d_keys.append(dot_tn(kept[rows, 384 * j : 384 * j + 256], mixed[rows, at]))
            d_values.append(dot_tn(low, heads[rows, at]))
        for j in range(pairs):
            at = slice(128 * j, 128 * j + 128)
            probs[rows, at] = jnp.where(low_half, d_keys[j][:128], d_keys[j][128:])
            past = slice(width + 128 * j, width + 128 * j + 128)
            probs[rows, past] = jnp.where(low_half, d_values[j][:128], d_values[j][128:])
        return carry

    lax.fori_loop(0, 2 * quarter, local_back, 0)
    out.sides_done()
    q_sum.core_done()
    lax.fori_loop(2 * quarter, spans, local_back, 0)
    second.wait()

    owned = jnp.sum(back[...], 0)
    back_sum = owned[0:1, 2 * width : 2 * width + 1]
    back_cross = owned[0:1, 2 * width + 64 : 2 * width + 65]
    mine_norm = r["knorm"][pl.ds(pl.multiple_of(place.s * spans, spans), spans)]
    d_sum_key = inv_sum * (
        owned[:, :width] - back_sum * (1.0 / entries) - mine_norm * (back_cross * (1.0 / entries))
    )
    r["dsum"][:, 0:width] = d_sum_key / count
    r["dsum"][:, width : 2 * width] = owned[:, width : 2 * width] / count
    slot = lax.broadcasted_iota(jnp.int32, (8, 128), 1)
    stats = jnp.where(slot == 0, stat_mean, stat_var)
    stats = jnp.where(slot == 2, -inv_sum * back_sum, stats)
    stats = jnp.where(slot == 3, -0.5 * inv_sum * inv_sum * back_cross, stats)
    r["stats"][...] = stats

    def join(p, carry):
        rows = pl.ds(pl.multiple_of(p * span, span), span)
        final = docs_ref[pl.ds(p, 1)][:, span - 1 : span]
        share = (r["dcol"][rows] == final).astype(f32)
        sums_row = r["dsum"][pl.ds(p, 1)]
        for j in range(pairs):
            at = slice(128 * j, 128 * j + 128)
            past = slice(width + 128 * j, width + 128 * j + 128)
            full = probs[rows, at] + share * sums_row[:, at]
            mixed[rows, past] = full.astype(bf16)
            full = probs[rows, past] + share * sums_row[:, past]
            mixed[rows, 2 * width + 128 * j : 2 * width + 128 * j + 128] = full.astype(bf16)
        return carry

    lax.fori_loop(0, spans, join, 0)
    down.mine_done()

    put(k_sum, dot_nn(r["act1T"][...], mixed[:, width : 2 * width]).astype(bf16), pl.ds(0, width))
    k_sum.start()
    put(v_sum, dot_nn(r["act1T"][...], mixed[:, 2 * width :]).astype(bf16), pl.ds(0, width))
    v_sum.start()
    q_sum.sides_done()
    out.mine_done()

    def first_back(i):
        rows = pl.ds(pl.multiple_of(i, chunk), chunk)
        d_one = dot_nt(r["act2"][rows], w_query[...])
        d_one = d_one + dot_nt(mixed[rows, width : 3 * width], w_past[...])
        values = x_ref[rows].astype(f32)
        inv = r["inv1"][rows][:, 0:1]
        normal = (values - jnp.mean(values, -1, keepdims=True)) * inv
        r["ngrad"][0] += fold_rows(d_one * normal)
        r["ngrad"][1] += fold_rows(d_one)
        scaled = d_one * r["nrows"][0:1]
        centred = (
            scaled
            - jnp.mean(scaled, -1, keepdims=True)
            - normal * jnp.mean(scaled * normal, -1, keepdims=True)
        )
        r["input_grad"][rows] = D[rows] + inv * centred

    half_chunks = chunks // 2
    lax.fori_loop(0, half_chunks, lambda i, c: (first_back(i * chunk), c)[1], 0)
    k_sum.core_done()
    v_sum.core_done()
    lax.fori_loop(half_chunks, chunks, lambda i, c: (first_back(i * chunk), c)[1], 0)

    pieces = jnp.concatenate(
        [jnp.sum(r["ngrad"][k], 0, keepdims=True) for k in range(4)]
        + [jnp.zeros((12, width), f32)],
        0,
    )
    spread_rows = jnp.broadcast_to(pieces[None], (devices, 16, width)).reshape(16 * devices, width)
    spread_rows = jnp.where(owner_row == owner_col, spread_rows, 0.0).astype(bf16)
    norm = scatters["norm"]
    narrow = dot_nt(spread_rows, pick).astype(bf16)
    put(norm, jnp.concatenate([narrow, jnp.zeros_like(narrow)], 1), pl.ds(0, 256))
    norm.start()

    def output(i):
        rows = pl.ds(pl.multiple_of(i, chunk), chunk)
        result = F[rows] + dot_nn(r["act3"][rows], w_down[...])
        r["block_out"][rows] = result.astype(bf16)

    lax.fori_loop(0, half_chunks, lambda i, c: (output(i * chunk), c)[1], 0)
    norm.core_done()
    k_sum.sides_done()
    v_sum.sides_done()
    q_sum.mine_done()
    lax.fori_loop(half_chunks, chunks, lambda i, c: (output(i * chunk), c)[1], 0)
    norm.sides_done()
    k_sum.mine_done()
    v_sum.mine_done()
    for copy in loads:
        copy.wait()
    for g in range(4):
        ups[g].done(update("up", g * quad))
    for name in ("down", "out"):
        scatters[name].done(update(name, 0))
    norm.mine_done()
    q_sum.done(update("qkv", 0))
    k_sum.done(update("qkv", width))
    v_sum.done(update("qkv", 2 * width))
    norm.done(update_norm)
    for part in list(gathers.values()) + list(scatters.values()) + [first, second]:
        part.drain()


def fused_layer(chain, rate, tokens, grad, doc_ids, shards, moments, averages):
    f32, bf16 = jnp.float32, jnp.bfloat16
    rows, width = tokens.shape
    spans = rows // SPAN
    order = ORDER
    devices = 8 * chain
    ins = [("tokens", tokens), ("grad", grad), ("doc_ids", doc_ids)]
    ins += [("s_" + name, shards[name]) for name in order]
    ins += [("m_" + name, moments[name]) for name in order]
    ins += [("a_" + name, averages[name]) for name in order]
    outs = [
        ("block_out", pltpu.VMEM((rows, width), bf16)),
        ("input_grad", pltpu.VMEM((rows, width), f32)),
        ("stats", pltpu.VMEM((8, 128), f32)),
    ]
    outs += [("t_" + name, pltpu.VMEM((3,) + shards[name].shape, f32)) for name in order]
    hidden = shards["up"].shape[1]
    scratch = {}
    down_rows = shards["down"].shape[0]
    scratch["w_first"] = pltpu.VMEM((devices * 16, 2 * width + 128), bf16)
    scratch["w_query"] = pltpu.VMEM((devices * 16, width), bf16)
    scratch["w_mid"] = pltpu.VMEM((devices * 16, width + hidden), bf16)
    scratch["w_down"] = pltpu.VMEM((devices * down_rows, width), bf16)
    for name, piece, cols in SUMS:
        for i, buf in enumerate(scatter_scratch(chain, piece, cols, name == "down")):
            scratch[f"c_{name}{i}"] = buf
    for name in order:
        scratch["vm_" + name] = pltpu.VMEM(shards[name].shape, f32)
        scratch["va_" + name] = pltpu.VMEM(shards[name].shape, f32)
    scratch["lsem"] = DMA((10,))
    payload = (8, spans, 2 * width + 128)
    pairs = width // 128
    scratch |= {
        "gsend": DMA((4, GATHER_SEMS)),
        "grecv": DMA((4, GATHER_SEMS)),
        "csend": DMA((10, SCATTER_SEMS)),
        "crecv": DMA((10, SCATTER_SEMS)),
        "esend": DMA((2, 7)),
        "erecv": DMA((2, 7)),
        "summ": pltpu.VMEM(payload, f32),
        "back": pltpu.VMEM(payload, f32),
        "sendback": pltpu.VMEM(payload, f32),
        "F": pltpu.VMEM((rows, width), f32),
        "inv1": pltpu.VMEM((rows, 128), f32),
        "dcol": pltpu.VMEM((rows, 128), f32),
        "nrows": pltpu.VMEM((16, width), f32),
        "ngrad": pltpu.VMEM((4, 8, width), f32),
        "act1T": pltpu.VMEM((width, rows), bf16),
        "dyT": pltpu.VMEM((width, rows), bf16),
        "act2T": pltpu.VMEM((width, rows), bf16),
        "headsT": pltpu.VMEM((width, rows), bf16),
        "mixed": pltpu.VMEM((rows, 3 * width), bf16),
        "probs": pltpu.VMEM((rows, 384 * pairs), f32),
        "heads": pltpu.VMEM((rows, width), bf16),
        "knorm": pltpu.VMEM((8 * spans, width), f32),
        "KR": pltpu.VMEM((pairs, 128, 128), bf16),
        "VR": pltpu.VMEM((pairs, 128, 128), bf16),
        "lastrow": pltpu.VMEM((8, 128), f32),
        "docs": pltpu.VMEM((spans, SPAN), f32),
        "npad": pltpu.VMEM((16, 128), f32),
        "inv2": pltpu.VMEM((rows, 128), f32),
        "act2": pltpu.VMEM((rows, width), bf16),
        "act3": pltpu.VMEM((rows, hidden), bf16),
        "dhid": pltpu.VMEM((rows, hidden), bf16),
        "dafter": pltpu.VMEM((rows, width), bf16),
        "D": pltpu.VMEM((rows, width), f32),
        "dsum": pltpu.VMEM((spans, 2 * width), f32),
    }
    names = [n for n, _ in ins] + [n for n, _ in outs] + list(scratch)
    vmem = pl.BlockSpec(memory_space=pltpu.VMEM)
    result = pl.pallas_call(
        functools.partial(layer_kernel, chain, rate, names),
        out_shape=[shape for _, shape in outs],
        in_specs=[vmem] * (len(ins) - 10) + [pl.BlockSpec(memory_space=pltpu.HBM)] * 10,
        out_specs=[vmem] * len(outs),
        scratch_shapes=list(scratch.values()),
        compiler_params=pltpu.CompilerParams(
            collective_id=0, has_side_effects=True, vmem_limit_bytes=59 * 2**20
        ),
    )(*[value for _, value in ins])
    return dict(zip([n for n, _ in outs], result))


def finish_kernel(count, *refs):
    ins, outs, sems = refs[:count], refs[count:-1], refs[-1]
    stats, two = ins[-1], outs[count - 1 :]
    copies = [pltpu.make_async_copy(ins[k], outs[k], sems.at[k]) for k in range(count - 1)]
    for copy in copies:
        copy.start()
    two[0][...] = stats[0:1, 0:2]
    two[1][...] = stats[0:1, 2:4]
    for copy in copies:
        copy.wait()


def finish(arrays, stats):
    vmem = pl.BlockSpec(memory_space=pltpu.VMEM)
    two = jax.ShapeDtypeStruct((1, 2), jnp.float32)
    count = len(arrays) + 1
    return pl.pallas_call(
        functools.partial(finish_kernel, count),
        out_shape=[jax.ShapeDtypeStruct(a.shape, a.dtype) for a in arrays] + [two, two],
        in_specs=[pl.BlockSpec(memory_space=pl.ANY)] * (count - 1) + [vmem],
        out_specs=[pl.BlockSpec(memory_space=pltpu.HBM)] * (count - 1) + [vmem] * 2,
        scratch_shapes=[DMA((count - 1,))],
        compiler_params=pltpu.CompilerParams(vmem_limit_bytes=2 * 2**20),
    )(*(pltpu.with_memory_space_constraint(a, pltpu.VMEM) for a in arrays), stats)


def norm_forward(values, gain_row, shift_row):
    centre = values - jnp.mean(values, -1, keepdims=True)
    spread = jnp.mean(centre * centre, -1, keepdims=True)
    inv_std = lax.rsqrt(spread + 1e-05)
    normal = centre * inv_std
    return (normal * gain_row + shift_row, normal, inv_std)


def norm_backward(grad_in, normal, inv_std, gain_row):
    scaled = grad_in * gain_row
    centred = (
        scaled
        - jnp.mean(scaled, -1, keepdims=True)
        - normal * jnp.mean(scaled * normal, -1, keepdims=True)
    )
    return (inv_std * centred, jnp.sum(grad_in * normal, 0), jnp.sum(grad_in, 0))


def gelu_tanh(values):
    return jax.nn.gelu(values, approximate=True)


def span_probs(query_blk, key_blk, key_remote, doc_span, last_remote, span_first):
    span_len = doc_span.shape[2]
    local = (
        jnp.einsum("bpqhe,bpkhe->bphqk", query_blk, key_blk, preferred_element_type=jnp.float32)
        * 0.125
    )
    remote = (
        jnp.einsum("bpqhe,bnhe->bphqn", query_blk, key_remote, preferred_element_type=jnp.float32)
        * 0.125
    )
    positions = jnp.arange(span_len)
    causal = positions[:, None] >= positions[None, :]
    same_doc = doc_span[:, :, :, None] == doc_span[:, :, None, :]
    mask_local = (same_doc & causal[None, None])[:, :, None]
    span_ids = span_first + jnp.arange(doc_span.shape[1])
    earlier = jnp.arange(key_remote.shape[1])[None, :] < span_ids[:, None]
    doc_float = doc_span.astype(jnp.float32)
    match = doc_float[:, :, :, None] == last_remote.astype(jnp.float32)[:, None, None, :]
    mask_remote = (match & earlier[None, :, None, :])[:, :, None]
    allowed = jnp.concatenate([mask_local, mask_remote], -1)
    scores = jnp.where(allowed, jnp.concatenate([local, remote], -1), -1e30)
    peak_score = jnp.max(scores, -1, keepdims=True)
    raised = jnp.exp(scores - peak_score)
    return raised / jnp.sum(raised, -1, keepdims=True)


def advance(weight, moment, average, grad, rate):
    new_moment = 0.9 * moment + rate * grad
    new_weight = weight - (rate * grad + 0.9 * new_moment)
    new_average = 0.99 * average + 0.01 * new_weight
    return jnp.stack([new_weight, new_moment, new_average])


def shards_plain(
    tokens,
    grad_out,
    doc_ids,
    qkv_w,
    qkv_m,
    qkv_a,
    out_w,
    out_m,
    out_a,
    up_w,
    up_m,
    up_a,
    down_w,
    down_m,
    down_a,
    norm_w,
    norm_m,
    norm_a,
):
    seqs, seq_len, width = tokens.shape
    span_len = SPAN
    cycle_size = lax.axis_size("seq")
    cycle_rank = lax.axis_index("seq")
    spans_dev = seq_len // span_len
    spans_all = spans_dev * cycle_size
    rows_dev = seqs * seq_len
    head_size = width // H
    bf16 = jnp.bfloat16
    f32 = jnp.float32
    w_qkv, w_out, w_up, w_down, norm_low = (
        lax.all_gather(qkv_w.astype(bf16), ("seq", "dp"), axis=0, tiled=True),
        lax.all_gather(out_w.astype(bf16), ("seq", "dp"), axis=0, tiled=True),
        lax.all_gather(up_w.astype(bf16), ("seq", "dp"), axis=0, tiled=True),
        lax.all_gather(down_w.astype(bf16), ("seq", "dp"), axis=0, tiled=True),
        lax.all_gather(norm_w.astype(bf16), ("seq", "dp"), axis=1, tiled=True),
    )
    norm_rows = norm_low.astype(f32)
    inputs = tokens.reshape(rows_dev, width).astype(f32)
    normed_one, normal_one, inv_one = norm_forward(inputs, norm_rows[0], norm_rows[1])
    act_one = normed_one.astype(bf16)
    mixed = jnp.dot(act_one, w_qkv, preferred_element_type=f32)
    query = mixed[:, :width].astype(bf16)
    key_all = mixed[:, width : 2 * width].astype(bf16)
    value_all = mixed[:, 2 * width :].astype(bf16)
    block_shape = (seqs, spans_dev, span_len, H, head_size)
    query_blk = query.reshape(block_shape)
    key_blk = key_all.reshape(block_shape)
    value_blk = value_all.reshape(block_shape)
    doc_span = doc_ids.reshape(seqs, spans_dev, span_len)
    last_doc = doc_span[:, :, -1]
    member = (doc_span == last_doc[:, :, None]).astype(f32)
    counts = jnp.sum(member, -1)
    member_low = member.astype(bf16)
    key_four = key_all.reshape(seqs, spans_dev, span_len, width)
    value_four = value_all.reshape(seqs, spans_dev, span_len, width)
    sum_key = (
        jnp.einsum("bpt,bptd->bpd", member_low, key_four, preferred_element_type=f32)
        / counts[..., None]
    )
    sum_value = (
        jnp.einsum("bpt,bptd->bpd", member_low, value_four, preferred_element_type=f32)
        / counts[..., None]
    )
    total_sum, total_square = lax.psum(
        (jnp.sum(sum_key, (1, 2)), jnp.sum(sum_key * sum_key, (1, 2))), "seq"
    )
    entries = spans_all * width
    stat_mean = total_sum / entries
    stat_var = total_square / entries - stat_mean * stat_mean
    inv_sum = lax.rsqrt(stat_var + 1e-05)
    key_norm = (sum_key - stat_mean[:, None, None]) * inv_sum[:, None, None]
    key_send = key_norm.astype(bf16)
    value_send = sum_value.astype(bf16)
    last_send = last_doc.astype(bf16)
    key_remote, value_remote, last_remote = (
        lax.all_gather(key_send, "seq", axis=1, tiled=True),
        lax.all_gather(value_send, "seq", axis=1, tiled=True),
        lax.all_gather(last_send, "seq", axis=1, tiled=True),
    )
    remote_shape = (seqs, spans_all, H, head_size)
    span_first = cycle_rank * spans_dev
    probs = span_probs(
        query_blk, key_blk, key_remote.reshape(remote_shape), doc_span, last_remote, span_first
    )
    probs_low = probs.astype(bf16)
    attended = jnp.einsum(
        "bphqk,bpkhe->bpqhe", probs_low[..., :span_len], value_blk, preferred_element_type=f32
    )
    attended = attended + jnp.einsum(
        "bphqn,bnhe->bpqhe",
        probs_low[..., span_len:],
        value_remote.reshape(remote_shape),
        preferred_element_type=f32,
    )
    heads_out = attended.reshape(rows_dev, width).astype(bf16)
    after_attn = inputs + jnp.dot(heads_out, w_out, preferred_element_type=f32)
    normed_two, normal_two, inv_two = norm_forward(after_attn, norm_rows[2], norm_rows[3])
    act_two = normed_two.astype(bf16)
    hidden = jnp.dot(act_two, w_up, preferred_element_type=f32)
    act_three = gelu_tanh(hidden).astype(bf16)
    result = after_attn + jnp.dot(act_three, w_down, preferred_element_type=f32)
    block_out = result.astype(bf16).reshape(seqs, seq_len, width)
    stats_out = jnp.stack([stat_mean, stat_var], -1)
    grad_low = grad_out.reshape(rows_dev, width)
    grad_down = jnp.einsum("tf,td->fd", act_three, grad_low, preferred_element_type=f32)
    d_three = jnp.einsum("td,fd->tf", grad_low, w_down, preferred_element_type=f32)
    unused_out, gelu_pull = jax.vjp(gelu_tanh, hidden)
    d_hidden = gelu_pull(d_three)[0].astype(bf16)
    grad_up = jnp.einsum("td,tf->df", act_two, d_hidden, preferred_element_type=f32)
    d_two = jnp.einsum("tf,df->td", d_hidden, w_up, preferred_element_type=f32)
    d_norm_two, gain_two, shift_two = norm_backward(d_two, normal_two, inv_two, norm_rows[2])
    d_after = grad_low.astype(f32) + d_norm_two
    d_after_low = d_after.astype(bf16)
    grad_outw = jnp.einsum("tc,td->cd", heads_out, d_after_low, preferred_element_type=f32)
    d_heads = jnp.einsum("td,cd->tc", d_after_low, w_out, preferred_element_type=f32).astype(bf16)
    key_back, value_back, last_back = (key_remote, value_remote, last_remote)
    key_back_blk = key_back.reshape(remote_shape)
    value_back_blk = value_back.reshape(remote_shape)
    probs_back = span_probs(query_blk, key_blk, key_back_blk, doc_span, last_back, span_first)
    probs_back_low = probs_back.astype(bf16)
    d_heads_blk = d_heads.reshape(block_shape)
    d_probs = jnp.concatenate(
        [
            jnp.einsum("bpqhe,bpkhe->bphqk", d_heads_blk, value_blk, preferred_element_type=f32),
            jnp.einsum(
                "bpqhe,bnhe->bphqn", d_heads_blk, value_back_blk, preferred_element_type=f32
            ),
        ],
        -1,
    )
    row_dot = jnp.sum(probs_back * d_probs, -1, keepdims=True)
    d_scores = (probs_back * (d_probs - row_dot)).astype(bf16)
    d_local = d_scores[..., :span_len]
    d_remote = d_scores[..., span_len:]
    d_query = 0.125 * (
        jnp.einsum("bphqk,bpkhe->bpqhe", d_local, key_blk, preferred_element_type=f32)
        + jnp.einsum("bphqn,bnhe->bpqhe", d_remote, key_back_blk, preferred_element_type=f32)
    )
    d_key = 0.125 * jnp.einsum("bphqk,bpqhe->bpkhe", d_local, query_blk, preferred_element_type=f32)
    d_value = jnp.einsum(
        "bphqk,bpqhe->bpkhe",
        probs_back_low[..., :span_len],
        d_heads_blk,
        preferred_element_type=f32,
    )
    d_key_sum = (
        0.125 * jnp.einsum("bphqn,bpqhe->bnhe", d_remote, query_blk, preferred_element_type=f32)
    ).reshape(seqs, spans_all, width)
    d_value_sum = jnp.einsum(
        "bphqn,bpqhe->bnhe", probs_back_low[..., span_len:], d_heads_blk, preferred_element_type=f32
    ).reshape(seqs, spans_all, width)
    owned_key, owned_value = (
        lax.psum_scatter(
            d_key_sum.astype(jnp.bfloat16), "seq", scatter_dimension=1, tiled=True
        ).astype(jnp.float32),
        lax.psum_scatter(
            d_value_sum.astype(jnp.bfloat16), "seq", scatter_dimension=1, tiled=True
        ).astype(jnp.float32),
    )
    back_sum, back_cross = lax.psum(
        (jnp.sum(owned_key, (1, 2)), jnp.sum(owned_key * key_norm, (1, 2))), "seq"
    )
    stat_grads = jnp.stack([-inv_sum * back_sum, -0.5 * inv_sum * inv_sum * back_cross], -1)
    d_sum_key = inv_sum[:, None, None] * (
        owned_key
        - back_sum[:, None, None] / entries
        - key_norm * back_cross[:, None, None] / entries
    )
    share = member / counts[..., None]
    d_key_all = (
        d_key.reshape(seqs, spans_dev, span_len, width)
        + share[..., None] * d_sum_key[:, :, None, :]
    )
    d_value_all = (
        d_value.reshape(seqs, spans_dev, span_len, width)
        + share[..., None] * owned_value[:, :, None, :]
    )
    d_mixed = jnp.concatenate(
        [
            d_query.reshape(rows_dev, width),
            d_key_all.reshape(rows_dev, width),
            d_value_all.reshape(rows_dev, width),
        ],
        -1,
    ).astype(bf16)
    grad_qkv = jnp.einsum("td,tf->df", act_one, d_mixed, preferred_element_type=f32)
    d_one = jnp.einsum("tf,df->td", d_mixed, w_qkv, preferred_element_type=f32)
    d_norm_one, gain_one, shift_one = norm_backward(d_one, normal_one, inv_one, norm_rows[0])
    input_grad = (d_after + d_norm_one).reshape(seqs, seq_len, width)
    grad_norm = jnp.stack([gain_one, shift_one, gain_two, shift_two])
    sum_qkv, sum_outw, sum_up, sum_down, sum_norm = (
        lax.psum_scatter(grad_qkv, ("seq", "dp"), scatter_dimension=0, tiled=True),
        lax.psum_scatter(grad_outw, ("seq", "dp"), scatter_dimension=0, tiled=True),
        lax.psum_scatter(grad_up, ("seq", "dp"), scatter_dimension=0, tiled=True),
        lax.psum_scatter(grad_down, ("seq", "dp"), scatter_dimension=0, tiled=True),
        lax.psum_scatter(grad_norm, ("seq", "dp"), scatter_dimension=1, tiled=True),
    )
    tokens_all = rows_dev * cycle_size * lax.axis_size("dp")
    rate = 0.02 / math.sqrt(tokens_all)
    return (
        block_out,
        input_grad,
        stats_out,
        stat_grads,
        advance(qkv_w, qkv_m, qkv_a, sum_qkv, rate),
        advance(out_w, out_m, out_a, sum_outw, rate),
        advance(up_w, up_m, up_a, sum_up, rate),
        advance(down_w, down_m, down_a, sum_down, rate),
        advance(norm_w, norm_m, norm_a, sum_norm, rate),
    )


def shards(*args):
    tokens, grad_out, doc_ids = args[:3]
    qkv_w = args[3]
    seqs, seq_len, width = tokens.shape
    fits = lax.axis_size("seq") == 8 and qkv_w.shape[0] % 16 == 0
    fits = fits and seqs == 1 and seq_len == 8 * SPAN and width == 512
    if not fits:
        return shards_plain(*args)
    chain = lax.axis_size("dp")
    names = {"qkv": 3, "out": 6, "up": 9, "down": 12, "norm": 15}
    done = fused_layer(
        chain,
        0.02 / math.sqrt(seq_len * 8 * chain),
        tokens.reshape(seq_len, width),
        grad_out.reshape(seq_len, width),
        doc_ids,
        *({name: args[k + j] for name, k in names.items()} for j in range(3)),
    )
    order = ["block_out", "input_grad"] + ["t_" + name for name in names]
    result = finish([done[name] for name in order], done["stats"])
    return (
        result[0].reshape(tokens.shape),
        result[1].reshape(tokens.shape),
        *result[7:],
        *result[2:7],
    )


def solution(mesh):
    placed = (
        P("dp", "seq", None),
        P("dp", "seq", None),
        P("dp", "seq"),
        P(("seq", "dp"), None),
        P(("seq", "dp"), None),
        P(("seq", "dp"), None),
        P(("seq", "dp"), None),
        P(("seq", "dp"), None),
        P(("seq", "dp"), None),
        P(("seq", "dp"), None),
        P(("seq", "dp"), None),
        P(("seq", "dp"), None),
        P(("seq", "dp"), None),
        P(("seq", "dp"), None),
        P(("seq", "dp"), None),
        P(None, ("seq", "dp")),
        P(None, ("seq", "dp")),
        P(None, ("seq", "dp")),
    )
    return jax.shard_map(
        shards,
        mesh=mesh,
        in_specs=placed,
        out_specs=(
            P("dp", "seq", None),
            P("dp", "seq", None),
            P("dp", None),
            P("dp", None),
            P(None, ("seq", "dp"), None),
            P(None, ("seq", "dp"), None),
            P(None, ("seq", "dp"), None),
            P(None, ("seq", "dp"), None),
            P(None, None, ("seq", "dp")),
        ),
        check_vma=False,
    )
```

```python
import functools
import math

import jax
import jax.numpy as jnp
from jax import lax
from jax.experimental import pallas as pl
from jax.experimental.pallas import tpu as pltpu
from jax.sharding import PartitionSpec as P

H = 8
SPAN = 128
MESH = pl.DeviceIdType.MESH
DMA = pltpu.SemaphoreType.DMA


class Place:
    def __init__(self, chain):
        self.chain = chain
        self.s = lax.axis_index("seq")
        self.z = lax.axis_index("dp")
        self.core = lax.rem(self.s, 2)
        self.group = lax.div(self.s, 2)
        self.sib = self.flip(self.s, 1)
        self.xs = self.flip(self.s, 2)
        self.ys = self.flip(self.s, 4)
        self.ds = self.flip(self.xs, 4)

    @staticmethod
    def flip(value, bit):
        return value + bit - 2 * bit * lax.rem(lax.div(value, bit), 2)

    def dev(self, s, z=None):
        return {"seq": s, "dp": self.z if z is None else z}

    def zflip(self, bits):
        z = self.z
        for bit in (1, 2):
            if bits & bit:
                z = self.flip(z, bit)
        return z

    def zpeer(self, step):
        return lax.rem(self.z + step, self.chain)

    def barrier(self, extra=()):
        sem = pltpu.get_barrier_semaphore()
        peers = [self.dev(self.sib), self.dev(self.xs), self.dev(self.ys)]
        peers += [self.dev(self.s, self.zpeer(k)) for k in range(1, self.chain)]
        peers += list(extra)
        for peer in peers:
            pl.semaphore_signal(sem, inc=1, device_id=peer, device_id_type=MESH)
        pl.semaphore_wait(sem, len(peers))


def remote(src, dst, send, recv, peer):
    return pltpu.make_async_remote_copy(
        src_ref=src, dst_ref=dst, send_sem=send, recv_sem=recv, device_id=peer, device_id_type=MESH
    )


class Gather:
    def __init__(self, place, full, rows, send, recv):
        self.p, self.full, self.rows = place, full, rows
        self.send, self.recv = send, recv
        self.gr = place.chain * rows
        self.sent = []

    def region(self, s):
        return self.full.at[pl.ds(pl.multiple_of(s * self.gr, self.gr), self.gr)]

    def piece(self, s, z):
        start = pl.multiple_of(s * self.gr + z * self.rows, self.rows)
        return self.full.at[pl.ds(start, self.rows)]

    def go(self, k, ref, peer):
        copy = remote(ref, ref, self.send.at[k], self.recv.at[k], peer)
        copy.start()
        self.sent.append(copy)

    def got(self, k, ref):
        remote(ref, ref, self.send.at[k], self.recv.at[k], self.p.dev(self.p.sib)).wait_recv()

    def sides(self, k):
        p = self.p
        piece = self.piece(p.s, p.zflip(k))
        self.go(3 + k, piece, p.dev(p.xs))
        self.go(7 + k, piece, p.dev(p.ys))

    def start(self):
        p = self.p
        for k in range(1, p.chain):
            self.go(k - 1, self.piece(p.s, p.z), p.dev(p.s, p.zflip(k)))

    def chain_piece(self, k):
        p = self.p
        if 0 < k < p.chain:
            self.got(k - 1, self.piece(p.s, p.zflip(k)))
            self.sides(k)
        if k == 3:
            self.go(19, self.region(p.s), p.dev(p.sib))

    def chain_done(self):
        for k in range(1, 4):
            self.chain_piece(k)

    def sides_done(self, part=(0, 1)):
        p = self.p
        middle = (p.chain + 1) // 2
        steps = [range(middle), range(middle, p.chain)]
        for k in [k for one in part for k in steps[one]]:
            self.got(3 + k, self.piece(p.xs, p.zflip(k)))
            if k < middle:
                self.go(11 + k, self.piece(p.xs, p.zflip(k)), p.dev(p.ys))
            self.got(7 + k, self.piece(p.ys, p.zflip(k)))
            if k >= middle:
                self.go(11 + k, self.piece(p.ys, p.zflip(k)), p.dev(p.xs))
        if part[-1] == 1:
            self.go(20, self.region(p.xs), p.dev(p.sib))
            self.go(21, self.region(p.ys), p.dev(p.sib))

    def corner_done(self):
        p = self.p
        for k in range(p.chain):
            self.got(11 + k, self.piece(p.ds, p.zflip(k)))
        self.go(22, self.region(p.ds), p.dev(p.sib))

    def done(self):
        p = self.p
        for k, s in ((19, p.s), (20, p.xs), (21, p.ys), (22, p.ds)):
            self.got(k, self.region(p.flip(s, 1)))

    def drain(self):
        for copy in self.sent:
            copy.wait_send()


GATHER_SEMS = 23


def by_rows(count, step, body):
    def trip(i, carry):
        body(pl.multiple_of(i * step, step))
        return carry

    lax.fori_loop(0, count // step, trip, 0)


class Scatter:
    def __init__(self, place, rows, flip, bufs, send, recv):
        self.p, self.rows, self.turned = place, rows, flip
        self.full, self.in2, self.stage, self.land, self.mine, self.zout, self.zin = bufs
        self.gr, self.cols = self.full.shape[2], self.full.shape[3]
        self.half = self.cols // 2
        self.step = 16
        self.send, self.recv = send, recv
        self.sent = []

    def go(self, k, src, dst, peer):
        copy = remote(src, dst, self.send.at[k], self.recv.at[k], peer)
        copy.start()
        self.sent.append(copy)

    def got(self, k, ref):
        remote(ref, ref, self.send.at[k], self.recv.at[k], self.p.dev(self.p.sib)).wait_recv()

    def near(self, bits):
        g = self.p.group
        for bit in (1, 2):
            if bits & bit:
                g = Place.flip(g, bit)
        return g

    def cut(self, ref, slot, which):
        return ref.at[slot, :, pl.ds(which * self.half, self.half)]

    def both(self, g, rows, cols):
        mine = self.full[g, self.p.core, rows, cols].astype(jnp.float32)
        return mine + self.in2[g, rows, cols].astype(jnp.float32)

    def start(self):
        self.go(0, self.full.at[:, 1 - self.p.core], self.in2, self.p.dev(self.p.sib))

    def start_group(self, g):
        self.go(10 + g, self.full.at[g, 1 - self.p.core], self.in2.at[g], self.p.dev(self.p.sib))

    def core_done(self):
        self.core_far()
        self.core_near()

    def core_far(self):
        p, step = self.p, self.step
        if self.turned:
            for g in range(4):
                self.got(10 + g, self.in2.at[g])
        else:
            self.got(0, self.in2)
        far = self.near(3)
        whole = pl.ds(0, self.cols)

        def sum_far(i):
            rows = pl.ds(i, step)
            self.stage[0, rows] = self.both(far, rows, whole).astype(jnp.bfloat16)

        by_rows(self.gr, step, sum_far)
        self.go(1, self.cut(self.stage, 0, 0), self.cut(self.land, 0, 0), p.dev(p.xs))
        self.go(2, self.cut(self.stage, 0, 1), self.cut(self.land, 0, 1), p.dev(p.ys))

    def core_near(self):
        p, step = self.p, self.step
        xg, yg = self.near(1), self.near(2)
        first, second = pl.ds(0, self.half), pl.ds(self.half, self.half)

        def sum_sides(i):
            rows = pl.ds(i, step)
            self.stage[1, rows, first] = self.both(xg, rows, first).astype(jnp.bfloat16)
            self.stage[2, rows, second] = self.both(yg, rows, second).astype(jnp.bfloat16)

        by_rows(self.gr, step, sum_sides)
        self.go(3, self.cut(self.stage, 1, 0), self.cut(self.land, 1, 0), p.dev(p.xs))
        self.go(4, self.cut(self.stage, 2, 1), self.cut(self.land, 2, 1), p.dev(p.ys))

    def sides_done(self):
        p, step = self.p, self.step
        for k, slot, which, bits, peer in ((5, 2, 0, 2, p.ys), (6, 1, 1, 1, p.xs)):
            self.got(k - 4, self.cut(self.land, 0, which))
            cols = pl.ds(which * self.half, self.half)
            g = self.near(bits)

            def add(i, slot=slot, cols=cols, g=g):
                rows = pl.ds(i, step)
                total = self.both(g, rows, cols) + self.land[0, rows, cols].astype(jnp.float32)
                self.stage[slot, rows, cols] = total.astype(jnp.bfloat16)

            by_rows(self.gr, step, add)
            self.go(k, self.cut(self.stage, slot, which), self.cut(self.land, slot, which), p.dev(peer))

    def mine_done(self):
        p, step = self.p, self.step
        me = p.group
        for k, slot, which in ((3, 1, 0), (4, 2, 1), (5, 2, 0), (6, 1, 1)):
            self.got(k, self.cut(self.land, slot, which))

        def total(rows, cols):
            sides = self.land[1, rows, cols].astype(jnp.float32)
            sides = sides + self.land[2, rows, cols].astype(jnp.float32)
            return self.both(me, rows, cols) + sides

        if self.turned:

            def turn(i):
                cols = pl.ds(pl.multiple_of(i, 128), 128)
                value = total(pl.ds(0, self.gr), cols).T
                self.mine[cols] = value
                self.zout[cols] = value.astype(jnp.bfloat16)

            by_rows(self.cols, 128, turn)
        else:

            def add(i):
                rows = pl.ds(i, step)
                value = total(rows, pl.ds(0, self.cols))
                self.mine[rows] = value
                self.zout[rows] = value.astype(jnp.bfloat16)

            by_rows(self.gr, step, add)
        for k in range(1, p.chain):
            z = p.zpeer(k)
            src = self.zout.at[pl.ds(pl.multiple_of(z * self.rows, self.rows), self.rows)]
            dst = self.zin.at[pl.ds((k - 1) * self.rows, self.rows)]
            self.go(6 + k, src, dst, p.dev(p.s, z))

    def done(self, result):
        p, step = self.p, self.step
        for k in range(1, p.chain):
            self.got(6 + k, self.zin.at[pl.ds((k - 1) * self.rows, self.rows)])
        start = p.z * self.rows

        def add(i):
            value = self.mine[pl.ds(pl.multiple_of(start + i, step), step)]
            for k in range(1, p.chain):
                value = value + self.zin[pl.ds((k - 1) * self.rows + i, step)].astype(jnp.float32)
            result(i, value)

        by_rows(self.rows, step, add)

    def drain(self):
        for copy in self.sent:
            copy.wait_send()


SCATTER_SEMS = 14


def scatter_scratch(chain, rows, cols, flip):
    f32, bf16 = jnp.float32, jnp.bfloat16
    gr = chain * rows
    block = (cols, gr) if flip else (gr, cols)
    return [
        pltpu.VMEM((4, 2) + block, bf16),
        pltpu.VMEM((4,) + block, bf16),
        pltpu.VMEM((3,) + block, bf16),
        pltpu.VMEM((3,) + block, bf16),
        pltpu.VMEM((gr, cols), f32),
        pltpu.VMEM((gr, cols), bf16),
        pltpu.VMEM((max(1, chain - 1) * rows, cols), bf16),
    ]


class Exchange:
    def __init__(self, place, land, send, recv):
        self.p, self.land, self.send, self.recv = place, land, send, recv
        self.sent = []

    def go(self, source):
        p = self.p
        for d in range(1, 8):
            peer = lax.rem(p.s + d, 8)
            copy = remote(
                source(peer), self.land.at[p.s], self.send.at[d - 1], self.recv.at[d - 1], p.dev(peer)
            )
            copy.start()
            self.sent.append(copy)

    def wait(self):
        p = self.p
        for d in range(1, 8):
            ref = self.land.at[lax.rem(p.s + 8 - d, 8)]
            remote(ref, ref, self.send.at[d - 1], self.recv.at[d - 1], p.dev(p.sib)).wait_recv()

    def drain(self):
        for copy in self.sent:
            copy.wait_send()


def dot_nn(a, b):
    return lax.dot_general(a, b, (((1,), (0,)), ((), ())), preferred_element_type=jnp.float32)


def dot_nt(a, b):
    return lax.dot_general(a, b, (((1,), (1,)), ((), ())), preferred_element_type=jnp.float32)


def dot_tn(a, b):
    return lax.dot_general(a, b, (((0,), (0,)), ((), ())), preferred_element_type=jnp.float32)


def total_of(values):
    return jnp.sum(jnp.sum(values, 1, keepdims=True), 0, keepdims=True)


def fold_rows(values):
    rows, cols = values.shape
    return jnp.sum(values.reshape(rows // 8, 8, cols), 0)


NEG = -1e30
ORDER = ("norm", "qkv", "out", "up", "down")
SUMS = (("norm", 16, 256), ("q", 16, 512), ("k", 16, 512), ("v", 16, 512), ("out", 16, 512), ("up0", 16, 512), ("up1", 16, 512), ("up2", 16, 512), ("up3", 16, 512), ("down", 64, 512))
LEFT = math.sqrt(2.0 / math.pi)
CUBE = 0.044715


def layer_kernel(chain, rate, names, *refs):
    r = dict(zip(names, refs))
    f32, bf16 = jnp.float32, jnp.bfloat16
    place = Place(chain)
    x_ref, dy_ref, docs_ref = r["tokens"], r["grad"], r["docs"]
    rows_all, width = x_ref.shape
    span, spans = SPAN, rows_all // SPAN
    pairs = width // 128
    hidden_size = r["s_up"].shape[1]
    devices = 8 * chain
    per = width // devices
    entries = 8 * spans * width
    chunk = 256
    chunks = rows_all // chunk

    gathers = {}
    r["npad"][...] = jnp.zeros_like(r["npad"])
    r["npad"][0:4, 0:per] = r["s_norm"][...]
    past_cols, mid_cols = 2 * width, width
    w_past = r["w_first"].at[:, 0:past_cols]
    w_norm = r["w_first"].at[:, past_cols : past_cols + 128]
    w_query = r["w_query"]
    w_out, w_up = r["w_mid"].at[:, 0:mid_cols], r["w_mid"].at[:, mid_cols : mid_cols + hidden_size]
    w_down = r["w_down"]
    r["past"] = r["s_qkv"].at[:, width : 3 * width]
    r["query"] = r["s_qkv"].at[:, 0:width]
    for m, (name, parts) in enumerate(
        (
            ("first", ("past", "npad")),
            ("query", ("query",)),
            ("mid", ("s_out", "s_up")),
            ("down", ("s_down",)),
        )
    ):
        piece = r[parts[0]].shape[0]
        g = Gather(place, r["w_" + name], piece, r["gsend"].at[m], r["grecv"].at[m])
        own, start = g.piece(place.s, place.z), 0
        for part in parts:
            cols = r[part].shape[1]
            own[:, start : start + cols] = r[part][...].astype(bf16)
            start += cols
        gathers[name] = g
    scatters = {}
    for m, (name, piece, _) in enumerate(SUMS):
        bufs = [r[f"c_{name}{i}"] for i in range(7)]
        scatters[name] = Scatter(
            place, piece, name == "down", bufs, r["csend"].at[m], r["crecv"].at[m]
        )
    first = Exchange(place, r["summ"], r["esend"].at[0], r["erecv"].at[0])
    second = Exchange(place, r["back"], r["esend"].at[1], r["erecv"].at[1])
    first_values = Exchange(place, r["summ_value"], r["esend"].at[2], r["erecv"].at[2])
    second_sums = Exchange(place, r["back_sums"], r["esend"].at[3], r["erecv"].at[3])
    place.barrier()
    for name in ("first", "query"):
        gathers[name].start()
    for name in ("first", "query", "mid"):
        gathers[name].sides(0)

    F, D, mixed, heads = r["F"], r["D"], r["mixed"], r["heads"]
    loads = []
    for name in ORDER:
        for kind in ("m_", "a_"):
            sem = r["lsem"].at[len(loads)]
            loads.append(pltpu.make_async_copy(r[kind + name], r["v" + kind + name], sem))
            loads[-1].start()

    def advance_rows(name, rows, cols, total):
        scaled = rate * total
        moment = 0.9 * r["vm_" + name][rows, cols] + scaled
        weight = r["s_" + name][rows, cols] - (scaled + 0.9 * moment)
        average = 0.99 * r["va_" + name][rows, cols] + 0.01 * weight
        for k, value in enumerate((weight, moment, average)):
            r["t_" + name][k, rows, cols] = value

    def update(name, start):
        def rows_done(i, total):
            advance_rows(name, pl.ds(i, 16), slice(start, start + total.shape[1]), total)

        return rows_done

    def update_norm(i, total):
        advance_rows("norm", slice(0, 4), slice(0, per), total[0:4, 0:per])

    def norm_one(i):
        rows = pl.ds(i, 128)
        values = x_ref[rows].astype(f32)
        centre = values - jnp.mean(values, -1, keepdims=True)
        spread = jnp.mean(centre * centre, -1, keepdims=True)
        inv = lax.rsqrt(spread + 1e-05)
        F[rows] = centre * inv
        r["inv1"][rows] = jnp.broadcast_to(inv, (128, 128))

    by_rows(rows_all // 2, 128, norm_one)
    gathers["first"].chain_done()
    gathers["mid"].start()
    lax.fori_loop(rows_all // 256, rows_all // 128, lambda i, c: (norm_one(i * 128), c)[1], 0)

    ids = r["doc_ids"]
    docs = jnp.concatenate([ids[0:1, p * span : p * span + span] for p in range(spans)], 0).astype(f32)
    docs_ref[...] = docs
    wide = jnp.concatenate([docs] * (128 // spans), 0).T
    for p in range(spans):
        r["dcol"][pl.ds(p * span, span)] = jnp.broadcast_to(wide[:, p : p + 1], (span, 128))

    gathers["query"].chain_done()
    gathers["down"].start()
    gathers["first"].sides_done()
    gathers["query"].sides_done()
    gathers["mid"].chain_piece(1)

    def turn_grad(i):
        rows = pl.ds(pl.multiple_of(i, 128), 128)
        r["dyT"][:, rows] = dy_ref[rows].T

    gathers["first"].corner_done()
    gathers["first"].done()
    gathers["mid"].chain_piece(2)

    place_row = lax.broadcasted_iota(jnp.int32, (128, width), 0)
    place_col = lax.broadcasted_iota(jnp.int32, (128, width), 1)
    pick = ((place_col & (per - 1)) == place_row).astype(f32).astype(bf16)
    owner_row = lax.shift_right_logical(
        lax.broadcasted_iota(jnp.int32, (16 * devices, width), 0), 4
    )
    owner_col = lax.shift_right_logical(
        lax.broadcasted_iota(jnp.int32, (16 * devices, width), 1), per.bit_length() - 1
    )
    spread_rows = dot_nn(w_norm[...], pick)
    spread_rows = jnp.where(owner_row == owner_col, spread_rows, 0.0)
    norm_rows = jnp.sum(spread_rows.reshape(devices, 16, width), 0)
    r["nrows"][...] = norm_rows


    def project(i):
        rows = pl.ds(pl.multiple_of(i, chunk), chunk)
        act = (F[rows] * r["nrows"][0:1] + r["nrows"][1:2]).astype(bf16)
        r["act1T"][:, rows] = act.T
        mixed[rows, width : 3 * width] = dot_nn(act, w_past[...]).astype(bf16)
        r["act2"][rows] = act

    by_rows(rows_all, chunk, project)

    last_doc = docs[:, span - 1 : span]
    member = (docs == last_doc).astype(f32)
    count = jnp.sum(member, 1, keepdims=True)
    which = lax.broadcasted_iota(jnp.int32, (spans, span), 0)
    blocks = [jnp.where(which == p, member, 0.0) for p in range(spans)]
    left = jnp.concatenate(blocks, 1)
    left = jnp.concatenate([left, jnp.zeros_like(left)], 0).astype(bf16)
    means = dot_nn(left, mixed[:, width : 3 * width])[:spans] / count
    summ = r["summ"]
    summ[place.s, :, 0:width] = means[:, :width]
    summ[place.s, :, width : width + 128] = jnp.broadcast_to(last_doc, (spans, 128))
    r["summ_value"][place.s] = means[:, width:].astype(bf16)
    first.go(lambda peer: summ.at[place.s])
    first_values.go(lambda peer: r["summ_value"].at[place.s])
    gathers["query"].corner_done()
    gathers["mid"].chain_piece(3)
    gathers["mid"].sides_done((0,))
    gathers["query"].done()

    def project_query(i):
        rows = pl.ds(pl.multiple_of(i, chunk), chunk)
        mixed[rows, 0:width] = (dot_nn(r["act2"][rows], w_query[...]) * 0.125).astype(bf16)

    by_rows(rows_all, chunk, project_query)
    by_rows(rows_all, 128, turn_grad)
    first.wait()
    first_values.wait()
    gathers["mid"].sides_done((1,))
    gathers["down"].sides(0)

    sums = summ[...].reshape(8 * spans, width + 128)
    sum_values = r["summ_value"][...].astype(f32).reshape(8 * spans, width)
    keys = sums[:, :width]
    stat_mean = total_of(keys) / entries
    centred = keys - stat_mean
    stat_var = total_of(centred * centred) / entries
    inv_sum = lax.rsqrt(stat_var + 1e-05)
    key_norm = centred * inv_sum
    r["knorm"][...] = key_norm
    lane = lax.broadcasted_iota(jnp.int32, (span, 128), 1)
    low_half = lane < 64
    lane_row = lax.broadcasted_iota(jnp.int32, (1, 128), 1)
    pick0 = (lane_row < 64).astype(f32).astype(bf16)
    pick1 = (lane_row >= 64).astype(f32).astype(bf16)
    for j in range(pairs):
        cols = slice(128 * j, 128 * j + 128)
        part = key_norm[:, cols].astype(bf16)
        r["KR"][j] = jnp.concatenate([part * pick0, part * pick1], 0)
        part = sum_values[:, cols].astype(bf16)
        r["VR"][j] = jnp.concatenate([part * pick0, part * pick1], 0)
    last = sums[:, width:]
    r["lastrow"][...] = jnp.concatenate([last, last], 0).T[0:8]

    probs = r["probs"]
    causal = lax.broadcasted_iota(jnp.int32, (span, 128), 0) >= lax.broadcasted_iota(
        jnp.int32, (span, 128), 1
    )
    span_first = place.s * spans
    quarter = spans // 4

    def attend(p, carry):
        rows = pl.ds(pl.multiple_of(p * span, span), span)
        column = r["dcol"][rows]
        mask_local = (column == docs_ref[pl.ds(p, 1)]) & causal
        mask_remote = (column == r["lastrow"][0:1]) & (lax.rem(lane, 64) < span_first + p)
        scores, lows = [], []
        for j in range(pairs):
            query = mixed[rows, 128 * j : 128 * j + 128]
            key = mixed[rows, width + 128 * j : width + 128 * j + 128]
            scores.append(dot_nt(query, jnp.concatenate([key * pick0, key * pick1, r["KR"][j]], 0)))
        for j in range(pairs):
            one = jnp.where(mask_local, scores[j][:, :128], NEG)
            two = jnp.where(mask_local, scores[j][:, 128:256], NEG)
            far = jnp.where(mask_remote, scores[j][:, 256:], NEG)
            peak1 = jnp.max(jnp.maximum(one, jnp.where(low_half, far, NEG)), -1, keepdims=True)
            peak2 = jnp.max(jnp.maximum(two, jnp.where(low_half, NEG, far)), -1, keepdims=True)
            one = jnp.exp(one - peak1)
            two = jnp.exp(two - peak2)
            far = jnp.exp(far - jnp.where(low_half, peak1, peak2))
            scale1 = 1.0 / jnp.sum(one + jnp.where(low_half, far, 0.0), -1, keepdims=True)
            scale2 = 1.0 / jnp.sum(two + jnp.where(low_half, 0.0, far), -1, keepdims=True)
            one = one * scale1
            two = two * scale2
            far = far * jnp.where(low_half, scale1, scale2)
            base = 384 * j
            probs[rows, base : base + 128] = one
            probs[rows, base + 128 : base + 256] = two
            probs[rows, base + 256 : base + 384] = far
            lows.append(jnp.concatenate([one, two, far], 1).astype(bf16))
        for j in range(pairs):
            value = mixed[rows, 2 * width + 128 * j : 2 * width + 128 * j + 128]
            values = jnp.concatenate([value * pick0, value * pick1, r["VR"][j]], 0)
            heads[rows, 128 * j : 128 * j + 128] = dot_nn(lows[j], values).astype(bf16)
        return carry

    gathers["down"].chain_done()
    lax.fori_loop(0, 3 * quarter, attend, 0)
    gathers["mid"].corner_done()
    lax.fori_loop(3 * quarter, spans, attend, 0)
    gathers["mid"].done()

    r["ngrad"][...] = jnp.zeros_like(r["ngrad"])
    tile = 256

    def feed(i):
        rows = pl.ds(pl.multiple_of(i, chunk), chunk)
        part = heads[rows]
        r["headsT"][:, rows] = part.T
        after = x_ref[rows].astype(f32) + dot_nn(part, w_out[...])
        centre = after - jnp.mean(after, -1, keepdims=True)
        spread = jnp.mean(centre * centre, -1, keepdims=True)
        inv = lax.rsqrt(spread + 1e-05)
        normal = centre * inv
        F[rows] = after
        D[rows] = normal
        r["inv2"][rows] = jnp.broadcast_to(inv, (chunk, 128))
        act_two = (normal * r["nrows"][2:3] + r["nrows"][3:4]).astype(bf16)
        r["act2"][rows] = act_two
        r["act2T"][:, rows] = act_two.T

    lax.fori_loop(0, chunks // 2, lambda i, c: (feed(i * chunk), c)[1], 0)
    gathers["down"].sides_done()
    lax.fori_loop(chunks // 2, chunks, lambda i, c: (feed(i * chunk), c)[1], 0)
    gathers["down"].corner_done()
    gathers["down"].done()

    down, out = scatters["down"], scatters["out"]
    ups = [scatters[f"up{g}"] for g in range(4)]
    quad = hidden_size // 4

    def put(target, grad, cols):
        gr = target.gr
        for g in range(4):
            for c in range(2):
                k = (2 * g + c) * gr
                target.full[g, c, :, cols] = grad[k : k + gr]

    for g in range(4):

        def mlp(i, g=g):
            parts = [
                (pl.ds(pl.multiple_of(i + top, chunk), chunk), slice(start, start + tile))
                for top in (0, chunk)
                for start in range(g * quad, g * quad + quad, tile)
            ]
            waiting = []
            for step in range(len(parts) + 1):
                if step < len(parts):
                    rows, cols = parts[step]
                    h = dot_nn(r["act2"][rows], w_up[:, cols])
                    d = dot_nt(dy_ref[rows], w_down[cols])
                    waiting.append((rows, cols, h, d))
                if step:
                    rows, cols, h, d = waiting[step - 1]
                    square = h * h
                    gate = 0.5 + 0.5 * jnp.tanh(h * (LEFT + (LEFT * CUBE) * square))
                    act = h * gate
                    r["act3"][rows, cols] = act.astype(bf16)
                    slope = gate + act * (2.0 * LEFT + (6.0 * LEFT * CUBE) * square) * (1.0 - gate)
                    r["dhid"][rows, cols] = (d * slope).astype(bf16)

        by_rows(rows_all, 2 * chunk, mlp)
        if g:
            ups[g - 1].core_done()
        if g > 1:
            ups[g - 2].sides_done()
        grad = dot_nn(r["dyT"][...], r["act3"][:, g * quad : g * quad + quad]).astype(bf16)
        down.full[g, 0] = grad[:, : quad // 2]
        down.full[g, 1] = grad[:, quad // 2 :]
        down.start_group(g)
        grad = dot_nn(r["act2T"][...], r["dhid"][:, g * quad : g * quad + quad]).astype(bf16)
        put(ups[g], grad, pl.ds(0, quad))
        ups[g].start()

    def feed_back(i):
        rows = pl.ds(pl.multiple_of(i, chunk), chunk)
        d_two = dot_nt(r["dhid"][rows], w_up[...])
        normal = D[rows]
        r["ngrad"][2] += fold_rows(d_two * normal)
        r["ngrad"][3] += fold_rows(d_two)
        scaled = d_two * r["nrows"][2:3]
        centred = (
            scaled
            - jnp.mean(scaled, -1, keepdims=True)
            - normal * jnp.mean(scaled * normal, -1, keepdims=True)
        )
        d_after = dy_ref[rows].astype(f32) + r["inv2"][rows][:, 0:1] * centred
        D[rows] = d_after
        low = d_after.astype(bf16)
        r["dafter"][rows] = low
        heads[rows] = dot_nt(low, w_out[...]).astype(bf16)

    lax.fori_loop(0, chunks // 2, lambda i, c: (feed_back(i * chunk), c)[1], 0)
    ups[3].core_done()
    ups[2].sides_done()
    down.core_done()
    lax.fori_loop(chunks // 2, chunks, lambda i, c: (feed_back(i * chunk), c)[1], 0)
    ups[3].sides_done()
    put(out, dot_nn(r["headsT"][...], r["dafter"][...]).astype(bf16), pl.ds(0, width))
    out.start()

    kept = r["dhid"]
    side = 384 * pairs

    def attend_back(p, carry):
        rows = pl.ds(pl.multiple_of(p * span, span), span)
        wide_probs, d_scores, stacks = [], [], []
        for j in range(pairs):
            key = mixed[rows, width + 128 * j : width + 128 * j + 128]
            value = mixed[rows, 2 * width + 128 * j : 2 * width + 128 * j + 128]
            stacks.append(jnp.concatenate([key * pick0, key * pick1, r["KR"][j]], 0))
            values_all = jnp.concatenate([value * pick0, value * pick1, r["VR"][j]], 0)
            wide_probs.append(dot_nt(heads[rows, 128 * j : 128 * j + 128], values_all))
        for j in range(pairs):
            d_probs = wide_probs[j]
            base = 384 * j
            one = probs[rows, base : base + 128]
            two = probs[rows, base + 128 : base + 256]
            far = probs[rows, base + 256 : base + 384]
            d_far = far * d_probs[:, 256:]
            sum1 = jnp.sum(one * d_probs[:, :128] + jnp.where(low_half, d_far, 0.0), -1, keepdims=True)
            sum2 = jnp.sum(two * d_probs[:, 128:256] + jnp.where(low_half, 0.0, d_far), -1, keepdims=True)
            d_one = one * (d_probs[:, :128] - sum1)
            d_two = two * (d_probs[:, 128:256] - sum2)
            d_far = far * (d_probs[:, 256:] - jnp.where(low_half, sum1, sum2))
            d_scores.append(jnp.concatenate([d_one, d_two, d_far], 1).astype(bf16))
            kept[rows, base : base + 384] = d_scores[j]
            kept[rows, side + 128 * j : side + 128 * j + 128] = far.astype(bf16)
        for j in range(pairs):
            at = slice(128 * j, 128 * j + 128)
            r["act2"][rows, at] = (0.125 * dot_nn(d_scores[j], stacks[j])).astype(bf16)
        return carry

    lax.fori_loop(0, quarter, attend_back, 0)
    ups[0].mine_done()
    lax.fori_loop(quarter, 2 * quarter, attend_back, 0)
    ups[1].mine_done()
    lax.fori_loop(2 * quarter, 3 * quarter, attend_back, 0)
    ups[2].mine_done()
    lax.fori_loop(3 * quarter, spans, attend_back, 0)

    half_spans = 8 * spans
    parts = []
    for name in ("key", "value"):
        for j in range(pairs):
            at = slice(128 * j, 128 * j + 128)
            if name == "key":
                both = dot_tn(kept[:, 384 * j + 256 : 384 * j + 384], mixed[:, at])
            else:
                both = dot_tn(kept[:, side + 128 * j : side + 128 * j + 128], heads[:, at])
            low = low_half[:half_spans]
            parts.append(jnp.where(low, both[:half_spans], both[half_spans:]))
    d_keys = jnp.concatenate(parts[:pairs], 1)
    d_values = jnp.concatenate(parts[pairs:], 1)
    key_norm = r["knorm"][...]
    flat = jnp.where(lane_row < 64, total_of(d_keys), total_of(d_keys * key_norm))
    send = r["sendback"]
    send[:, :, 0:width] = d_keys.reshape(8, spans, width).astype(bf16)
    send[:, :, width : 2 * width] = d_values.reshape(8, spans, width).astype(bf16)
    back, back_sums = r["back"], r["back_sums"]
    back[place.s] = send[place.s]
    back_sums[place.s] = jnp.broadcast_to(flat, (spans, 128))
    second.go(lambda peer: send.at[peer])
    second_sums.go(lambda peer: back_sums.at[place.s])

    q_sum, k_sum, v_sum = scatters["q"], scatters["k"], scatters["v"]
    put(q_sum, dot_nn(r["act1T"][...], r["act2"][...]).astype(bf16), pl.ds(0, width))
    q_sum.start()
    out.core_done()
    down.sides_done()
    ups[3].mine_done()

    def local_back(p, carry):
        rows = pl.ds(pl.multiple_of(p * span, span), span)
        d_keys, d_values = [], []
        for j in range(pairs):
            at = slice(128 * j, 128 * j + 128)
            low = probs[rows, 384 * j : 384 * j + 256].astype(bf16)
            d_keys.append(dot_tn(kept[rows, 384 * j : 384 * j + 256], mixed[rows, at]))
            d_values.append(dot_tn(low, heads[rows, at]))
        for j in range(pairs):
            at = slice(128 * j, 128 * j + 128)
            probs[rows, at] = jnp.where(low_half, d_keys[j][:128], d_keys[j][128:])
            past = slice(width + 128 * j, width + 128 * j + 128)
            probs[rows, past] = jnp.where(low_half, d_values[j][:128], d_values[j][128:])
        return carry

    lax.fori_loop(0, 2 * quarter, local_back, 0)
    out.sides_done()
    q_sum.core_done()
    lax.fori_loop(2 * quarter, spans, local_back, 0)
    second.wait()
    second_sums.wait()

    owned = jnp.sum(back[...].astype(f32), 0)
    flat = jnp.sum(back_sums[...], 0)
    back_sum, back_cross = flat[0:1, 0:1], flat[0:1, 64:65]
    mine_norm = r["knorm"][pl.ds(pl.multiple_of(place.s * spans, spans), spans)]
    d_sum_key = inv_sum * (
        owned[:, :width] - back_sum * (1.0 / entries) - mine_norm * (back_cross * (1.0 / entries))
    )
    r["dsum"][:, 0:width] = d_sum_key / count
    r["dsum"][:, width : 2 * width] = owned[:, width : 2 * width] / count
    slot = lax.broadcasted_iota(jnp.int32, (8, 128), 1)
    stats = jnp.where(slot == 0, stat_mean, stat_var)
    stats = jnp.where(slot == 2, -inv_sum * back_sum, stats)
    stats = jnp.where(slot == 3, -0.5 * inv_sum * inv_sum * back_cross, stats)
    r["stats"][...] = stats

    def join(p, carry):
        rows = pl.ds(pl.multiple_of(p * span, span), span)
        final = docs_ref[pl.ds(p, 1)][:, span - 1 : span]
        share = (r["dcol"][rows] == final).astype(f32)
        sums_row = r["dsum"][pl.ds(p, 1)]
        for j in range(pairs):
            at = slice(128 * j, 128 * j + 128)
            past = slice(width + 128 * j, width + 128 * j + 128)
            full = probs[rows, at] + share * sums_row[:, at]
            mixed[rows, past] = full.astype(bf16)
            full = probs[rows, past] + share * sums_row[:, past]
            mixed[rows, 2 * width + 128 * j : 2 * width + 128 * j + 128] = full.astype(bf16)
        return carry

    lax.fori_loop(0, spans, join, 0)

    put(k_sum, dot_nn(r["act1T"][...], mixed[:, width : 2 * width]).astype(bf16), pl.ds(0, width))
    k_sum.start()
    put(v_sum, dot_nn(r["act1T"][...], mixed[:, 2 * width :]).astype(bf16), pl.ds(0, width))
    v_sum.start()

    def first_back(i):
        rows = pl.ds(pl.multiple_of(i, chunk), chunk)
        d_one = dot_nt(r["act2"][rows], w_query[...])
        d_one = d_one + dot_nt(mixed[rows, width : 3 * width], w_past[...])
        values = x_ref[rows].astype(f32)
        inv = r["inv1"][rows][:, 0:1]
        normal = (values - jnp.mean(values, -1, keepdims=True)) * inv
        r["ngrad"][0] += fold_rows(d_one * normal)
        r["ngrad"][1] += fold_rows(d_one)
        scaled = d_one * r["nrows"][0:1]
        centred = (
            scaled
            - jnp.mean(scaled, -1, keepdims=True)
            - normal * jnp.mean(scaled * normal, -1, keepdims=True)
        )
        r["input_grad"][rows] = D[rows] + inv * centred

    half_chunks = chunks // 2
    lax.fori_loop(0, half_chunks, lambda i, c: (first_back(i * chunk), c)[1], 0)
    k_sum.core_far()
    v_sum.core_far()
    k_sum.core_near()
    v_sum.core_near()
    q_sum.sides_done()
    down.mine_done()
    out.mine_done()
    lax.fori_loop(half_chunks, chunks, lambda i, c: (first_back(i * chunk), c)[1], 0)

    pieces = jnp.concatenate(
        [jnp.sum(r["ngrad"][k], 0, keepdims=True) for k in range(4)]
        + [jnp.zeros((12, width), f32)],
        0,
    )
    spread_rows = jnp.broadcast_to(pieces[None], (devices, 16, width)).reshape(16 * devices, width)
    spread_rows = jnp.where(owner_row == owner_col, spread_rows, 0.0).astype(bf16)
    norm = scatters["norm"]
    narrow = dot_nt(spread_rows, pick).astype(bf16)
    put(norm, jnp.concatenate([narrow, jnp.zeros_like(narrow)], 1), pl.ds(0, 256))
    norm.start()

    def output(i):
        rows = pl.ds(pl.multiple_of(i, chunk), chunk)
        result = F[rows] + dot_nn(r["act3"][rows], w_down[...])
        r["block_out"][rows] = result.astype(bf16)

    lax.fori_loop(0, half_chunks, lambda i, c: (output(i * chunk), c)[1], 0)
    norm.core_done()
    k_sum.sides_done()
    v_sum.sides_done()
    q_sum.mine_done()
    lax.fori_loop(half_chunks, chunks, lambda i, c: (output(i * chunk), c)[1], 0)
    norm.sides_done()
    k_sum.mine_done()
    v_sum.mine_done()
    for copy in loads:
        copy.wait()
    for g in range(4):
        ups[g].done(update("up", g * quad))
    for name in ("down", "out"):
        scatters[name].done(update(name, 0))
    norm.mine_done()
    q_sum.done(update("qkv", 0))
    k_sum.done(update("qkv", width))
    v_sum.done(update("qkv", 2 * width))
    norm.done(update_norm)
    for part in list(gathers.values()) + list(scatters.values()) + [first, first_values, second, second_sums]:
        part.drain()


def fused_layer(chain, rate, tokens, grad, doc_ids, shards, moments, averages):
    f32, bf16 = jnp.float32, jnp.bfloat16
    rows, width = tokens.shape
    spans = rows // SPAN
    order = ORDER
    devices = 8 * chain
    ins = [("tokens", tokens), ("grad", grad), ("doc_ids", doc_ids)]
    ins += [("s_" + name, shards[name]) for name in order]
    ins += [("m_" + name, moments[name]) for name in order]
    ins += [("a_" + name, averages[name]) for name in order]
    outs = [
        ("block_out", pltpu.VMEM((rows, width), bf16)),
        ("input_grad", pltpu.VMEM((rows, width), f32)),
        ("stats", pltpu.VMEM((8, 128), f32)),
    ]
    outs += [("t_" + name, pltpu.VMEM((3,) + shards[name].shape, f32)) for name in order]
    hidden = shards["up"].shape[1]
    scratch = {}
    down_rows = shards["down"].shape[0]
    scratch["w_first"] = pltpu.VMEM((devices * 16, 2 * width + 128), bf16)
    scratch["w_query"] = pltpu.VMEM((devices * 16, width), bf16)
    scratch["w_mid"] = pltpu.VMEM((devices * 16, width + hidden), bf16)
    scratch["w_down"] = pltpu.VMEM((devices * down_rows, width), bf16)
    for name, piece, cols in SUMS:
        for i, buf in enumerate(scatter_scratch(chain, piece, cols, name == "down")):
            scratch[f"c_{name}{i}"] = buf
    for name in order:
        scratch["vm_" + name] = pltpu.VMEM(shards[name].shape, f32)
        scratch["va_" + name] = pltpu.VMEM(shards[name].shape, f32)
    scratch["lsem"] = DMA((10,))
    pairs = width // 128
    scratch |= {
        "gsend": DMA((4, GATHER_SEMS)),
        "grecv": DMA((4, GATHER_SEMS)),
        "csend": DMA((10, SCATTER_SEMS)),
        "crecv": DMA((10, SCATTER_SEMS)),
        "esend": DMA((4, 7)),
        "erecv": DMA((4, 7)),
        "summ": pltpu.VMEM((8, spans, width + 128), f32),
        "summ_value": pltpu.VMEM((8, spans, width), bf16),
        "back": pltpu.VMEM((8, spans, 2 * width), bf16),
        "back_sums": pltpu.VMEM((8, spans, 128), f32),
        "sendback": pltpu.VMEM((8, spans, 2 * width), bf16),
        "F": pltpu.VMEM((rows, width), f32),
        "inv1": pltpu.VMEM((rows, 128), f32),
        "dcol": pltpu.VMEM((rows, 128), f32),
        "nrows": pltpu.VMEM((16, width), f32),
        "ngrad": pltpu.VMEM((4, 8, width), f32),
        "act1T": pltpu.VMEM((width, rows), bf16),
        "dyT": pltpu.VMEM((width, rows), bf16),
        "act2T": pltpu.VMEM((width, rows), bf16),
        "headsT": pltpu.VMEM((width, rows), bf16),
        "mixed": pltpu.VMEM((rows, 3 * width), bf16),
        "probs": pltpu.VMEM((rows, 384 * pairs), f32),
        "heads": pltpu.VMEM((rows, width), bf16),
        "knorm": pltpu.VMEM((8 * spans, width), f32),
        "KR": pltpu.VMEM((pairs, 128, 128), bf16),
        "VR": pltpu.VMEM((pairs, 128, 128), bf16),
        "lastrow": pltpu.VMEM((8, 128), f32),
        "docs": pltpu.VMEM((spans, SPAN), f32),
        "npad": pltpu.VMEM((16, 128), f32),
        "inv2": pltpu.VMEM((rows, 128), f32),
        "act2": pltpu.VMEM((rows, width), bf16),
        "act3": pltpu.VMEM((rows, hidden), bf16),
        "dhid": pltpu.VMEM((rows, hidden), bf16),
        "dafter": pltpu.VMEM((rows, width), bf16),
        "D": pltpu.VMEM((rows, width), f32),
        "dsum": pltpu.VMEM((spans, 2 * width), f32),
    }
    names = [n for n, _ in ins] + [n for n, _ in outs] + list(scratch)
    vmem = pl.BlockSpec(memory_space=pltpu.VMEM)
    result = pl.pallas_call(
        functools.partial(layer_kernel, chain, rate, names),
        out_shape=[shape for _, shape in outs],
        in_specs=[vmem] * (len(ins) - 10) + [pl.BlockSpec(memory_space=pltpu.HBM)] * 10,
        out_specs=[vmem] * len(outs),
        scratch_shapes=list(scratch.values()),
        compiler_params=pltpu.CompilerParams(
            collective_id=0, has_side_effects=True, vmem_limit_bytes=59 * 2**20
        ),
    )(*[value for _, value in ins])
    return dict(zip([n for n, _ in outs], result))


def finish_kernel(count, *refs):
    ins, outs, sems = refs[:count], refs[count:-1], refs[-1]
    stats, two = ins[-1], outs[count - 1 :]
    copies = [pltpu.make_async_copy(ins[k], outs[k], sems.at[k]) for k in range(count - 1)]
    for copy in copies:
        copy.start()
    two[0][...] = stats[0:1, 0:2]
    two[1][...] = stats[0:1, 2:4]
    for copy in copies:
        copy.wait()


def finish(arrays, stats):
    vmem = pl.BlockSpec(memory_space=pltpu.VMEM)
    two = jax.ShapeDtypeStruct((1, 2), jnp.float32)
    count = len(arrays) + 1
    return pl.pallas_call(
        functools.partial(finish_kernel, count),
        out_shape=[jax.ShapeDtypeStruct(a.shape, a.dtype) for a in arrays] + [two, two],
        in_specs=[pl.BlockSpec(memory_space=pl.ANY)] * (count - 1) + [vmem],
        out_specs=[pl.BlockSpec(memory_space=pltpu.HBM)] * (count - 1) + [vmem] * 2,
        scratch_shapes=[DMA((count - 1,))],
        compiler_params=pltpu.CompilerParams(vmem_limit_bytes=2 * 2**20),
    )(*(pltpu.with_memory_space_constraint(a, pltpu.VMEM) for a in arrays), stats)


def norm_forward(values, gain_row, shift_row):
    centre = values - jnp.mean(values, -1, keepdims=True)
    spread = jnp.mean(centre * centre, -1, keepdims=True)
    inv_std = lax.rsqrt(spread + 1e-05)
    normal = centre * inv_std
    return (normal * gain_row + shift_row, normal, inv_std)


def norm_backward(grad_in, normal, inv_std, gain_row):
    scaled = grad_in * gain_row
    centred = (
        scaled
        - jnp.mean(scaled, -1, keepdims=True)
        - normal * jnp.mean(scaled * normal, -1, keepdims=True)
    )
    return (inv_std * centred, jnp.sum(grad_in * normal, 0), jnp.sum(grad_in, 0))


def gelu_tanh(values):
    return jax.nn.gelu(values, approximate=True)


def span_probs(query_blk, key_blk, key_remote, doc_span, last_remote, span_first):
    span_len = doc_span.shape[2]
    local = (
        jnp.einsum("bpqhe,bpkhe->bphqk", query_blk, key_blk, preferred_element_type=jnp.float32)
        * 0.125
    )
    remote = (
        jnp.einsum("bpqhe,bnhe->bphqn", query_blk, key_remote, preferred_element_type=jnp.float32)
        * 0.125
    )
    positions = jnp.arange(span_len)
    causal = positions[:, None] >= positions[None, :]
    same_doc = doc_span[:, :, :, None] == doc_span[:, :, None, :]
    mask_local = (same_doc & causal[None, None])[:, :, None]
    span_ids = span_first + jnp.arange(doc_span.shape[1])
    earlier = jnp.arange(key_remote.shape[1])[None, :] < span_ids[:, None]
    doc_float = doc_span.astype(jnp.float32)
    match = doc_float[:, :, :, None] == last_remote.astype(jnp.float32)[:, None, None, :]
    mask_remote = (match & earlier[None, :, None, :])[:, :, None]
    allowed = jnp.concatenate([mask_local, mask_remote], -1)
    scores = jnp.where(allowed, jnp.concatenate([local, remote], -1), -1e30)
    peak_score = jnp.max(scores, -1, keepdims=True)
    raised = jnp.exp(scores - peak_score)
    return raised / jnp.sum(raised, -1, keepdims=True)


def advance(weight, moment, average, grad, rate):
    new_moment = 0.9 * moment + rate * grad
    new_weight = weight - (rate * grad + 0.9 * new_moment)
    new_average = 0.99 * average + 0.01 * new_weight
    return jnp.stack([new_weight, new_moment, new_average])


def shards_plain(
    tokens,
    grad_out,
    doc_ids,
    qkv_w,
    qkv_m,
    qkv_a,
    out_w,
    out_m,
    out_a,
    up_w,
    up_m,
    up_a,
    down_w,
    down_m,
    down_a,
    norm_w,
    norm_m,
    norm_a,
):
    seqs, seq_len, width = tokens.shape
    span_len = SPAN
    cycle_size = lax.axis_size("seq")
    cycle_rank = lax.axis_index("seq")
    spans_dev = seq_len // span_len
    spans_all = spans_dev * cycle_size
    rows_dev = seqs * seq_len
    head_size = width // H
    bf16 = jnp.bfloat16
    f32 = jnp.float32
    w_qkv, w_out, w_up, w_down, norm_low = (
        lax.all_gather(qkv_w.astype(bf16), ("seq", "dp"), axis=0, tiled=True),
        lax.all_gather(out_w.astype(bf16), ("seq", "dp"), axis=0, tiled=True),
        lax.all_gather(up_w.astype(bf16), ("seq", "dp"), axis=0, tiled=True),
        lax.all_gather(down_w.astype(bf16), ("seq", "dp"), axis=0, tiled=True),
        lax.all_gather(norm_w.astype(bf16), ("seq", "dp"), axis=1, tiled=True),
    )
    norm_rows = norm_low.astype(f32)
    inputs = tokens.reshape(rows_dev, width).astype(f32)
    normed_one, normal_one, inv_one = norm_forward(inputs, norm_rows[0], norm_rows[1])
    act_one = normed_one.astype(bf16)
    mixed = jnp.dot(act_one, w_qkv, preferred_element_type=f32)
    query = mixed[:, :width].astype(bf16)
    key_all = mixed[:, width : 2 * width].astype(bf16)
    value_all = mixed[:, 2 * width :].astype(bf16)
    block_shape = (seqs, spans_dev, span_len, H, head_size)
    query_blk = query.reshape(block_shape)
    key_blk = key_all.reshape(block_shape)
    value_blk = value_all.reshape(block_shape)
    doc_span = doc_ids.reshape(seqs, spans_dev, span_len)
    last_doc = doc_span[:, :, -1]
    member = (doc_span == last_doc[:, :, None]).astype(f32)
    counts = jnp.sum(member, -1)
    member_low = member.astype(bf16)
    key_four = key_all.reshape(seqs, spans_dev, span_len, width)
    value_four = value_all.reshape(seqs, spans_dev, span_len, width)
    sum_key = (
        jnp.einsum("bpt,bptd->bpd", member_low, key_four, preferred_element_type=f32)
        / counts[..., None]
    )
    sum_value = (
        jnp.einsum("bpt,bptd->bpd", member_low, value_four, preferred_element_type=f32)
        / counts[..., None]
    )
    total_sum, total_square = lax.psum(
        (jnp.sum(sum_key, (1, 2)), jnp.sum(sum_key * sum_key, (1, 2))), "seq"
    )
    entries = spans_all * width
    stat_mean = total_sum / entries
    stat_var = total_square / entries - stat_mean * stat_mean
    inv_sum = lax.rsqrt(stat_var + 1e-05)
    key_norm = (sum_key - stat_mean[:, None, None]) * inv_sum[:, None, None]
    key_send = key_norm.astype(bf16)
    value_send = sum_value.astype(bf16)
    last_send = last_doc.astype(bf16)
    key_remote, value_remote, last_remote = (
        lax.all_gather(key_send, "seq", axis=1, tiled=True),
        lax.all_gather(value_send, "seq", axis=1, tiled=True),
        lax.all_gather(last_send, "seq", axis=1, tiled=True),
    )
    remote_shape = (seqs, spans_all, H, head_size)
    span_first = cycle_rank * spans_dev
    probs = span_probs(
        query_blk, key_blk, key_remote.reshape(remote_shape), doc_span, last_remote, span_first
    )
    probs_low = probs.astype(bf16)
    attended = jnp.einsum(
        "bphqk,bpkhe->bpqhe", probs_low[..., :span_len], value_blk, preferred_element_type=f32
    )
    attended = attended + jnp.einsum(
        "bphqn,bnhe->bpqhe",
        probs_low[..., span_len:],
        value_remote.reshape(remote_shape),
        preferred_element_type=f32,
    )
    heads_out = attended.reshape(rows_dev, width).astype(bf16)
    after_attn = inputs + jnp.dot(heads_out, w_out, preferred_element_type=f32)
    normed_two, normal_two, inv_two = norm_forward(after_attn, norm_rows[2], norm_rows[3])
    act_two = normed_two.astype(bf16)
    hidden = jnp.dot(act_two, w_up, preferred_element_type=f32)
    act_three = gelu_tanh(hidden).astype(bf16)
    result = after_attn + jnp.dot(act_three, w_down, preferred_element_type=f32)
    block_out = result.astype(bf16).reshape(seqs, seq_len, width)
    stats_out = jnp.stack([stat_mean, stat_var], -1)
    grad_low = grad_out.reshape(rows_dev, width)
    grad_down = jnp.einsum("tf,td->fd", act_three, grad_low, preferred_element_type=f32)
    d_three = jnp.einsum("td,fd->tf", grad_low, w_down, preferred_element_type=f32)
    unused_out, gelu_pull = jax.vjp(gelu_tanh, hidden)
    d_hidden = gelu_pull(d_three)[0].astype(bf16)
    grad_up = jnp.einsum("td,tf->df", act_two, d_hidden, preferred_element_type=f32)
    d_two = jnp.einsum("tf,df->td", d_hidden, w_up, preferred_element_type=f32)
    d_norm_two, gain_two, shift_two = norm_backward(d_two, normal_two, inv_two, norm_rows[2])
    d_after = grad_low.astype(f32) + d_norm_two
    d_after_low = d_after.astype(bf16)
    grad_outw = jnp.einsum("tc,td->cd", heads_out, d_after_low, preferred_element_type=f32)
    d_heads = jnp.einsum("td,cd->tc", d_after_low, w_out, preferred_element_type=f32).astype(bf16)
    key_back, value_back, last_back = (key_remote, value_remote, last_remote)
    key_back_blk = key_back.reshape(remote_shape)
    value_back_blk = value_back.reshape(remote_shape)
    probs_back = span_probs(query_blk, key_blk, key_back_blk, doc_span, last_back, span_first)
    probs_back_low = probs_back.astype(bf16)
    d_heads_blk = d_heads.reshape(block_shape)
    d_probs = jnp.concatenate(
        [
            jnp.einsum("bpqhe,bpkhe->bphqk", d_heads_blk, value_blk, preferred_element_type=f32),
            jnp.einsum(
                "bpqhe,bnhe->bphqn", d_heads_blk, value_back_blk, preferred_element_type=f32
            ),
        ],
        -1,
    )
    row_dot = jnp.sum(probs_back * d_probs, -1, keepdims=True)
    d_scores = (probs_back * (d_probs - row_dot)).astype(bf16)
    d_local = d_scores[..., :span_len]
    d_remote = d_scores[..., span_len:]
    d_query = 0.125 * (
        jnp.einsum("bphqk,bpkhe->bpqhe", d_local, key_blk, preferred_element_type=f32)
        + jnp.einsum("bphqn,bnhe->bpqhe", d_remote, key_back_blk, preferred_element_type=f32)
    )
    d_key = 0.125 * jnp.einsum("bphqk,bpqhe->bpkhe", d_local, query_blk, preferred_element_type=f32)
    d_value = jnp.einsum(
        "bphqk,bpqhe->bpkhe",
        probs_back_low[..., :span_len],
        d_heads_blk,
        preferred_element_type=f32,
    )
    d_key_sum = (
        0.125 * jnp.einsum("bphqn,bpqhe->bnhe", d_remote, query_blk, preferred_element_type=f32)
    ).reshape(seqs, spans_all, width)
    d_value_sum = jnp.einsum(
        "bphqn,bpqhe->bnhe", probs_back_low[..., span_len:], d_heads_blk, preferred_element_type=f32
    ).reshape(seqs, spans_all, width)
    owned_key, owned_value = (
        lax.psum_scatter(
            d_key_sum.astype(jnp.bfloat16), "seq", scatter_dimension=1, tiled=True
        ).astype(jnp.float32),
        lax.psum_scatter(
            d_value_sum.astype(jnp.bfloat16), "seq", scatter_dimension=1, tiled=True
        ).astype(jnp.float32),
    )
    back_sum, back_cross = lax.psum(
        (jnp.sum(owned_key, (1, 2)), jnp.sum(owned_key * key_norm, (1, 2))), "seq"
    )
    stat_grads = jnp.stack([-inv_sum * back_sum, -0.5 * inv_sum * inv_sum * back_cross], -1)
    d_sum_key = inv_sum[:, None, None] * (
        owned_key
        - back_sum[:, None, None] / entries
        - key_norm * back_cross[:, None, None] / entries
    )
    share = member / counts[..., None]
    d_key_all = (
        d_key.reshape(seqs, spans_dev, span_len, width)
        + share[..., None] * d_sum_key[:, :, None, :]
    )
    d_value_all = (
        d_value.reshape(seqs, spans_dev, span_len, width)
        + share[..., None] * owned_value[:, :, None, :]
    )
    d_mixed = jnp.concatenate(
        [
            d_query.reshape(rows_dev, width),
            d_key_all.reshape(rows_dev, width),
            d_value_all.reshape(rows_dev, width),
        ],
        -1,
    ).astype(bf16)
    grad_qkv = jnp.einsum("td,tf->df", act_one, d_mixed, preferred_element_type=f32)
    d_one = jnp.einsum("tf,df->td", d_mixed, w_qkv, preferred_element_type=f32)
    d_norm_one, gain_one, shift_one = norm_backward(d_one, normal_one, inv_one, norm_rows[0])
    input_grad = (d_after + d_norm_one).reshape(seqs, seq_len, width)
    grad_norm = jnp.stack([gain_one, shift_one, gain_two, shift_two])
    sum_qkv, sum_outw, sum_up, sum_down, sum_norm = (
        lax.psum_scatter(grad_qkv, ("seq", "dp"), scatter_dimension=0, tiled=True),
        lax.psum_scatter(grad_outw, ("seq", "dp"), scatter_dimension=0, tiled=True),
        lax.psum_scatter(grad_up, ("seq", "dp"), scatter_dimension=0, tiled=True),
        lax.psum_scatter(grad_down, ("seq", "dp"), scatter_dimension=0, tiled=True),
        lax.psum_scatter(grad_norm, ("seq", "dp"), scatter_dimension=1, tiled=True),
    )
    tokens_all = rows_dev * cycle_size * lax.axis_size("dp")
    rate = 0.02 / math.sqrt(tokens_all)
    return (
        block_out,
        input_grad,
        stats_out,
        stat_grads,
        advance(qkv_w, qkv_m, qkv_a, sum_qkv, rate),
        advance(out_w, out_m, out_a, sum_outw, rate),
        advance(up_w, up_m, up_a, sum_up, rate),
        advance(down_w, down_m, down_a, sum_down, rate),
        advance(norm_w, norm_m, norm_a, sum_norm, rate),
    )


def shards(*args):
    tokens, grad_out, doc_ids = args[:3]
    qkv_w = args[3]
    seqs, seq_len, width = tokens.shape
    fits = lax.axis_size("seq") == 8 and qkv_w.shape[0] % 16 == 0
    fits = fits and seqs == 1 and seq_len == 8 * SPAN and width == 512
    if not fits:
        return shards_plain(*args)
    chain = lax.axis_size("dp")
    names = {"qkv": 3, "out": 6, "up": 9, "down": 12, "norm": 15}
    done = fused_layer(
        chain,
        0.02 / math.sqrt(seq_len * 8 * chain),
        tokens.reshape(seq_len, width),
        grad_out.reshape(seq_len, width),
        doc_ids,
        *({name: args[k + j] for name, k in names.items()} for j in range(3)),
    )
    order = ["block_out", "input_grad"] + ["t_" + name for name in names]
    result = finish([done[name] for name in order], done["stats"])
    return (
        result[0].reshape(tokens.shape),
        result[1].reshape(tokens.shape),
        *result[7:],
        *result[2:7],
    )


def solution(mesh):
    placed = (
        P("dp", "seq", None),
        P("dp", "seq", None),
        P("dp", "seq"),
        P(("seq", "dp"), None),
        P(("seq", "dp"), None),
        P(("seq", "dp"), None),
        P(("seq", "dp"), None),
        P(("seq", "dp"), None),
        P(("seq", "dp"), None),
        P(("seq", "dp"), None),
        P(("seq", "dp"), None),
        P(("seq", "dp"), None),
        P(("seq", "dp"), None),
        P(("seq", "dp"), None),
        P(("seq", "dp"), None),
        P(None, ("seq", "dp")),
        P(None, ("seq", "dp")),
        P(None, ("seq", "dp")),
    )
    return jax.shard_map(
        shards,
        mesh=mesh,
        in_specs=placed,
        out_specs=(
            P("dp", "seq", None),
            P("dp", "seq", None),
            P("dp", None),
            P("dp", None),
            P(None, ("seq", "dp"), None),
            P(None, ("seq", "dp"), None),
            P(None, ("seq", "dp"), None),
            P(None, ("seq", "dp"), None),
            P(None, None, ("seq", "dp")),
        ),
        check_vma=False,
    )
```

```python
import functools
import math

import jax
import jax.numpy as jnp
from jax import lax
from jax.experimental import pallas as pl
from jax.experimental.pallas import tpu as pltpu
from jax.sharding import PartitionSpec as P

H = 8
SPAN = 128
MESH = pl.DeviceIdType.MESH
DMA = pltpu.SemaphoreType.DMA


class Place:
    def __init__(self, chain):
        self.chain = chain
        self.s = lax.axis_index("seq")
        self.z = lax.axis_index("dp")
        self.core = lax.rem(self.s, 2)
        self.group = lax.div(self.s, 2)
        self.sib = self.flip(self.s, 1)
        self.xs = self.flip(self.s, 2)
        self.ys = self.flip(self.s, 4)
        self.ds = self.flip(self.xs, 4)

    @staticmethod
    def flip(value, bit):
        return value + bit - 2 * bit * lax.rem(lax.div(value, bit), 2)

    def dev(self, s, z=None):
        return {"seq": s, "dp": self.z if z is None else z}

    def zflip(self, bits):
        z = self.z
        for bit in (1, 2):
            if bits & bit:
                z = self.flip(z, bit)
        return z

    def zpeer(self, step):
        return lax.rem(self.z + step, self.chain)

    def barrier(self, extra=()):
        sem = pltpu.get_barrier_semaphore()
        peers = [self.dev(self.sib), self.dev(self.xs), self.dev(self.ys)]
        peers += [self.dev(self.s, self.zpeer(k)) for k in range(1, self.chain)]
        peers += list(extra)
        for peer in peers:
            pl.semaphore_signal(sem, inc=1, device_id=peer, device_id_type=MESH)
        pl.semaphore_wait(sem, len(peers))


def remote(src, dst, send, recv, peer):
    return pltpu.make_async_remote_copy(
        src_ref=src, dst_ref=dst, send_sem=send, recv_sem=recv, device_id=peer, device_id_type=MESH
    )


class Gather:
    def __init__(self, place, full, rows, send, recv):
        self.p, self.full, self.rows = place, full, rows
        self.send, self.recv = send, recv
        self.gr = place.chain * rows
        self.sent = []

    def region(self, s):
        return self.full.at[pl.ds(pl.multiple_of(s * self.gr, self.gr), self.gr)]

    def piece(self, s, z):
        start = pl.multiple_of(s * self.gr + z * self.rows, self.rows)
        return self.full.at[pl.ds(start, self.rows)]

    def go(self, k, ref, peer):
        copy = remote(ref, ref, self.send.at[k], self.recv.at[k], peer)
        copy.start()
        self.sent.append(copy)

    def got(self, k, ref):
        remote(ref, ref, self.send.at[k], self.recv.at[k], self.p.dev(self.p.sib)).wait_recv()

    def sides(self, k):
        p = self.p
        piece = self.piece(p.s, p.zflip(k))
        self.go(3 + k, piece, p.dev(p.xs))
        self.go(7 + k, piece, p.dev(p.ys))

    def start(self):
        p = self.p
        for k in range(1, p.chain):
            self.go(k - 1, self.piece(p.s, p.z), p.dev(p.s, p.zflip(k)))

    def chain_piece(self, k):
        p = self.p
        if 0 < k < p.chain:
            self.got(k - 1, self.piece(p.s, p.zflip(k)))
            self.sides(k)
        if k == 3:
            self.go(19, self.region(p.s), p.dev(p.sib))

    def chain_done(self):
        for k in range(1, 4):
            self.chain_piece(k)

    def sides_done(self, part=(0, 1)):
        p = self.p
        middle = (p.chain + 1) // 2
        steps = [range(middle), range(middle, p.chain)]
        for k in [k for one in part for k in steps[one]]:
            self.got(3 + k, self.piece(p.xs, p.zflip(k)))
            if k < middle:
                self.go(11 + k, self.piece(p.xs, p.zflip(k)), p.dev(p.ys))
            self.got(7 + k, self.piece(p.ys, p.zflip(k)))
            if k >= middle:
                self.go(11 + k, self.piece(p.ys, p.zflip(k)), p.dev(p.xs))
        if part[-1] == 1:
            self.go(20, self.region(p.xs), p.dev(p.sib))
            self.go(21, self.region(p.ys), p.dev(p.sib))

    def corner_done(self):
        p = self.p
        for k in range(p.chain):
            self.got(11 + k, self.piece(p.ds, p.zflip(k)))
        self.go(22, self.region(p.ds), p.dev(p.sib))

    def done(self):
        p = self.p
        for k, s in ((19, p.s), (20, p.xs), (21, p.ys), (22, p.ds)):
            self.got(k, self.region(p.flip(s, 1)))

    def drain(self):
        for copy in self.sent:
            copy.wait_send()


GATHER_SEMS = 23


def by_rows(count, step, body):
    def trip(i, carry):
        body(pl.multiple_of(i * step, step))
        return carry

    lax.fori_loop(0, count // step, trip, 0)


class Scatter:
    def __init__(self, place, rows, flip, bufs, send, recv):
        self.p, self.rows, self.turned = place, rows, flip
        self.full, self.in2, self.stage, self.land, self.mine, self.zout, self.zin = bufs
        self.gr, self.cols = self.full.shape[2], self.full.shape[3]
        self.half = self.cols // 2
        self.step = 16
        self.send, self.recv = send, recv
        self.sent = []

    def go(self, k, src, dst, peer):
        copy = remote(src, dst, self.send.at[k], self.recv.at[k], peer)
        copy.start()
        self.sent.append(copy)

    def got(self, k, ref):
        remote(ref, ref, self.send.at[k], self.recv.at[k], self.p.dev(self.p.sib)).wait_recv()

    def near(self, bits):
        g = self.p.group
        for bit in (1, 2):
            if bits & bit:
                g = Place.flip(g, bit)
        return g

    def cut(self, ref, slot, which):
        return ref.at[slot, :, pl.ds(which * self.half, self.half)]

    def both(self, g, rows, cols):
        mine = self.full[g, self.p.core, rows, cols].astype(jnp.float32)
        return mine + self.in2[g, rows, cols].astype(jnp.float32)

    def start(self):
        self.go(0, self.full.at[:, 1 - self.p.core], self.in2, self.p.dev(self.p.sib))

    def start_group(self, g):
        self.go(10 + g, self.full.at[g, 1 - self.p.core], self.in2.at[g], self.p.dev(self.p.sib))

    def core_done(self):
        self.core_far()
        self.core_near()

    def core_far(self):
        p, step = self.p, self.step
        if self.turned:
            for g in range(4):
                self.got(10 + g, self.in2.at[g])
        else:
            self.got(0, self.in2)
        far = self.near(3)
        whole = pl.ds(0, self.cols)

        def sum_far(i):
            rows = pl.ds(i, step)
            self.stage[0, rows] = self.both(far, rows, whole).astype(jnp.bfloat16)

        by_rows(self.gr, step, sum_far)
        self.go(1, self.cut(self.stage, 0, 0), self.cut(self.land, 0, 0), p.dev(p.xs))
        self.go(2, self.cut(self.stage, 0, 1), self.cut(self.land, 0, 1), p.dev(p.ys))

    def core_near(self):
        p, step = self.p, self.step
        xg, yg = self.near(1), self.near(2)
        first, second = pl.ds(0, self.half), pl.ds(self.half, self.half)

        def sum_sides(i):
            rows = pl.ds(i, step)
            self.stage[1, rows, first] = self.both(xg, rows, first).astype(jnp.bfloat16)
            self.stage[2, rows, second] = self.both(yg, rows, second).astype(jnp.bfloat16)

        by_rows(self.gr, step, sum_sides)
        self.go(3, self.cut(self.stage, 1, 0), self.cut(self.land, 1, 0), p.dev(p.xs))
        self.go(4, self.cut(self.stage, 2, 1), self.cut(self.land, 2, 1), p.dev(p.ys))

    def sides_done(self):
        p, step = self.p, self.step
        for k, slot, which, bits, peer in ((5, 2, 0, 2, p.ys), (6, 1, 1, 1, p.xs)):
            self.got(k - 4, self.cut(self.land, 0, which))
            cols = pl.ds(which * self.half, self.half)
            g = self.near(bits)

            def add(i, slot=slot, cols=cols, g=g):
                rows = pl.ds(i, step)
                total = self.both(g, rows, cols) + self.land[0, rows, cols].astype(jnp.float32)
                self.stage[slot, rows, cols] = total.astype(jnp.bfloat16)

            by_rows(self.gr, step, add)
            self.go(k, self.cut(self.stage, slot, which), self.cut(self.land, slot, which), p.dev(peer))

    def mine_done(self):
        p, step = self.p, self.step
        me = p.group
        for k, slot, which in ((3, 1, 0), (4, 2, 1), (5, 2, 0), (6, 1, 1)):
            self.got(k, self.cut(self.land, slot, which))

        def total(rows, cols):
            sides = self.land[1, rows, cols].astype(jnp.float32)
            sides = sides + self.land[2, rows, cols].astype(jnp.float32)
            return self.both(me, rows, cols) + sides

        if self.turned:

            def turn(i):
                cols = pl.ds(pl.multiple_of(i, 128), 128)
                value = total(pl.ds(0, self.gr), cols).T
                self.mine[cols] = value
                self.zout[cols] = value.astype(jnp.bfloat16)

            by_rows(self.cols, 128, turn)
        else:

            def add(i):
                rows = pl.ds(i, step)
                value = total(rows, pl.ds(0, self.cols))
                self.mine[rows] = value
                self.zout[rows] = value.astype(jnp.bfloat16)

            by_rows(self.gr, step, add)
        for k in range(1, p.chain):
            z = p.zpeer(k)
            src = self.zout.at[pl.ds(pl.multiple_of(z * self.rows, self.rows), self.rows)]
            dst = self.zin.at[pl.ds((k - 1) * self.rows, self.rows)]
            self.go(6 + k, src, dst, p.dev(p.s, z))

    def done(self, result):
        p, step = self.p, self.step
        for k in range(1, p.chain):
            self.got(6 + k, self.zin.at[pl.ds((k - 1) * self.rows, self.rows)])
        start = p.z * self.rows

        def add(i):
            value = self.mine[pl.ds(pl.multiple_of(start + i, step), step)]
            for k in range(1, p.chain):
                value = value + self.zin[pl.ds((k - 1) * self.rows + i, step)].astype(jnp.float32)
            result(i, value)

        by_rows(self.rows, step, add)

    def drain(self):
        for copy in self.sent:
            copy.wait_send()


SCATTER_SEMS = 14


def scatter_scratch(chain, rows, cols, flip):
    f32, bf16 = jnp.float32, jnp.bfloat16
    gr = chain * rows
    block = (cols, gr) if flip else (gr, cols)
    return [
        pltpu.VMEM((4, 2) + block, bf16),
        pltpu.VMEM((4,) + block, bf16),
        pltpu.VMEM((3,) + block, bf16),
        pltpu.VMEM((3,) + block, bf16),
        pltpu.VMEM((gr, cols), f32),
        pltpu.VMEM((gr, cols), bf16),
        pltpu.VMEM((max(1, chain - 1) * rows, cols), bf16),
    ]


class Exchange:
    def __init__(self, place, land, send, recv):
        self.p, self.land, self.send, self.recv = place, land, send, recv
        self.sent = []

    def go(self, source):
        p = self.p
        for d in range(1, 8):
            peer = lax.rem(p.s + d, 8)
            copy = remote(
                source(peer), self.land.at[p.s], self.send.at[d - 1], self.recv.at[d - 1], p.dev(peer)
            )
            copy.start()
            self.sent.append(copy)

    def wait(self):
        p = self.p
        for d in range(1, 8):
            ref = self.land.at[lax.rem(p.s + 8 - d, 8)]
            remote(ref, ref, self.send.at[d - 1], self.recv.at[d - 1], p.dev(p.sib)).wait_recv()

    def drain(self):
        for copy in self.sent:
            copy.wait_send()


def dot_nn(a, b):
    return lax.dot_general(a, b, (((1,), (0,)), ((), ())), preferred_element_type=jnp.float32)


def dot_nt(a, b):
    return lax.dot_general(a, b, (((1,), (1,)), ((), ())), preferred_element_type=jnp.float32)


def dot_tn(a, b):
    return lax.dot_general(a, b, (((0,), (0,)), ((), ())), preferred_element_type=jnp.float32)


def total_of(values):
    return jnp.sum(jnp.sum(values, 1, keepdims=True), 0, keepdims=True)


def fold_rows(values):
    rows, cols = values.shape
    return jnp.sum(values.reshape(rows // 8, 8, cols), 0)


NEG = -1e30
ORDER = ("norm", "qkv", "out", "up", "down")
SUMS = (("norm", 16, 256), ("q", 16, 512), ("k", 16, 512), ("v", 16, 512), ("out", 16, 512), ("up0", 16, 512), ("up1", 16, 512), ("up2", 16, 512), ("up3", 16, 512), ("down", 64, 512))
LEFT = math.sqrt(2.0 / math.pi)
CUBE = 0.044715


def layer_kernel(chain, rate, names, *refs):
    r = dict(zip(names, refs))
    f32, bf16 = jnp.float32, jnp.bfloat16
    place = Place(chain)
    x_ref, dy_ref, docs_ref = r["tokens"], r["grad"], r["docs"]
    rows_all, width = x_ref.shape
    arrive = [
        pltpu.make_async_copy(r["h_tokens"], x_ref, r["isem"].at[0]),
        pltpu.make_async_copy(r["h_grad"], dy_ref, r["isem"].at[1]),
    ]
    for copy in arrive:
        copy.start()
    span, spans = SPAN, rows_all // SPAN
    pairs = width // 128
    hidden_size = r["s_up"].shape[1]
    devices = 8 * chain
    per = width // devices
    entries = 8 * spans * width
    chunk = 256
    chunks = rows_all // chunk

    gathers = {}
    r["npad"][...] = jnp.zeros_like(r["npad"])
    r["npad"][0:4, 0:per] = r["s_norm"][...]
    past_cols, mid_cols = 2 * width, width
    w_past = r["w_first"].at[:, 0:past_cols]
    w_norm = r["w_first"].at[:, past_cols : past_cols + 128]
    w_query = r["w_query"]
    w_out, w_up = r["w_mid"].at[:, 0:mid_cols], r["w_mid"].at[:, mid_cols : mid_cols + hidden_size]
    w_down = r["w_down"]
    r["past"] = r["s_qkv"].at[:, width : 3 * width]
    r["query"] = r["s_qkv"].at[:, 0:width]
    for m, (name, parts) in enumerate(
        (
            ("first", ("past", "npad")),
            ("query", ("query",)),
            ("mid", ("s_out", "s_up")),
            ("down", ("s_down",)),
        )
    ):
        piece = r[parts[0]].shape[0]
        g = Gather(place, r["w_" + name], piece, r["gsend"].at[m], r["grecv"].at[m])
        own, start = g.piece(place.s, place.z), 0
        for part in parts:
            cols = r[part].shape[1]
            own[:, start : start + cols] = r[part][...].astype(bf16)
            start += cols
        gathers[name] = g
    scatters = {}
    for m, (name, piece, _) in enumerate(SUMS):
        bufs = [r[f"c_{name}{i}"] for i in range(7)]
        scatters[name] = Scatter(
            place, piece, name == "down", bufs, r["csend"].at[m], r["crecv"].at[m]
        )
    first = Exchange(place, r["summ"], r["esend"].at[0], r["erecv"].at[0])
    second = Exchange(place, r["back"], r["esend"].at[1], r["erecv"].at[1])
    first_values = Exchange(place, r["summ_value"], r["esend"].at[2], r["erecv"].at[2])
    second_sums = Exchange(place, r["back_sums"], r["esend"].at[3], r["erecv"].at[3])
    place.barrier()
    for name in ("first", "query"):
        gathers[name].start()
    for name in ("first", "query", "mid"):
        gathers[name].sides(0)

    F, D, mixed, heads = r["F"], r["D"], r["mixed"], r["heads"]
    loads = []
    for name in ORDER:
        for kind in ("m_", "a_"):
            sem = r["lsem"].at[len(loads)]
            loads.append(pltpu.make_async_copy(r[kind + name], r["v" + kind + name], sem))
            loads[-1].start()

    def advance_rows(name, rows, cols, total):
        scaled = rate * total
        moment = 0.9 * r["vm_" + name][rows, cols] + scaled
        weight = r["s_" + name][rows, cols] - (scaled + 0.9 * moment)
        average = 0.99 * r["va_" + name][rows, cols] + 0.01 * weight
        for k, value in enumerate((weight, moment, average)):
            r["t_" + name][k, rows, cols] = value

    def update(name, start):
        def rows_done(i, total):
            advance_rows(name, pl.ds(i, 16), slice(start, start + total.shape[1]), total)

        return rows_done

    def update_norm(i, total):
        advance_rows("norm", slice(0, 4), slice(0, per), total[0:4, 0:per])

    def norm_one(i):
        rows = pl.ds(i, 128)
        values = x_ref[rows].astype(f32)
        centre = values - jnp.mean(values, -1, keepdims=True)
        spread = jnp.mean(centre * centre, -1, keepdims=True)
        inv = lax.rsqrt(spread + 1e-05)
        F[rows] = centre * inv
        r["inv1"][rows] = jnp.broadcast_to(inv, (128, 128))

    for copy in arrive:
        copy.wait()
    by_rows(rows_all // 2, 128, norm_one)
    gathers["first"].chain_done()
    gathers["mid"].start()
    lax.fori_loop(rows_all // 256, rows_all // 128, lambda i, c: (norm_one(i * 128), c)[1], 0)

    ids = r["doc_ids"]
    docs = jnp.concatenate([ids[0:1, p * span : p * span + span] for p in range(spans)], 0).astype(f32)
    docs_ref[...] = docs
    wide = jnp.concatenate([docs] * (128 // spans), 0).T
    for p in range(spans):
        r["dcol"][pl.ds(p * span, span)] = jnp.broadcast_to(wide[:, p : p + 1], (span, 128))

    gathers["query"].chain_done()
    gathers["down"].start()
    gathers["first"].sides_done()
    gathers["query"].sides_done()
    gathers["mid"].chain_piece(1)

    def turn_grad(i):
        rows = pl.ds(pl.multiple_of(i, 128), 128)
        r["dyT"][:, rows] = dy_ref[rows].T

    gathers["first"].corner_done()
    gathers["first"].done()
    gathers["mid"].chain_piece(2)

    place_row = lax.broadcasted_iota(jnp.int32, (128, width), 0)
    place_col = lax.broadcasted_iota(jnp.int32, (128, width), 1)
    pick = ((place_col & (per - 1)) == place_row).astype(f32).astype(bf16)
    owner_row = lax.shift_right_logical(
        lax.broadcasted_iota(jnp.int32, (16 * devices, width), 0), 4
    )
    owner_col = lax.shift_right_logical(
        lax.broadcasted_iota(jnp.int32, (16 * devices, width), 1), per.bit_length() - 1
    )
    spread_rows = dot_nn(w_norm[...], pick)
    spread_rows = jnp.where(owner_row == owner_col, spread_rows, 0.0)
    norm_rows = jnp.sum(spread_rows.reshape(devices, 16, width), 0)
    r["nrows"][...] = norm_rows


    def project(i):
        rows = pl.ds(pl.multiple_of(i, chunk), chunk)
        act = (F[rows] * r["nrows"][0:1] + r["nrows"][1:2]).astype(bf16)
        r["act1T"][:, rows] = act.T
        mixed[rows, width : 3 * width] = dot_nn(act, w_past[...]).astype(bf16)
        r["act2"][rows] = act

    by_rows(rows_all, chunk, project)

    last_doc = docs[:, span - 1 : span]
    member = (docs == last_doc).astype(f32)
    count = jnp.sum(member, 1, keepdims=True)
    which = lax.broadcasted_iota(jnp.int32, (spans, span), 0)
    blocks = [jnp.where(which == p, member, 0.0) for p in range(spans)]
    left = jnp.concatenate(blocks, 1)
    left = jnp.concatenate([left, jnp.zeros_like(left)], 0).astype(bf16)
    means = dot_nn(left, mixed[:, width : 3 * width])[:spans] / count
    summ = r["summ"]
    summ[place.s, :, 0:width] = means[:, :width]
    summ[place.s, :, width : width + 128] = jnp.broadcast_to(last_doc, (spans, 128))
    r["summ_value"][place.s] = means[:, width:].astype(bf16)
    first.go(lambda peer: summ.at[place.s])
    first_values.go(lambda peer: r["summ_value"].at[place.s])
    gathers["query"].corner_done()
    gathers["mid"].chain_piece(3)
    gathers["mid"].sides_done((0,))
    gathers["query"].done()

    def project_query(i):
        rows = pl.ds(pl.multiple_of(i, chunk), chunk)
        mixed[rows, 0:width] = (dot_nn(r["act2"][rows], w_query[...]) * 0.125).astype(bf16)

    by_rows(rows_all, chunk, project_query)
    by_rows(rows_all, 128, turn_grad)
    first.wait()
    first_values.wait()
    gathers["mid"].sides_done((1,))
    gathers["down"].sides(0)

    sums = summ[...].reshape(8 * spans, width + 128)
    sum_values = r["summ_value"][...].astype(f32).reshape(8 * spans, width)
    keys = sums[:, :width]
    stat_mean = total_of(keys) / entries
    centred = keys - stat_mean
    stat_var = total_of(centred * centred) / entries
    inv_sum = lax.rsqrt(stat_var + 1e-05)
    key_norm = centred * inv_sum
    r["knorm"][...] = key_norm
    lane = lax.broadcasted_iota(jnp.int32, (span, 128), 1)
    low_half = lane < 64
    lane_row = lax.broadcasted_iota(jnp.int32, (1, 128), 1)
    pick0 = (lane_row < 64).astype(f32).astype(bf16)
    pick1 = (lane_row >= 64).astype(f32).astype(bf16)
    for j in range(pairs):
        cols = slice(128 * j, 128 * j + 128)
        part = key_norm[:, cols].astype(bf16)
        r["KR"][j] = jnp.concatenate([part * pick0, part * pick1], 0)
        part = sum_values[:, cols].astype(bf16)
        r["VR"][j] = jnp.concatenate([part * pick0, part * pick1], 0)
    last = sums[:, width:]
    r["lastrow"][...] = jnp.concatenate([last, last], 0).T[0:8]

    probs = r["probs"]
    causal = lax.broadcasted_iota(jnp.int32, (span, 128), 0) >= lax.broadcasted_iota(
        jnp.int32, (span, 128), 1
    )
    span_first = place.s * spans
    quarter = spans // 4

    def attend(p, carry):
        rows = pl.ds(pl.multiple_of(p * span, span), span)
        column = r["dcol"][rows]
        mask_local = (column == docs_ref[pl.ds(p, 1)]) & causal
        mask_remote = (column == r["lastrow"][0:1]) & (lax.rem(lane, 64) < span_first + p)
        scores, lows = [], []
        for j in range(pairs):
            query = mixed[rows, 128 * j : 128 * j + 128]
            key = mixed[rows, width + 128 * j : width + 128 * j + 128]
            scores.append(dot_nt(query, jnp.concatenate([key * pick0, key * pick1, r["KR"][j]], 0)))
        for j in range(pairs):
            one = jnp.where(mask_local, scores[j][:, :128], NEG)
            two = jnp.where(mask_local, scores[j][:, 128:256], NEG)
            far = jnp.where(mask_remote, scores[j][:, 256:], NEG)
            peak1 = jnp.max(jnp.maximum(one, jnp.where(low_half, far, NEG)), -1, keepdims=True)
            peak2 = jnp.max(jnp.maximum(two, jnp.where(low_half, NEG, far)), -1, keepdims=True)
            one = jnp.exp(one - peak1)
            two = jnp.exp(two - peak2)
            far = jnp.exp(far - jnp.where(low_half, peak1, peak2))
            scale1 = 1.0 / jnp.sum(one + jnp.where(low_half, far, 0.0), -1, keepdims=True)
            scale2 = 1.0 / jnp.sum(two + jnp.where(low_half, 0.0, far), -1, keepdims=True)
            one = one * scale1
            two = two * scale2
            far = far * jnp.where(low_half, scale1, scale2)
            base = 384 * j
            probs[rows, base : base + 128] = one
            probs[rows, base + 128 : base + 256] = two
            probs[rows, base + 256 : base + 384] = far
            lows.append(jnp.concatenate([one, two, far], 1).astype(bf16))
        for j in range(pairs):
            value = mixed[rows, 2 * width + 128 * j : 2 * width + 128 * j + 128]
            values = jnp.concatenate([value * pick0, value * pick1, r["VR"][j]], 0)
            heads[rows, 128 * j : 128 * j + 128] = dot_nn(lows[j], values).astype(bf16)
        return carry

    gathers["down"].chain_done()
    lax.fori_loop(0, 3 * quarter, attend, 0)
    gathers["mid"].corner_done()
    lax.fori_loop(3 * quarter, spans, attend, 0)
    gathers["mid"].done()

    r["ngrad"][...] = jnp.zeros_like(r["ngrad"])
    tile = 256

    def feed(i):
        rows = pl.ds(pl.multiple_of(i, chunk), chunk)
        part = heads[rows]
        r["headsT"][:, rows] = part.T
        after = x_ref[rows].astype(f32) + dot_nn(part, w_out[...])
        centre = after - jnp.mean(after, -1, keepdims=True)
        spread = jnp.mean(centre * centre, -1, keepdims=True)
        inv = lax.rsqrt(spread + 1e-05)
        normal = centre * inv
        F[rows] = after
        D[rows] = normal
        r["inv2"][rows] = jnp.broadcast_to(inv, (chunk, 128))
        act_two = (normal * r["nrows"][2:3] + r["nrows"][3:4]).astype(bf16)
        r["act2"][rows] = act_two
        r["act2T"][:, rows] = act_two.T

    lax.fori_loop(0, chunks // 2, lambda i, c: (feed(i * chunk), c)[1], 0)
    gathers["down"].sides_done()
    lax.fori_loop(chunks // 2, chunks, lambda i, c: (feed(i * chunk), c)[1], 0)
    gathers["down"].corner_done()
    gathers["down"].done()

    down, out = scatters["down"], scatters["out"]
    ups = [scatters[f"up{g}"] for g in range(4)]
    quad = hidden_size // 4

    def put(target, grad, cols):
        gr = target.gr
        for g in range(4):
            for c in range(2):
                k = (2 * g + c) * gr
                target.full[g, c, :, cols] = grad[k : k + gr]

    for g in range(4):

        def mlp(i, g=g):
            parts = [
                (pl.ds(pl.multiple_of(i + top, chunk), chunk), slice(start, start + tile))
                for top in (0, chunk)
                for start in range(g * quad, g * quad + quad, tile)
            ]
            waiting = []
            for step in range(len(parts) + 1):
                if step < len(parts):
                    rows, cols = parts[step]
                    h = dot_nn(r["act2"][rows], w_up[:, cols])
                    d = dot_nt(dy_ref[rows], w_down[cols])
                    waiting.append((rows, cols, h, d))
                if step:
                    rows, cols, h, d = waiting[step - 1]
                    square = h * h
                    gate = 0.5 + 0.5 * jnp.tanh(h * (LEFT + (LEFT * CUBE) * square))
                    act = h * gate
                    r["act3"][rows, cols] = act.astype(bf16)
                    slope = gate + act * (2.0 * LEFT + (6.0 * LEFT * CUBE) * square) * (1.0 - gate)
                    r["dhid"][rows, cols] = (d * slope).astype(bf16)

        by_rows(rows_all, 2 * chunk, mlp)
        if g:
            ups[g - 1].core_done()
        if g > 1:
            ups[g - 2].sides_done()
        grad = dot_nn(r["dyT"][...], r["act3"][:, g * quad : g * quad + quad]).astype(bf16)
        down.full[g, 0] = grad[:, : quad // 2]
        down.full[g, 1] = grad[:, quad // 2 :]
        down.start_group(g)
        grad = dot_nn(r["act2T"][...], r["dhid"][:, g * quad : g * quad + quad]).astype(bf16)
        put(ups[g], grad, pl.ds(0, quad))
        ups[g].start()

    def feed_back(i):
        rows = pl.ds(pl.multiple_of(i, chunk), chunk)
        d_two = dot_nt(r["dhid"][rows], w_up[...])
        normal = D[rows]
        r["ngrad"][2] += fold_rows(d_two * normal)
        r["ngrad"][3] += fold_rows(d_two)
        scaled = d_two * r["nrows"][2:3]
        centred = (
            scaled
            - jnp.mean(scaled, -1, keepdims=True)
            - normal * jnp.mean(scaled * normal, -1, keepdims=True)
        )
        d_after = dy_ref[rows].astype(f32) + r["inv2"][rows][:, 0:1] * centred
        D[rows] = d_after
        low = d_after.astype(bf16)
        r["dafter"][rows] = low
        heads[rows] = dot_nt(low, w_out[...]).astype(bf16)

    lax.fori_loop(0, chunks // 2, lambda i, c: (feed_back(i * chunk), c)[1], 0)
    ups[3].core_done()
    ups[2].sides_done()
    down.core_done()
    lax.fori_loop(chunks // 2, chunks, lambda i, c: (feed_back(i * chunk), c)[1], 0)
    ups[3].sides_done()
    put(out, dot_nn(r["headsT"][...], r["dafter"][...]).astype(bf16), pl.ds(0, width))
    out.start()

    kept = r["dhid"]
    side = 384 * pairs

    def attend_back(p, carry):
        rows = pl.ds(pl.multiple_of(p * span, span), span)
        wide_probs, d_scores, stacks = [], [], []
        for j in range(pairs):
            key = mixed[rows, width + 128 * j : width + 128 * j + 128]
            value = mixed[rows, 2 * width + 128 * j : 2 * width + 128 * j + 128]
            stacks.append(jnp.concatenate([key * pick0, key * pick1, r["KR"][j]], 0))
            values_all = jnp.concatenate([value * pick0, value * pick1, r["VR"][j]], 0)
            wide_probs.append(dot_nt(heads[rows, 128 * j : 128 * j + 128], values_all))
        for j in range(pairs):
            d_probs = wide_probs[j]
            base = 384 * j
            one = probs[rows, base : base + 128]
            two = probs[rows, base + 128 : base + 256]
            far = probs[rows, base + 256 : base + 384]
            d_far = far * d_probs[:, 256:]
            sum1 = jnp.sum(one * d_probs[:, :128] + jnp.where(low_half, d_far, 0.0), -1, keepdims=True)
            sum2 = jnp.sum(two * d_probs[:, 128:256] + jnp.where(low_half, 0.0, d_far), -1, keepdims=True)
            d_one = one * (d_probs[:, :128] - sum1)
            d_two = two * (d_probs[:, 128:256] - sum2)
            d_far = far * (d_probs[:, 256:] - jnp.where(low_half, sum1, sum2))
            d_scores.append(jnp.concatenate([d_one, d_two, d_far], 1).astype(bf16))
            kept[rows, base : base + 384] = d_scores[j]
            kept[rows, side + 128 * j : side + 128 * j + 128] = far.astype(bf16)
        for j in range(pairs):
            at = slice(128 * j, 128 * j + 128)
            r["act2"][rows, at] = (0.125 * dot_nn(d_scores[j], stacks[j])).astype(bf16)
        return carry

    lax.fori_loop(0, quarter, attend_back, 0)
    ups[0].mine_done()
    lax.fori_loop(quarter, 2 * quarter, attend_back, 0)
    ups[1].mine_done()
    lax.fori_loop(2 * quarter, 3 * quarter, attend_back, 0)
    ups[2].mine_done()
    lax.fori_loop(3 * quarter, spans, attend_back, 0)

    half_spans = 8 * spans
    parts = []
    for name in ("key", "value"):
        for j in range(pairs):
            at = slice(128 * j, 128 * j + 128)
            if name == "key":
                both = dot_tn(kept[:, 384 * j + 256 : 384 * j + 384], mixed[:, at])
            else:
                both = dot_tn(kept[:, side + 128 * j : side + 128 * j + 128], heads[:, at])
            low = low_half[:half_spans]
            parts.append(jnp.where(low, both[:half_spans], both[half_spans:]))
    d_keys = jnp.concatenate(parts[:pairs], 1)
    d_values = jnp.concatenate(parts[pairs:], 1)
    key_norm = r["knorm"][...]
    flat = jnp.where(lane_row < 64, total_of(d_keys), total_of(d_keys * key_norm))
    send = r["sendback"]
    send[:, :, 0:width] = d_keys.reshape(8, spans, width).astype(bf16)
    send[:, :, width : 2 * width] = d_values.reshape(8, spans, width).astype(bf16)
    back, back_sums = r["back"], r["back_sums"]
    back[place.s] = send[place.s]
    back_sums[place.s] = jnp.broadcast_to(flat, (spans, 128))
    second.go(lambda peer: send.at[peer])
    second_sums.go(lambda peer: back_sums.at[place.s])

    q_sum, k_sum, v_sum = scatters["q"], scatters["k"], scatters["v"]
    put(q_sum, dot_nn(r["act1T"][...], r["act2"][...]).astype(bf16), pl.ds(0, width))
    q_sum.start()
    out.core_done()
    down.sides_done()
    ups[3].mine_done()

    def local_back(p, carry):
        rows = pl.ds(pl.multiple_of(p * span, span), span)
        d_keys, d_values = [], []
        for j in range(pairs):
            at = slice(128 * j, 128 * j + 128)
            low = probs[rows, 384 * j : 384 * j + 256].astype(bf16)
            d_keys.append(dot_tn(kept[rows, 384 * j : 384 * j + 256], mixed[rows, at]))
            d_values.append(dot_tn(low, heads[rows, at]))
        for j in range(pairs):
            at = slice(128 * j, 128 * j + 128)
            probs[rows, at] = jnp.where(low_half, d_keys[j][:128], d_keys[j][128:])
            past = slice(width + 128 * j, width + 128 * j + 128)
            probs[rows, past] = jnp.where(low_half, d_values[j][:128], d_values[j][128:])
        return carry

    lax.fori_loop(0, 2 * quarter, local_back, 0)
    out.sides_done()
    q_sum.core_done()
    lax.fori_loop(2 * quarter, spans, local_back, 0)
    second.wait()
    second_sums.wait()

    owned = jnp.sum(back[...].astype(f32), 0)
    flat = jnp.sum(back_sums[...], 0)
    back_sum, back_cross = flat[0:1, 0:1], flat[0:1, 64:65]
    mine_norm = r["knorm"][pl.ds(pl.multiple_of(place.s * spans, spans), spans)]
    d_sum_key = inv_sum * (
        owned[:, :width] - back_sum * (1.0 / entries) - mine_norm * (back_cross * (1.0 / entries))
    )
    r["dsum"][:, 0:width] = d_sum_key / count
    r["dsum"][:, width : 2 * width] = owned[:, width : 2 * width] / count
    slot = lax.broadcasted_iota(jnp.int32, (8, 128), 1)
    stats = jnp.where(slot == 0, stat_mean, stat_var)
    stats = jnp.where(slot == 2, -inv_sum * back_sum, stats)
    stats = jnp.where(slot == 3, -0.5 * inv_sum * inv_sum * back_cross, stats)
    r["stats"][...] = stats

    def join(p, carry):
        rows = pl.ds(pl.multiple_of(p * span, span), span)
        final = docs_ref[pl.ds(p, 1)][:, span - 1 : span]
        share = (r["dcol"][rows] == final).astype(f32)
        sums_row = r["dsum"][pl.ds(p, 1)]
        for j in range(pairs):
            at = slice(128 * j, 128 * j + 128)
            past = slice(width + 128 * j, width + 128 * j + 128)
            full = probs[rows, at] + share * sums_row[:, at]
            mixed[rows, past] = full.astype(bf16)
            full = probs[rows, past] + share * sums_row[:, past]
            mixed[rows, 2 * width + 128 * j : 2 * width + 128 * j + 128] = full.astype(bf16)
        return carry

    lax.fori_loop(0, spans, join, 0)

    put(k_sum, dot_nn(r["act1T"][...], mixed[:, width : 2 * width]).astype(bf16), pl.ds(0, width))
    k_sum.start()
    put(v_sum, dot_nn(r["act1T"][...], mixed[:, 2 * width :]).astype(bf16), pl.ds(0, width))
    v_sum.start()

    def first_back(i):
        rows = pl.ds(pl.multiple_of(i, chunk), chunk)
        d_one = dot_nt(r["act2"][rows], w_query[...])
        d_one = d_one + dot_nt(mixed[rows, width : 3 * width], w_past[...])
        values = x_ref[rows].astype(f32)
        inv = r["inv1"][rows][:, 0:1]
        normal = (values - jnp.mean(values, -1, keepdims=True)) * inv
        r["ngrad"][0] += fold_rows(d_one * normal)
        r["ngrad"][1] += fold_rows(d_one)
        scaled = d_one * r["nrows"][0:1]
        centred = (
            scaled
            - jnp.mean(scaled, -1, keepdims=True)
            - normal * jnp.mean(scaled * normal, -1, keepdims=True)
        )
        r["input_grad"][rows] = D[rows] + inv * centred

    half_chunks = chunks // 2
    lax.fori_loop(0, half_chunks, lambda i, c: (first_back(i * chunk), c)[1], 0)
    k_sum.core_far()
    v_sum.core_far()
    k_sum.core_near()
    v_sum.core_near()
    q_sum.sides_done()
    down.mine_done()
    out.mine_done()
    lax.fori_loop(half_chunks, chunks, lambda i, c: (first_back(i * chunk), c)[1], 0)

    pieces = jnp.concatenate(
        [jnp.sum(r["ngrad"][k], 0, keepdims=True) for k in range(4)]
        + [jnp.zeros((12, width), f32)],
        0,
    )
    spread_rows = jnp.broadcast_to(pieces[None], (devices, 16, width)).reshape(16 * devices, width)
    spread_rows = jnp.where(owner_row == owner_col, spread_rows, 0.0).astype(bf16)
    norm = scatters["norm"]
    narrow = dot_nt(spread_rows, pick).astype(bf16)
    put(norm, jnp.concatenate([narrow, jnp.zeros_like(narrow)], 1), pl.ds(0, 256))
    norm.start()

    def output(i):
        rows = pl.ds(pl.multiple_of(i, chunk), chunk)
        result = F[rows] + dot_nn(r["act3"][rows], w_down[...])
        r["block_out"][rows] = result.astype(bf16)

    lax.fori_loop(0, half_chunks, lambda i, c: (output(i * chunk), c)[1], 0)
    norm.core_done()
    k_sum.sides_done()
    v_sum.sides_done()
    q_sum.mine_done()
    lax.fori_loop(half_chunks, chunks, lambda i, c: (output(i * chunk), c)[1], 0)
    norm.sides_done()
    k_sum.mine_done()
    v_sum.mine_done()
    for copy in loads:
        copy.wait()
    for g in range(4):
        ups[g].done(update("up", g * quad))
    for name in ("down", "out"):
        scatters[name].done(update(name, 0))
    norm.mine_done()
    q_sum.done(update("qkv", 0))
    k_sum.done(update("qkv", width))
    v_sum.done(update("qkv", 2 * width))
    norm.done(update_norm)
    for part in list(gathers.values()) + list(scatters.values()) + [first, first_values, second, second_sums]:
        part.drain()


def fused_layer(chain, rate, tokens, grad, doc_ids, shards, moments, averages):
    f32, bf16 = jnp.float32, jnp.bfloat16
    rows, width = tokens.shape
    spans = rows // SPAN
    order = ORDER
    devices = 8 * chain
    ins = [("h_tokens", tokens), ("h_grad", grad), ("doc_ids", doc_ids)]
    ins += [("s_" + name, shards[name]) for name in order]
    ins += [("m_" + name, moments[name]) for name in order]
    ins += [("a_" + name, averages[name]) for name in order]
    outs = [
        ("block_out", pltpu.VMEM((rows, width), bf16)),
        ("input_grad", pltpu.VMEM((rows, width), f32)),
        ("stats", pltpu.VMEM((8, 128), f32)),
    ]
    outs += [("t_" + name, pltpu.VMEM((3,) + shards[name].shape, f32)) for name in order]
    hidden = shards["up"].shape[1]
    scratch = {}
    down_rows = shards["down"].shape[0]
    scratch["w_first"] = pltpu.VMEM((devices * 16, 2 * width + 128), bf16)
    scratch["w_query"] = pltpu.VMEM((devices * 16, width), bf16)
    scratch["w_mid"] = pltpu.VMEM((devices * 16, width + hidden), bf16)
    scratch["w_down"] = pltpu.VMEM((devices * down_rows, width), bf16)
    for name, piece, cols in SUMS:
        for i, buf in enumerate(scatter_scratch(chain, piece, cols, name == "down")):
            scratch[f"c_{name}{i}"] = buf
    for name in order:
        scratch["vm_" + name] = pltpu.VMEM(shards[name].shape, f32)
        scratch["va_" + name] = pltpu.VMEM(shards[name].shape, f32)
    scratch["lsem"] = DMA((10,))
    pairs = width // 128
    scratch |= {
        "gsend": DMA((4, GATHER_SEMS)),
        "grecv": DMA((4, GATHER_SEMS)),
        "csend": DMA((10, SCATTER_SEMS)),
        "crecv": DMA((10, SCATTER_SEMS)),
        "esend": DMA((4, 7)),
        "erecv": DMA((4, 7)),
        "summ": pltpu.VMEM((8, spans, width + 128), f32),
        "summ_value": pltpu.VMEM((8, spans, width), bf16),
        "back": pltpu.VMEM((8, spans, 2 * width), bf16),
        "back_sums": pltpu.VMEM((8, spans, 128), f32),
        "sendback": pltpu.VMEM((8, spans, 2 * width), bf16),
        "F": pltpu.VMEM((rows, width), f32),
        "inv1": pltpu.VMEM((rows, 128), f32),
        "dcol": pltpu.VMEM((rows, 128), f32),
        "nrows": pltpu.VMEM((16, width), f32),
        "ngrad": pltpu.VMEM((4, 8, width), f32),
        "act1T": pltpu.VMEM((width, rows), bf16),
        "dyT": pltpu.VMEM((width, rows), bf16),
        "act2T": pltpu.VMEM((width, rows), bf16),
        "headsT": pltpu.VMEM((width, rows), bf16),
        "mixed": pltpu.VMEM((rows, 3 * width), bf16),
        "probs": pltpu.VMEM((rows, 384 * pairs), f32),
        "heads": pltpu.VMEM((rows, width), bf16),
        "knorm": pltpu.VMEM((8 * spans, width), f32),
        "KR": pltpu.VMEM((pairs, 128, 128), bf16),
        "VR": pltpu.VMEM((pairs, 128, 128), bf16),
        "lastrow": pltpu.VMEM((8, 128), f32),
        "isem": DMA((2,)),
        "tokens": pltpu.VMEM((rows, width), bf16),
        "grad": pltpu.VMEM((rows, width), bf16),
        "docs": pltpu.VMEM((spans, SPAN), f32),
        "npad": pltpu.VMEM((16, 128), f32),
        "inv2": pltpu.VMEM((rows, 128), f32),
        "act2": pltpu.VMEM((rows, width), bf16),
        "act3": pltpu.VMEM((rows, hidden), bf16),
        "dhid": pltpu.VMEM((rows, hidden), bf16),
        "dafter": pltpu.VMEM((rows, width), bf16),
        "D": pltpu.VMEM((rows, width), f32),
        "dsum": pltpu.VMEM((spans, 2 * width), f32),
    }
    names = [n for n, _ in ins] + [n for n, _ in outs] + list(scratch)
    vmem = pl.BlockSpec(memory_space=pltpu.VMEM)
    hbm = pl.BlockSpec(memory_space=pltpu.HBM)
    scratch_shapes = list(scratch.values())
    result = pl.pallas_call(
        functools.partial(layer_kernel, chain, rate, names),
        out_shape=[shape for _, shape in outs],
        in_specs=[hbm] * 2 + [vmem] * (len(ins) - 12) + [hbm] * 10,
        out_specs=[vmem] * len(outs),
        scratch_shapes=scratch_shapes,
        compiler_params=pltpu.CompilerParams(
            collective_id=0, has_side_effects=True, vmem_limit_bytes=59 * 2**20
        ),
    )(*[value for _, value in ins])
    return dict(zip([n for n, _ in outs], result))


def finish_kernel(count, *refs):
    ins, outs, sems = refs[:count], refs[count:-1], refs[-1]
    stats, two = ins[-1], outs[count - 1 :]
    copies = [pltpu.make_async_copy(ins[k], outs[k], sems.at[k]) for k in range(count - 1)]
    for copy in copies:
        copy.start()
    two[0][...] = stats[0:1, 0:2]
    two[1][...] = stats[0:1, 2:4]
    for copy in copies:
        copy.wait()


def finish(arrays, stats):
    vmem = pl.BlockSpec(memory_space=pltpu.VMEM)
    two = jax.ShapeDtypeStruct((1, 2), jnp.float32)
    count = len(arrays) + 1
    return pl.pallas_call(
        functools.partial(finish_kernel, count),
        out_shape=[jax.ShapeDtypeStruct(a.shape, a.dtype) for a in arrays] + [two, two],
        in_specs=[pl.BlockSpec(memory_space=pl.ANY)] * (count - 1) + [vmem],
        out_specs=[pl.BlockSpec(memory_space=pltpu.HBM)] * (count - 1) + [vmem] * 2,
        scratch_shapes=[DMA((count - 1,))],
        compiler_params=pltpu.CompilerParams(vmem_limit_bytes=2 * 2**20),
    )(*(pltpu.with_memory_space_constraint(a, pltpu.VMEM) for a in arrays), stats)


def norm_forward(values, gain_row, shift_row):
    centre = values - jnp.mean(values, -1, keepdims=True)
    spread = jnp.mean(centre * centre, -1, keepdims=True)
    inv_std = lax.rsqrt(spread + 1e-05)
    normal = centre * inv_std
    return (normal * gain_row + shift_row, normal, inv_std)


def norm_backward(grad_in, normal, inv_std, gain_row):
    scaled = grad_in * gain_row
    centred = (
        scaled
        - jnp.mean(scaled, -1, keepdims=True)
        - normal * jnp.mean(scaled * normal, -1, keepdims=True)
    )
    return (inv_std * centred, jnp.sum(grad_in * normal, 0), jnp.sum(grad_in, 0))


def gelu_tanh(values):
    return jax.nn.gelu(values, approximate=True)


def span_probs(query_blk, key_blk, key_remote, doc_span, last_remote, span_first):
    span_len = doc_span.shape[2]
    local = (
        jnp.einsum("bpqhe,bpkhe->bphqk", query_blk, key_blk, preferred_element_type=jnp.float32)
        * 0.125
    )
    remote = (
        jnp.einsum("bpqhe,bnhe->bphqn", query_blk, key_remote, preferred_element_type=jnp.float32)
        * 0.125
    )
    positions = jnp.arange(span_len)
    causal = positions[:, None] >= positions[None, :]
    same_doc = doc_span[:, :, :, None] == doc_span[:, :, None, :]
    mask_local = (same_doc & causal[None, None])[:, :, None]
    span_ids = span_first + jnp.arange(doc_span.shape[1])
    earlier = jnp.arange(key_remote.shape[1])[None, :] < span_ids[:, None]
    doc_float = doc_span.astype(jnp.float32)
    match = doc_float[:, :, :, None] == last_remote.astype(jnp.float32)[:, None, None, :]
    mask_remote = (match & earlier[None, :, None, :])[:, :, None]
    allowed = jnp.concatenate([mask_local, mask_remote], -1)
    scores = jnp.where(allowed, jnp.concatenate([local, remote], -1), -1e30)
    peak_score = jnp.max(scores, -1, keepdims=True)
    raised = jnp.exp(scores - peak_score)
    return raised / jnp.sum(raised, -1, keepdims=True)


def advance(weight, moment, average, grad, rate):
    new_moment = 0.9 * moment + rate * grad
    new_weight = weight - (rate * grad + 0.9 * new_moment)
    new_average = 0.99 * average + 0.01 * new_weight
    return jnp.stack([new_weight, new_moment, new_average])


def shards_plain(
    tokens,
    grad_out,
    doc_ids,
    qkv_w,
    qkv_m,
    qkv_a,
    out_w,
    out_m,
    out_a,
    up_w,
    up_m,
    up_a,
    down_w,
    down_m,
    down_a,
    norm_w,
    norm_m,
    norm_a,
):
    seqs, seq_len, width = tokens.shape
    span_len = SPAN
    cycle_size = lax.axis_size("seq")
    cycle_rank = lax.axis_index("seq")
    spans_dev = seq_len // span_len
    spans_all = spans_dev * cycle_size
    rows_dev = seqs * seq_len
    head_size = width // H
    bf16 = jnp.bfloat16
    f32 = jnp.float32
    w_qkv, w_out, w_up, w_down, norm_low = (
        lax.all_gather(qkv_w.astype(bf16), ("seq", "dp"), axis=0, tiled=True),
        lax.all_gather(out_w.astype(bf16), ("seq", "dp"), axis=0, tiled=True),
        lax.all_gather(up_w.astype(bf16), ("seq", "dp"), axis=0, tiled=True),
        lax.all_gather(down_w.astype(bf16), ("seq", "dp"), axis=0, tiled=True),
        lax.all_gather(norm_w.astype(bf16), ("seq", "dp"), axis=1, tiled=True),
    )
    norm_rows = norm_low.astype(f32)
    inputs = tokens.reshape(rows_dev, width).astype(f32)
    normed_one, normal_one, inv_one = norm_forward(inputs, norm_rows[0], norm_rows[1])
    act_one = normed_one.astype(bf16)
    mixed = jnp.dot(act_one, w_qkv, preferred_element_type=f32)
    query = mixed[:, :width].astype(bf16)
    key_all = mixed[:, width : 2 * width].astype(bf16)
    value_all = mixed[:, 2 * width :].astype(bf16)
    block_shape = (seqs, spans_dev, span_len, H, head_size)
    query_blk = query.reshape(block_shape)
    key_blk = key_all.reshape(block_shape)
    value_blk = value_all.reshape(block_shape)
    doc_span = doc_ids.reshape(seqs, spans_dev, span_len)
    last_doc = doc_span[:, :, -1]
    member = (doc_span == last_doc[:, :, None]).astype(f32)
    counts = jnp.sum(member, -1)
    member_low = member.astype(bf16)
    key_four = key_all.reshape(seqs, spans_dev, span_len, width)
    value_four = value_all.reshape(seqs, spans_dev, span_len, width)
    sum_key = (
        jnp.einsum("bpt,bptd->bpd", member_low, key_four, preferred_element_type=f32)
        / counts[..., None]
    )
    sum_value = (
        jnp.einsum("bpt,bptd->bpd", member_low, value_four, preferred_element_type=f32)
        / counts[..., None]
    )
    total_sum, total_square = lax.psum(
        (jnp.sum(sum_key, (1, 2)), jnp.sum(sum_key * sum_key, (1, 2))), "seq"
    )
    entries = spans_all * width
    stat_mean = total_sum / entries
    stat_var = total_square / entries - stat_mean * stat_mean
    inv_sum = lax.rsqrt(stat_var + 1e-05)
    key_norm = (sum_key - stat_mean[:, None, None]) * inv_sum[:, None, None]
    key_send = key_norm.astype(bf16)
    value_send = sum_value.astype(bf16)
    last_send = last_doc.astype(bf16)
    key_remote, value_remote, last_remote = (
        lax.all_gather(key_send, "seq", axis=1, tiled=True),
        lax.all_gather(value_send, "seq", axis=1, tiled=True),
        lax.all_gather(last_send, "seq", axis=1, tiled=True),
    )
    remote_shape = (seqs, spans_all, H, head_size)
    span_first = cycle_rank * spans_dev
    probs = span_probs(
        query_blk, key_blk, key_remote.reshape(remote_shape), doc_span, last_remote, span_first
    )
    probs_low = probs.astype(bf16)
    attended = jnp.einsum(
        "bphqk,bpkhe->bpqhe", probs_low[..., :span_len], value_blk, preferred_element_type=f32
    )
    attended = attended + jnp.einsum(
        "bphqn,bnhe->bpqhe",
        probs_low[..., span_len:],
        value_remote.reshape(remote_shape),
        preferred_element_type=f32,
    )
    heads_out = attended.reshape(rows_dev, width).astype(bf16)
    after_attn = inputs + jnp.dot(heads_out, w_out, preferred_element_type=f32)
    normed_two, normal_two, inv_two = norm_forward(after_attn, norm_rows[2], norm_rows[3])
    act_two = normed_two.astype(bf16)
    hidden = jnp.dot(act_two, w_up, preferred_element_type=f32)
    act_three = gelu_tanh(hidden).astype(bf16)
    result = after_attn + jnp.dot(act_three, w_down, preferred_element_type=f32)
    block_out = result.astype(bf16).reshape(seqs, seq_len, width)
    stats_out = jnp.stack([stat_mean, stat_var], -1)
    grad_low = grad_out.reshape(rows_dev, width)
    grad_down = jnp.einsum("tf,td->fd", act_three, grad_low, preferred_element_type=f32)
    d_three = jnp.einsum("td,fd->tf", grad_low, w_down, preferred_element_type=f32)
    unused_out, gelu_pull = jax.vjp(gelu_tanh, hidden)
    d_hidden = gelu_pull(d_three)[0].astype(bf16)
    grad_up = jnp.einsum("td,tf->df", act_two, d_hidden, preferred_element_type=f32)
    d_two = jnp.einsum("tf,df->td", d_hidden, w_up, preferred_element_type=f32)
    d_norm_two, gain_two, shift_two = norm_backward(d_two, normal_two, inv_two, norm_rows[2])
    d_after = grad_low.astype(f32) + d_norm_two
    d_after_low = d_after.astype(bf16)
    grad_outw = jnp.einsum("tc,td->cd", heads_out, d_after_low, preferred_element_type=f32)
    d_heads = jnp.einsum("td,cd->tc", d_after_low, w_out, preferred_element_type=f32).astype(bf16)
    key_back, value_back, last_back = (key_remote, value_remote, last_remote)
    key_back_blk = key_back.reshape(remote_shape)
    value_back_blk = value_back.reshape(remote_shape)
    probs_back = span_probs(query_blk, key_blk, key_back_blk, doc_span, last_back, span_first)
    probs_back_low = probs_back.astype(bf16)
    d_heads_blk = d_heads.reshape(block_shape)
    d_probs = jnp.concatenate(
        [
            jnp.einsum("bpqhe,bpkhe->bphqk", d_heads_blk, value_blk, preferred_element_type=f32),
            jnp.einsum(
                "bpqhe,bnhe->bphqn", d_heads_blk, value_back_blk, preferred_element_type=f32
            ),
        ],
        -1,
    )
    row_dot = jnp.sum(probs_back * d_probs, -1, keepdims=True)
    d_scores = (probs_back * (d_probs - row_dot)).astype(bf16)
    d_local = d_scores[..., :span_len]
    d_remote = d_scores[..., span_len:]
    d_query = 0.125 * (
        jnp.einsum("bphqk,bpkhe->bpqhe", d_local, key_blk, preferred_element_type=f32)
        + jnp.einsum("bphqn,bnhe->bpqhe", d_remote, key_back_blk, preferred_element_type=f32)
    )
    d_key = 0.125 * jnp.einsum("bphqk,bpqhe->bpkhe", d_local, query_blk, preferred_element_type=f32)
    d_value = jnp.einsum(
        "bphqk,bpqhe->bpkhe",
        probs_back_low[..., :span_len],
        d_heads_blk,
        preferred_element_type=f32,
    )
    d_key_sum = (
        0.125 * jnp.einsum("bphqn,bpqhe->bnhe", d_remote, query_blk, preferred_element_type=f32)
    ).reshape(seqs, spans_all, width)
    d_value_sum = jnp.einsum(
        "bphqn,bpqhe->bnhe", probs_back_low[..., span_len:], d_heads_blk, preferred_element_type=f32
    ).reshape(seqs, spans_all, width)
    owned_key, owned_value = (
        lax.psum_scatter(
            d_key_sum.astype(jnp.bfloat16), "seq", scatter_dimension=1, tiled=True
        ).astype(jnp.float32),
        lax.psum_scatter(
            d_value_sum.astype(jnp.bfloat16), "seq", scatter_dimension=1, tiled=True
        ).astype(jnp.float32),
    )
    back_sum, back_cross = lax.psum(
        (jnp.sum(owned_key, (1, 2)), jnp.sum(owned_key * key_norm, (1, 2))), "seq"
    )
    stat_grads = jnp.stack([-inv_sum * back_sum, -0.5 * inv_sum * inv_sum * back_cross], -1)
    d_sum_key = inv_sum[:, None, None] * (
        owned_key
        - back_sum[:, None, None] / entries
        - key_norm * back_cross[:, None, None] / entries
    )
    share = member / counts[..., None]
    d_key_all = (
        d_key.reshape(seqs, spans_dev, span_len, width)
        + share[..., None] * d_sum_key[:, :, None, :]
    )
    d_value_all = (
        d_value.reshape(seqs, spans_dev, span_len, width)
        + share[..., None] * owned_value[:, :, None, :]
    )
    d_mixed = jnp.concatenate(
        [
            d_query.reshape(rows_dev, width),
            d_key_all.reshape(rows_dev, width),
            d_value_all.reshape(rows_dev, width),
        ],
        -1,
    ).astype(bf16)
    grad_qkv = jnp.einsum("td,tf->df", act_one, d_mixed, preferred_element_type=f32)
    d_one = jnp.einsum("tf,df->td", d_mixed, w_qkv, preferred_element_type=f32)
    d_norm_one, gain_one, shift_one = norm_backward(d_one, normal_one, inv_one, norm_rows[0])
    input_grad = (d_after + d_norm_one).reshape(seqs, seq_len, width)
    grad_norm = jnp.stack([gain_one, shift_one, gain_two, shift_two])
    sum_qkv, sum_outw, sum_up, sum_down, sum_norm = (
        lax.psum_scatter(grad_qkv, ("seq", "dp"), scatter_dimension=0, tiled=True),
        lax.psum_scatter(grad_outw, ("seq", "dp"), scatter_dimension=0, tiled=True),
        lax.psum_scatter(grad_up, ("seq", "dp"), scatter_dimension=0, tiled=True),
        lax.psum_scatter(grad_down, ("seq", "dp"), scatter_dimension=0, tiled=True),
        lax.psum_scatter(grad_norm, ("seq", "dp"), scatter_dimension=1, tiled=True),
    )
    tokens_all = rows_dev * cycle_size * lax.axis_size("dp")
    rate = 0.02 / math.sqrt(tokens_all)
    return (
        block_out,
        input_grad,
        stats_out,
        stat_grads,
        advance(qkv_w, qkv_m, qkv_a, sum_qkv, rate),
        advance(out_w, out_m, out_a, sum_outw, rate),
        advance(up_w, up_m, up_a, sum_up, rate),
        advance(down_w, down_m, down_a, sum_down, rate),
        advance(norm_w, norm_m, norm_a, sum_norm, rate),
    )


def shards(*args):
    tokens, grad_out, doc_ids = args[:3]
    qkv_w = args[3]
    seqs, seq_len, width = tokens.shape
    fits = lax.axis_size("seq") == 8 and qkv_w.shape[0] % 16 == 0
    fits = fits and seqs == 1 and seq_len == 8 * SPAN and width == 512
    if not fits:
        return shards_plain(*args)
    chain = lax.axis_size("dp")
    names = {"qkv": 3, "out": 6, "up": 9, "down": 12, "norm": 15}
    done = fused_layer(
        chain,
        0.02 / math.sqrt(seq_len * 8 * chain),
        tokens.reshape(seq_len, width),
        grad_out.reshape(seq_len, width),
        doc_ids,
        *({name: args[k + j] for name, k in names.items()} for j in range(3)),
    )
    order = ["block_out", "input_grad"] + ["t_" + name for name in names]
    result = finish([done[name] for name in order], done["stats"])
    return (
        result[0].reshape(tokens.shape),
        result[1].reshape(tokens.shape),
        *result[7:],
        *result[2:7],
    )


def solution(mesh):
    placed = (
        P("dp", "seq", None),
        P("dp", "seq", None),
        P("dp", "seq"),
        P(("seq", "dp"), None),
        P(("seq", "dp"), None),
        P(("seq", "dp"), None),
        P(("seq", "dp"), None),
        P(("seq", "dp"), None),
        P(("seq", "dp"), None),
        P(("seq", "dp"), None),
        P(("seq", "dp"), None),
        P(("seq", "dp"), None),
        P(("seq", "dp"), None),
        P(("seq", "dp"), None),
        P(("seq", "dp"), None),
        P(None, ("seq", "dp")),
        P(None, ("seq", "dp")),
        P(None, ("seq", "dp")),
    )
    return jax.shard_map(
        shards,
        mesh=mesh,
        in_specs=placed,
        out_specs=(
            P("dp", "seq", None),
            P("dp", "seq", None),
            P("dp", None),
            P("dp", None),
            P(None, ("seq", "dp"), None),
            P(None, ("seq", "dp"), None),
            P(None, ("seq", "dp"), None),
            P(None, ("seq", "dp"), None),
            P(None, None, ("seq", "dp")),
        ),
        check_vma=False,
    )
```
